32 devices in a mesh: rep: 4 (over y, x), shard: 8 (over z, core).
Axes of the slice: x: 2, y: 2, z: 4, core: 2. Of those that a mesh axis runs over, the one named last changes fastest.
Arguments:
- tokens: bfloat16 [4096, 768], P(('rep', 'shard')), may hold values from -6 to 6
- segment_ids: int32 [32, 128], P(('rep', 'shard')), may hold values from 0 to 3, never falling along the last dimension, each value on 1 to 64 neighbouring positions
- first_gain: bfloat16 [768], P('shard'), may hold values from 0.5 to 1.5
- first_shift: bfloat16 [768], P('shard'), may hold values from -3 to 3
- qkv_weight: bfloat16 [768, 2304], P('shard'), may hold values from -3 to 3, as said below
- qv_bias: bfloat16 [2, 768], P(None, 'shard'), may hold values from -3 to 3
- proj_weight: bfloat16 [768, 768], P('shard'), may hold values from -0.625 to 0.625
- proj_bias: bfloat16 [768], P('shard'), may hold values from -3 to 3
- second_gain: bfloat16 [768], P('shard'), may hold values from 0.5 to 1.5
- second_shift: bfloat16 [768], P('shard'), may hold values from -3 to 3
- fc_weight: bfloat16 [768, 3072], P('shard'), may hold values from -0.21875 to 0.21875
- fc_bias: bfloat16 [3072], P('shard'), may hold values from -3 to 3
- out_weight: bfloat16 [3072, 768], P('shard'), may hold values from -0.109375 to 0.109375
- out_bias: bfloat16 [768], P('shard'), may hold values from -3 to 3
- cotangent: bfloat16 [4096, 768], P(('rep', 'shard')), may hold values from -6 to 6
Outputs:
- block_output: bfloat16 [4096, 768], P(('rep', 'shard'))
- grad_tokens: float32 [4096, 768], P(('rep', 'shard'))
- grad_first_gain: float32 [768], P('shard')
- grad_first_shift: float32 [768], P('shard')
- grad_qkv_weight: float32 [768, 2304], P('shard')
- grad_qv_bias: float32 [2, 768], P(None, 'shard')
- grad_proj_weight: float32 [768, 768], P('shard')
- grad_proj_bias: float32 [768], P('shard')
- grad_second_gain: float32 [768], P('shard')
- grad_second_shift: float32 [768], P('shard')
- grad_fc_weight: float32 [768, 3072], P('shard')
- grad_fc_bias: float32 [3072], P('shard')
- grad_out_weight: float32 [3072, 768], P('shard')
- grad_out_bias: float32 [768], P('shard')
The draws below stay inside these ranges and needn't reach their ends.
Inputs may be any that keep to these rules, and one draw needn't show every extreme that they name: `segment_ids`: each row holds 4 runs of equal numbers in rising order, each run 1 to 64 long, one of them exactly 64. `qkv_weight`: columns 0 to 767 project to queries, the next 768 columns to keys, the last 768 columns to values.
All inputs are finite; a program needn't handle non-finite values.
Results may differ from the reference program's by a relative error of at most 0.011.
Values may be sent and summed in bfloat16 or wider, within the bound.
A program may use at most 128 MiB of HBM per device.

```python
import math
import jax
import jax.numpy as jnp
import numpy as np
from jax import lax

D = 768
HEADS = 12
HD = 64
FF = 3072
TOK_DEV = 128
SEQ_DEV = 4
MOST = 64
TOKENS = 4096
DEVICES = 32


def draw_tokens(key, part):
    fresh_key = jax.random.fold_in(jax.random.fold_in(key, 5), 0)
    drawn_rows = jax.random.normal(fresh_key, (TOKENS, D), jnp.float32)
    return jnp.clip(drawn_rows, -6.0, 6.0).astype(jnp.bfloat16)


def draw_qkv_weight(key, part):
    base_key = jax.random.fold_in(key, 3)
    matrix = jax.random.normal(base_key, (D, 3 * D), jnp.float32) * (1.0 / math.sqrt(D))
    return jnp.clip(matrix, -3.0, 3.0).astype(jnp.bfloat16)


def strengthened(values, own_key, source, target, parts, factor):
    owner, partner = [(jnp.arange(values.shape[axis_at]) // (values.shape[axis_at] // parts)).reshape([-1 if axis == axis_at else 1 for axis in range(values.ndim)]) for axis_at in (source, target)]
    chosen = jax.random.permutation(own_key, parts)[partner]
    strong = (owner == chosen) | (owner == (partner + parts // 2) % parts)
    return jnp.where(strong, factor * values, values)


def level_of(stream_key, extent, cuts, least, high):
    def one(dim, parts):
        heights = jax.random.uniform(jax.random.fold_in(jax.random.fold_in(stream_key, 6), dim), (parts,), jnp.float32, least / len(cuts), high / len(cuts))
        return jnp.repeat(jnp.exp(heights), extent[dim] // parts).reshape((-1,) + (1,) * (len(extent) - dim - 1))

    loudness = one(*cuts[0])
    for cut in cuts[1:]:
        loudness = loudness * one(*cut)
    return loudness


def length_profile(count, total, limit, skew):
    portions = [(1 << 20) // math.isqrt(rank ** skew) + 1 for rank in range(2, count + 1)]
    rest, holding = total - limit - (count - 1), [1] * (count - 1)
    while rest > 0:
        movable = [i for i in range(count - 1) if holding[i] < limit]
        mass, remaining = sum([portions[i] for i in movable]), rest
        for i in movable:
            more = min(limit - holding[i], max(1, remaining * portions[i] // mass), rest)
            holding[i] = holding[i] + more
            rest = rest - more
    return np.array([limit] + holding)


def ragged(own_key, number_of, total, most, slope):
    if number_of == 2:
        one = jax.random.randint(own_key, (), max(1, total - most), min(most, total - 1) + 1)
        return jnp.stack([one, total - one])
    sizes = jnp.asarray(length_profile(number_of, total, most, slope), jnp.int32)
    couples = (number_of - 1) // 2
    donor, taker = sizes[1:1 + 2 * couples:2], sizes[2:2 + 2 * couples:2]
    slack = jnp.minimum(donor - 1, most - taker)
    shifted = jax.random.randint(jax.random.fold_in(own_key, 1), (couples,), 0, 1 << 20) % (slack + 1)
    sizes = sizes.at[1:1 + 2 * couples:2].set(donor - shifted).at[2:2 + 2 * couples:2].set(taker + shifted)
    return sizes[jax.random.permutation(jax.random.fold_in(own_key, 2), number_of)]


def gaussian(own_key, dims, deviation, most, cuts=(), kind=jnp.bfloat16):
    values = jax.random.normal(own_key, dims, jnp.float32) * deviation
    if len(cuts) > 0:
        values = level_of(own_key, dims, cuts, -0.22, 0.18) * values
    return jnp.clip(values, min=-most, max=most).astype(kind)


def heavy_noise(stream_key, dims, scale, most, cuts, heavy, kind=jnp.bfloat16):
    drawn = scale * jax.random.normal(stream_key, dims, jnp.float32)
    if cuts:
        drawn = drawn * level_of(stream_key, dims, cuts, -0.22, 0.18)
    return jnp.clip(strengthened(drawn, jax.random.fold_in(stream_key, 3), *heavy), -most, most).astype(kind)


def setup_inputs(seed: int = 0) -> dict:
    key_list = jax.random.split(jax.random.key(seed), 16)
    tokens = draw_tokens(jax.random.fold_in(key_list[15], 71), 0)
    segment_ids = jax.vmap(lambda own: jnp.searchsorted(jnp.cumsum(ragged(own, SEQ_DEV, TOK_DEV, MOST, 2)), jnp.arange(TOK_DEV), side="right"))(jax.random.split(key_list[1], DEVICES)).reshape((DEVICES, TOK_DEV)).astype(jnp.int32)
    first_gain = jnp.clip(1.0 + 0.1 * jax.random.normal(key_list[2], (D,), jnp.float32), 0.5, 1.5).astype(jnp.bfloat16)
    first_shift = gaussian(key_list[3], (D,), 0.5, 3.0, ((0, 8),))
    qkv_weight = draw_qkv_weight(jax.random.fold_in(key_list[15], 71), 0)
    qv_bias = gaussian(key_list[5], (2, D), 0.5, 3.0, ((1, 8),))
    proj_weight = gaussian(key_list[6], (D, D), (D // 8) ** -0.5, 0.625, ((0, 8),))
    proj_bias = gaussian(key_list[7], (D,), 0.5, 3.0, ((0, 8),))
    second_gain = jnp.clip(1.0 + 0.1 * jax.random.normal(key_list[8], (D,), jnp.float32), 0.5, 1.5).astype(jnp.bfloat16)
    second_shift = gaussian(key_list[9], (D,), 0.5, 3.0, ((0, 8),))
    fc_weight = gaussian(key_list[10], (D, FF), D ** -0.5, 0.21875, ((0, 8),))
    fc_bias = gaussian(key_list[11], (FF,), 0.5, 3.0, ((0, 8),))
    out_weight = gaussian(key_list[12], (FF, D), FF ** -0.5, 0.109375, ((0, 8),))
    out_bias = gaussian(key_list[13], (D,), 0.5, 3.0, ((0, 8),))
    cotangent = heavy_noise(key_list[14], (TOKENS, D), 1.0, 6.0, ((0, 32),), (0, 1, 32, 2.75))
    return {"tokens": tokens, "segment_ids": segment_ids, "first_gain": first_gain, "first_shift": first_shift, "qkv_weight": qkv_weight, "qv_bias": qv_bias, "proj_weight": proj_weight, "proj_bias": proj_bias, "second_gain": second_gain, "second_shift": second_shift, "fc_weight": fc_weight, "fc_bias": fc_bias, "out_weight": out_weight, "out_bias": out_bias, "cotangent": cotangent}


EPSILON = 1e-05

def layer_norm(field, norm_gain, norm_shift):
    center = field - lax.optimization_barrier(jnp.mean(field, axis=-1, keepdims=True))
    spread = lax.optimization_barrier(jnp.mean(center * center, axis=-1, keepdims=True))
    return center * lax.rsqrt(spread + EPSILON) * norm_gain + norm_shift

def gelu_tanh(field):
    return jax.nn.gelu(field, approximate=True)

def head_split(matrix):
    return matrix.reshape(matrix.shape[0], HEADS, HD).astype(jnp.float32)

def masked_scores(query, keys, segments):
    rows = query.shape[0]
    scores = jnp.einsum('qhd,khd->hqk', head_split(query), head_split(keys)) * (1.0 / math.sqrt(HD))
    position = jnp.arange(rows, dtype=jnp.int32)
    allowed = (segments[:, None] == segments[None, :]) & (position[None, :] <= position[:, None])
    return jnp.where(allowed[None], scores, -1e+30)

def attend_forward(query, keys, values, segments):
    rows = query.shape[0]
    scores = masked_scores(query, keys, segments)
    row_max = lax.optimization_barrier(jnp.max(scores, axis=-1, keepdims=True))
    row_total = lax.optimization_barrier(jnp.sum(jnp.exp(scores - row_max), axis=-1, keepdims=True))
    logsum = row_max + jnp.log(row_total)
    probs = jnp.exp(scores - logsum).astype(jnp.bfloat16)
    attended = jnp.einsum('hqk,khd->qhd', probs.astype(jnp.float32), head_split(values))
    return (attended.reshape(rows, D).astype(jnp.bfloat16), logsum)

def attend_backward(query, keys, values, segments, attended, logsum, grad_attended):
    rows = query.shape[0]
    scores = masked_scores(query, keys, segments)
    weights = jnp.exp(scores - logsum)
    probs_low = weights.astype(jnp.bfloat16).astype(jnp.float32)
    grad_heads = head_split(grad_attended)
    grad_values = jnp.einsum('hqk,qhd->khd', probs_low, grad_heads)
    grad_probs = jnp.einsum('qhd,khd->hqk', grad_heads, head_split(values))
    delta = jnp.einsum('qhd,qhd->hq', grad_heads, head_split(attended))[..., None]
    grad_scores = (weights * (grad_probs - delta) * (1.0 / math.sqrt(HD))).astype(jnp.bfloat16).astype(jnp.float32)
    grad_query = jnp.einsum('hqk,khd->qhd', grad_scores, head_split(keys))
    grad_keys = jnp.einsum('hqk,qhd->khd', grad_scores, head_split(query))
    return (grad_query.reshape(rows, D), grad_keys.reshape(rows, D), grad_values.reshape(rows, D))

def block_pass(tok_block, cot_block, segments, weights):
    first_gain, first_shift, qkv_weight, qv_bias, proj_weight, proj_bias, second_gain, second_shift, fc_weight, fc_bias, out_weight, out_bias = weights
    inputs = tok_block.astype(jnp.float32)
    normed_f, first_back = jax.vjp(layer_norm, inputs, first_gain.astype(jnp.float32), first_shift.astype(jnp.float32))
    normed_first = normed_f.astype(jnp.bfloat16)
    projected = jnp.dot(normed_first, qkv_weight, preferred_element_type=jnp.float32)
    query = (projected[:, :D] + qv_bias[0].astype(jnp.float32)).astype(jnp.bfloat16)
    keys = projected[:, D:2 * D].astype(jnp.bfloat16)
    values = (projected[:, 2 * D:] + qv_bias[1].astype(jnp.float32)).astype(jnp.bfloat16)
    attended, logsum = attend_forward(query, keys, values, segments)
    residual = inputs + jnp.dot(attended, proj_weight, preferred_element_type=jnp.float32) + proj_bias.astype(jnp.float32)
    normed_s, second_back = jax.vjp(layer_norm, residual, second_gain.astype(jnp.float32), second_shift.astype(jnp.float32))
    normed_second = normed_s.astype(jnp.bfloat16)
    pre_act = jnp.dot(normed_second, fc_weight, preferred_element_type=jnp.float32) + fc_bias.astype(jnp.float32)
    activated, gelu_back = jax.vjp(gelu_tanh, pre_act)
    hidden = activated.astype(jnp.bfloat16)
    result = (residual + jnp.dot(hidden, out_weight, preferred_element_type=jnp.float32) + out_bias.astype(jnp.float32)).astype(jnp.bfloat16)
    cot_f = cot_block.astype(jnp.float32)
    term_out_bias = lax.optimization_barrier(jnp.sum(cot_f, axis=0))
    term_out_weight = jnp.dot(hidden.T, cot_block, preferred_element_type=jnp.float32)
    grad_hidden = jnp.dot(cot_block, out_weight.T, preferred_element_type=jnp.float32)
    grad_pre, = gelu_back(grad_hidden)
    grad_pre_low = grad_pre.astype(jnp.bfloat16)
    term_fc_bias = lax.optimization_barrier(jnp.sum(grad_pre, axis=0))
    term_fc_weight = jnp.dot(normed_second.T, grad_pre_low, preferred_element_type=jnp.float32)
    grad_normed_second = jnp.dot(grad_pre_low, fc_weight.T, preferred_element_type=jnp.float32)
    grad_from_norm, term_second_gain, term_second_shift = second_back(grad_normed_second)
    grad_residual = cot_f + grad_from_norm
    grad_residual_low = grad_residual.astype(jnp.bfloat16)
    term_proj_bias = lax.optimization_barrier(jnp.sum(grad_residual, axis=0))
    term_proj_weight = jnp.dot(attended.T, grad_residual_low, preferred_element_type=jnp.float32)
    grad_attended = jnp.dot(grad_residual_low, proj_weight.T, preferred_element_type=jnp.float32).astype(jnp.bfloat16)
    grad_query, grad_keys, grad_values = attend_backward(query, keys, values, segments, attended, logsum, grad_attended)
    term_qv_bias = jnp.stack([lax.optimization_barrier(jnp.sum(grad_query, axis=0)), lax.optimization_barrier(jnp.sum(grad_values, axis=0))])
    grad_projected = jnp.concatenate([grad_query, grad_keys, grad_values], axis=1).astype(jnp.bfloat16)
    term_qkv_weight = jnp.dot(normed_first.T, grad_projected, preferred_element_type=jnp.float32)
    grad_normed_first = jnp.dot(grad_projected, qkv_weight.T, preferred_element_type=jnp.float32)
    grad_input_norm, term_first_gain, term_first_shift = first_back(grad_normed_first)
    grad_inputs = grad_residual + grad_input_norm
    terms = (term_first_gain, term_first_shift, term_qkv_weight, term_qv_bias, term_proj_weight, term_proj_bias, term_second_gain, term_second_shift, term_fc_weight, term_fc_bias, term_out_weight, term_out_bias)
    return (result, grad_inputs, terms)

def reference(tokens, segment_ids, first_gain, first_shift, qkv_weight, qv_bias, proj_weight, proj_bias, second_gain, second_shift, fc_weight, fc_bias, out_weight, out_bias, cotangent):
    weights = (first_gain, first_shift, qkv_weight, qv_bias, proj_weight, proj_bias, second_gain, second_shift, fc_weight, fc_bias, out_weight, out_bias)
    token_blocks = tokens.reshape(DEVICES, TOK_DEV, D)
    cot_blocks = cotangent.reshape(DEVICES, TOK_DEV, D)
    initial = tuple((jnp.zeros(weight.shape, jnp.float32) for weight in weights))

    def advance(running, pieces):
        tok_block, cot_block, seg_row = pieces
        result, grad_inputs, terms = block_pass(tok_block, cot_block, seg_row, weights)
        return (tuple((total + term for total, term in zip(running, terms))), (result, grad_inputs))
    totals, (results, grad_all) = lax.scan(advance, initial, (token_blocks, cot_blocks, segment_ids))
    factor = 1.0 / math.sqrt(TOKENS)
    return (results.reshape(TOKENS, D), grad_all.reshape(TOKENS, D), totals[0] * factor, totals[1] * factor, totals[2] * factor, totals[3] * factor, totals[4] * factor, totals[5] * factor, totals[6] * factor, totals[7] * factor, totals[8] * factor, totals[9] * factor, totals[10] * factor, totals[11] * factor)
```

```python
import functools
import math

import jax
import jax.numpy as jnp
from jax import lax
from jax.experimental import pallas as pl
from jax.experimental.pallas import tpu as pltpu
from jax.sharding import PartitionSpec as P

D = 768
HEADS = 12
HD = 64
FF = 3072


EPSILON = 1e-05


def layer_norm(field, norm_gain, norm_shift):
    center = field - jnp.mean(field, axis=-1, keepdims=True)
    spread = jnp.mean(center * center, axis=-1, keepdims=True)
    return center * lax.rsqrt(spread + EPSILON) * norm_gain + norm_shift


def gelu_tanh(field):
    return jax.nn.gelu(field, approximate=True)


def head_split(matrix):
    return matrix.reshape(matrix.shape[0], HEADS, HD)


def masked_scores(query, keys, segments):
    rows = query.shape[0]
    scores = jnp.einsum(
        "qhd,khd->hqk", head_split(query), head_split(keys), preferred_element_type=jnp.float32
    ) * (1.0 / math.sqrt(HD))
    position = lax.iota(jnp.int32, rows)
    allowed = (segments[:, None] == segments[None, :]) & (position[None, :] <= position[:, None])
    return jnp.where(allowed[None], scores, -1e30)


def attend_forward(query, keys, values, segments):
    rows = query.shape[0]
    scores = masked_scores(query, keys, segments)
    row_max = jnp.max(scores, axis=-1, keepdims=True)
    row_total = jnp.sum(jnp.exp(scores - row_max), axis=-1, keepdims=True)
    logsum = row_max + jnp.log(row_total)
    probs = jnp.exp(scores - logsum).astype(jnp.bfloat16)
    attended = jnp.einsum(
        "hqk,khd->qhd", probs, head_split(values), preferred_element_type=jnp.float32
    )
    return (attended.reshape(rows, D).astype(jnp.bfloat16), logsum)


def attend_backward(query, keys, values, segments, attended, logsum, grad_attended):
    rows = query.shape[0]
    scores = masked_scores(query, keys, segments)
    weights = jnp.exp(scores - logsum)
    grad_heads = head_split(grad_attended)
    grad_values = jnp.einsum(
        "hqk,qhd->khd", weights.astype(jnp.bfloat16), grad_heads, preferred_element_type=jnp.float32
    )
    grad_probs = jnp.einsum(
        "qhd,khd->hqk", grad_heads, head_split(values), preferred_element_type=jnp.float32
    )
    delta = jnp.einsum(
        "qhd,qhd->hq", grad_heads, head_split(attended), preferred_element_type=jnp.float32
    )
    grad_scores = (weights * (grad_probs - delta[..., None]) * (1.0 / math.sqrt(HD))).astype(
        jnp.bfloat16
    )
    grad_query = jnp.einsum(
        "hqk,khd->qhd", grad_scores, head_split(keys), preferred_element_type=jnp.float32
    )
    grad_keys = jnp.einsum(
        "hqk,qhd->khd", grad_scores, head_split(query), preferred_element_type=jnp.float32
    )
    return (grad_query.reshape(rows, D), grad_keys.reshape(rows, D), grad_values.reshape(rows, D))


def exchange(field, axis, split, concat):
    return lax.all_to_all(field, axis, split_axis=split, concat_axis=concat, tiled=True)


def spread(field, axis):
    parts = lax.axis_size(axis)
    return exchange(jnp.broadcast_to(field[None], (parts,) + field.shape), axis, 0, 0)


def by_replica(field, shards, reps):
    rows = field.shape[0]
    return (
        field.reshape(shards, reps, rows // (shards * reps), -1).swapaxes(0, 1).reshape(rows, -1)
    )


def per_device(
    tokens,
    segment_ids,
    first_gain,
    first_shift,
    qkv_weight,
    qv_bias,
    proj_weight,
    proj_bias,
    second_gain,
    second_shift,
    fc_weight,
    fc_bias,
    out_weight,
    out_bias,
    cotangent,
):
    low = jnp.bfloat16
    segments = segment_ids[0]
    own_rows = tokens.shape[0]
    shards = lax.axis_size("shard")
    reps = lax.axis_size("rep")
    factor = 1.0 / math.sqrt(own_rows * reps * shards)
    small = jnp.stack(
        [first_gain, first_shift, qv_bias[0], qv_bias[1], proj_bias, second_gain, second_shift, out_bias]
    )
    small_full = lax.all_gather(small, "shard", axis=1, tiled=True).astype(jnp.float32)
    gain_one, shift_one, q_bias, v_bias, proj_bias_full, gain_two, shift_two, out_bias_full = (
        small_full[i] for i in range(8)
    )
    qkv_full = lax.all_gather(qkv_weight, "shard", axis=0, tiled=True)
    proj_full = lax.all_gather(proj_weight, "shard", axis=0, tiled=True)
    fc_cols = exchange(fc_weight, "shard", 1, 0)
    inputs = tokens.astype(jnp.float32)
    normed_f, first_back = jax.vjp(layer_norm, inputs, gain_one, shift_one)
    normed_first = normed_f.astype(low)
    projected = jnp.dot(normed_first, qkv_full, preferred_element_type=jnp.float32)
    query = (projected[:, :D] + q_bias).astype(low)
    keys = projected[:, D : 2 * D].astype(low)
    values = (projected[:, 2 * D :] + v_bias).astype(low)
    attended, logsum = attend_forward(query, keys, values, segments)
    residual = (
        inputs + jnp.dot(attended, proj_full, preferred_element_type=jnp.float32) + proj_bias_full
    )
    cot_f = cotangent.astype(jnp.float32)
    normed_s, second_back = jax.vjp(layer_norm, residual, gain_two, shift_two)
    normed_all = lax.all_gather(normed_s.astype(low), "shard", axis=0, tiled=True)
    cot_later, normed_all = lax.optimization_barrier((cotangent, normed_all))
    cot_all = lax.all_gather(cot_later, "shard", axis=0, tiled=True)
    pre_act = jnp.dot(normed_all, fc_cols, preferred_element_type=jnp.float32) + fc_bias.astype(
        jnp.float32
    )
    activated, gelu_back = jax.vjp(gelu_tanh, pre_act)
    hidden = activated.astype(low)
    grad_hidden = jnp.dot(cot_all, out_weight.T, preferred_element_type=jnp.float32)
    (grad_pre,) = gelu_back(grad_hidden)
    grad_pre_low = grad_pre.astype(low)
    grad_normed_part = jnp.dot(grad_pre_low, fc_cols.T, preferred_element_type=jnp.float32).astype(low)
    grad_normed_low = lax.psum_scatter(grad_normed_part, "shard", scatter_dimension=0, tiled=True)
    term_out_weight = jnp.dot(hidden.T, cot_all, preferred_element_type=jnp.float32) * factor
    term_fc_weight = jnp.dot(normed_all.T, grad_pre_low, preferred_element_type=jnp.float32) * factor
    out_part = jnp.dot(hidden, out_weight, preferred_element_type=jnp.float32).astype(low)
    ff_terms = jnp.concatenate(
        [
            term_out_weight.astype(low).reshape(reps, -1, D),
            by_replica(term_fc_weight.astype(low), shards, reps).reshape(reps, -1, D),
        ],
        axis=1,
    )
    ff_sum = jnp.sum(exchange(ff_terms, "rep", 0, 0).astype(jnp.float32), axis=0).astype(low)
    first_later, attended_later, grad_normed_low, ff_sum = lax.optimization_barrier(
        (normed_first, attended, grad_normed_low, ff_sum)
    )
    first_all = lax.all_gather(first_later, "shard", axis=0, tiled=True)
    grad_normed_second = grad_normed_low.astype(jnp.float32)

    grad_from_norm, second_gain_sum, second_shift_sum = second_back(grad_normed_second)
    grad_residual = cot_f + grad_from_norm
    grad_residual_low = grad_residual.astype(low)
    grad_residual_all = lax.all_gather(grad_residual_low, "shard", axis=0, tiled=True)
    attended_cols = exchange(attended_later, "shard", 1, 0)
    grad_attended = jnp.dot(
        grad_residual_low, proj_full.T, preferred_element_type=jnp.float32
    ).astype(low)
    out_rows = out_weight.shape[0] // reps
    out_piece = ff_sum[:out_rows]
    fc_piece = ff_sum[out_rows:].reshape(D // reps, -1)
    fc_piece = exchange(fc_piece, "shard", 0, 1)
    ff_all = spread(jnp.concatenate([out_piece, fc_piece.reshape(-1, D)]), "rep").astype(jnp.float32)

    grad_query, grad_keys, grad_values = attend_backward(
        query, keys, values, segments, attended, logsum, grad_attended
    )
    grad_projected = jnp.concatenate([grad_query, grad_keys, grad_values], axis=1).astype(low)
    grad_projected, ff_all = lax.optimization_barrier((grad_projected, ff_all))
    out_grad = ff_all[:, :out_rows].reshape(-1, D)
    fc_grad = ff_all[:, out_rows:].reshape(-1, FF)
    grad_cols = exchange(grad_projected, "shard", 1, 0)
    grad_normed_first = jnp.dot(grad_projected, qkv_full.T, preferred_element_type=jnp.float32)
    out_later, grad_cols = lax.optimization_barrier((out_part, grad_cols))
    out_sum = lax.psum_scatter(out_later, "shard", scatter_dimension=0, tiled=True)
    result = (residual + out_sum.astype(jnp.float32) + out_bias_full).astype(low)
    term_qkv_weight = jnp.dot(first_all.T, grad_cols, preferred_element_type=jnp.float32) * factor
    term_proj_weight = (
        jnp.dot(attended_cols.T, grad_residual_all, preferred_element_type=jnp.float32) * factor
    )
    attn_terms = jnp.concatenate(
        [
            term_proj_weight.astype(low).reshape(reps, -1, D),
            by_replica(term_qkv_weight.astype(low), shards, reps).reshape(reps, -1, D),
        ],
        axis=1,
    )
    attn_sum = jnp.sum(exchange(attn_terms, "rep", 0, 0).astype(jnp.float32), axis=0).astype(low)
    proj_rows = proj_weight.shape[0] // reps
    proj_piece = attn_sum[:proj_rows]
    qkv_piece = attn_sum[proj_rows:].reshape(D // reps, -1)
    qkv_piece = exchange(qkv_piece, "shard", 0, 1)
    attn_all = spread(jnp.concatenate([proj_piece, qkv_piece.reshape(-1, D)]), "rep").astype(
        jnp.float32
    )
    proj_grad = attn_all[:, :proj_rows].reshape(-1, D)
    qkv_grad = attn_all[:, proj_rows:].reshape(-1, 3 * D)

    grad_input_norm, first_gain_sum, first_shift_sum = first_back(grad_normed_first)
    grad_inputs = grad_residual + grad_input_norm
    terms = jnp.stack(
        [
            first_gain_sum,
            first_shift_sum,
            jnp.sum(grad_query, axis=0),
            jnp.sum(grad_values, axis=0),
            jnp.sum(grad_residual, axis=0),
            second_gain_sum,
            second_shift_sum,
            jnp.sum(cot_f, axis=0),
        ]
    )
    count = terms.shape[0]
    terms = terms.reshape(count, shards, -1).swapaxes(0, 1).reshape(shards, -1)
    own_terms = jnp.concatenate(
        [jnp.sum(exchange(terms, "shard", 0, 0), axis=0), jnp.sum(grad_pre, axis=0)]
    )
    sums = jnp.sum(spread(own_terms, "rep"), axis=0) * factor
    own_cols = D // shards
    fc_bias_grad = sums[count * own_cols :]
    sums = sums[: count * own_cols].reshape(count, own_cols)
    return (
        result,
        grad_inputs,
        sums[0],
        sums[1],
        qkv_grad,
        sums[2:4],
        proj_grad,
        sums[4],
        sums[5],
        sums[6],
        fc_grad,
        fc_bias_grad,
        out_grad,
        sums[7],
    )

MESH = pl.DeviceIdType.MESH
LOW = jnp.bfloat16
WIDE = jnp.float32
ROWS = 128
BLOCK = 96
THIRD = 192
NEG = -1e30


def xor(a, b):
    return (a // 2 + b // 2) % 2 * 2 + (a + b) % 2


def mm(a, b):
    return jnp.dot(a, b, preferred_element_type=WIDE)


def mm_t(a, b):
    return lax.dot_general(a, b, (((1,), (1,)), ((), ())), preferred_element_type=WIDE)


def t_mm(a, b):
    return lax.dot_general(a, b, (((0,), (0,)), ((), ())), preferred_element_type=WIDE)


def three(field):
    first = field.astype(LOW)
    rest = field - first.astype(WIDE)
    second = rest.astype(LOW)
    return first, second, (rest - second.astype(WIDE)).astype(LOW)


def normalize(field):
    center = field - jnp.mean(field, axis=-1, keepdims=True)
    scale = lax.rsqrt(jnp.mean(center * center, axis=-1, keepdims=True) + EPSILON)
    return center * scale, scale


def normalize_back(grad, unit, scale, gain):
    inner = grad * gain
    mean = jnp.mean(inner, axis=-1, keepdims=True)
    along = jnp.mean(inner * unit, axis=-1, keepdims=True)
    return scale * (inner - mean - unit * along)


def heads_of(field):
    lane = lax.broadcasted_iota(jnp.int32, field.shape, 1)
    zero = jnp.zeros_like(field)
    return jnp.concatenate(
        [jnp.where((lane >= h * HD) & (lane < (h + 1) * HD), field, zero) for h in range(3)], axis=0
    )


def heads_join(stacked):
    lane = lax.broadcasted_iota(jnp.int32, (ROWS, THIRD), 1)
    return jnp.where(
        lane < HD, stacked[:ROWS], jnp.where(lane < 2 * HD, stacked[ROWS : 2 * ROWS], stacked[2 * ROWS :])
    )


class Links:
    def __init__(self, sends, recvs):
        self.sends, self.recvs, self.used, self.open = sends, recvs, 0, []

    def take(self, count=1):
        self.used += count
        return self.used - count

    def copy(self, src, dst, index, device, recv_index=None):
        recv_index = index if recv_index is None else recv_index
        return pltpu.make_async_remote_copy(
            src_ref=src,
            dst_ref=dst,
            send_sem=self.sends.at[index],
            recv_sem=self.recvs.at[recv_index],
            device_id=device,
            device_id_type=MESH,
        )

    def send(self, src, dst, index, device, recv_index=None):
        made = self.copy(src, dst, index, device, recv_index)
        made.start()
        self.open.append(made)
        return made

    def drain(self):
        for made in self.open:
            made.wait_send()


class Gather:
    def __init__(self, links, place, own, full):
        self.links, self.place, self.own, self.full = links, place, own, full
        self.base = links.take(7)

    def slot(self, z, c):
        return self.full.at[pl.ds(pl.multiple_of((2 * z + c) * BLOCK, 16), BLOCK)]

    def arrived(self, which, slot):
        self.links.copy(slot, slot, self.base + which, self.place.here).wait_recv()

    def pass_on(self, which, slot, device):
        self.links.send(slot, slot, self.base + which, device)

    def start(self):
        p = self.place
        mine = self.slot(p.z, p.c)
        self.links.send(self.own, mine, self.base, p.two)
        self.links.send(self.own, mine, self.base + 1, p.one)
        self.links.send(self.own, mine, self.base + 2, p.mate)
        mine[...] = self.own[...]

    def step1(self):
        p = self.place
        slot = self.slot(xor(p.z, 2), p.c)
        self.arrived(0, slot)
        self.pass_on(3, slot, p.one)
        self.pass_on(4, slot, p.mate)

    def step2(self):
        p = self.place
        slot = self.slot(xor(p.z, 1), p.c)
        self.arrived(1, slot)
        self.pass_on(5, slot, p.mate)

    def step3(self):
        p = self.place
        slot = self.slot(xor(p.z, 3), p.c)
        self.arrived(3, slot)
        self.pass_on(6, slot, p.mate)

    def finish(self):
        p = self.place
        for which, flip in ((2, 0), (4, 2), (5, 1), (6, 3)):
            self.arrived(which, self.slot(xor(p.z, flip), 1 - p.c))


class Reduce:
    def __init__(self, links, place, bufs):
        self.links, self.place = links, place
        self.part, self.got, self.total, self.near, self.second, self.far, self.final = bufs
        self.base = links.take(4)

    def fill(self, full):
        for z in range(4):
            for c in range(2):
                at = (2 * z + c) * BLOCK
                self.part[z, c] = full[at : at + BLOCK].astype(LOW)

    def pair(self):
        p = self.place
        self.sent = self.links.send(self.part.at[:, 1 - p.c], self.got, self.base, p.mate)

    def step1(self):
        p = self.place
        self.sent.wait_recv()
        for z in range(4):
            self.total[z] = (self.part[z, p.c].astype(WIDE) + self.got[z].astype(WIDE)).astype(LOW)
        self.first = [
            self.links.send(self.total.at[xor(p.z, 3)], self.near.at[1], self.base + 1, p.one),
            self.links.send(self.total.at[xor(p.z, 1)], self.near.at[0], self.base + 2, p.one),
        ]

    def step2(self):
        p = self.place
        self.first[0].wait_recv()
        self.second[...] = (self.total[xor(p.z, 2)].astype(WIDE) + self.near[1].astype(WIDE)).astype(LOW)
        self.last = self.links.send(self.second, self.far, self.base + 3, p.two)

    def finish(self, factor):
        p = self.place
        self.first[1].wait_recv()
        self.last.wait_recv()
        whole = self.total[p.z].astype(WIDE) + self.near[0].astype(WIDE) + self.far[...].astype(WIDE)
        self.final[...] = (whole * factor).astype(LOW)


class Place:
    def __init__(self):
        self.j, self.s = lax.axis_index("rep"), lax.axis_index("shard")
        self.z, self.c = self.s // 2, self.s % 2
        self.here = (self.j, self.s)
        self.mate = self.at(0, 1)
        self.one = self.at(1, 0)
        self.two = self.at(2, 0)

    def at(self, flip_z, flip_c):
        return (self.j, 2 * xor(self.z, flip_z) + (self.c + flip_c) % 2)

    def peer(self, k):
        return (xor(self.j, k), self.s)


def layer_kernel(
    factor,
    tok, cot, mask_in, vec_in, wq_in, wp_in, wf_in, wo_in,
    y_ref, gt_ref, dq_ref, dp_ref, df_ref, do_ref, dv_ref,
    sends, recvs,
    vec_all, nf, mk, cots, wq, wp, wf, wo, out_own, out_got, place_m, params,
    qkv, weights, att, att_rx, res, unit1, unit2, scales,
    ns, hid, gpl, gns_tx, gns_rx, op_tx, op_rx, ga_tx, ga_rx, gnf_tx, gnf_rx, gproj, gr,
    sums, acc, vt, vr, v2, vr2, dp_mine, dp_got,
    *reduce_bufs,
):
    p = Place()
    j, s, z, c = p.j, p.s, p.z, p.c
    links = Links(sends, recvs)
    partners = [p.at(fz, fc) for fz in range(4) for fc in range(2) if (fz, fc) != (0, 0)]
    partners += [p.peer(k) for k in (1, 2, 3)]
    partners += [(xor(j, k), 2 * z + 1 - c) for k in (1, 2, 3)]
    barrier = pltpu.get_barrier_semaphore()
    for device in partners:
        pl.semaphore_signal(barrier, inc=1, device_id=device, device_id_type=MESH)
    pl.semaphore_wait(barrier, len(partners))

    gq = Gather(links, p, wq_in, wq)
    gp = Gather(links, p, wp_in, wp)
    gf = Gather(links, p, wf_in, wf)
    go = Gather(links, p, out_own, wo)
    rq, rp, rf, ro = (Reduce(links, p, reduce_bufs[7 * i : 7 * i + 7]) for i in range(4))

    vec_base = links.take(8)
    vec_sent = []
    for i in range(1, 8):
        vec_sent.append(links.send(vec_in, vec_all.at[s], vec_base + i, p.at(i // 2, i % 2)))
    gq.start()
    out_base = links.take(1)
    out_sent = links.send(
        wo_in.at[pl.ds(pl.multiple_of((THIRD * j + BLOCK * (1 - c)) % 384, 16), BLOCK)], out_got, out_base, p.mate
    )

    def to_peers(src_of, dst, base):
        return [links.send(src_of(k), dst.at[j], base + k, p.peer(k)) for k in (1, 2, 3)]

    def await_peer(dst, base, k):
        slot = dst.at[xor(j, k)]
        links.copy(slot, slot, base + k, p.here).wait_recv()

    mask_base = links.take(4)
    to_peers(lambda k: mask_in, mk, mask_base)
    mk[j] = mask_in[...]
    vec_all[s] = vec_in[...]

    row = lax.broadcasted_iota(jnp.int32, (1024, D), 0)
    col = lax.broadcasted_iota(jnp.int32, (1024, D), 1)
    inside = (row & 127) < BLOCK
    place_m[...] = jnp.where(inside & (col == BLOCK * (row >> 7) + (row & 127)), 1.0, 0.0).astype(LOW)

    tokens = tok[...].astype(WIDE)
    unit, scale1 = normalize(tokens)
    unit1[...] = unit
    for i in range(1, 8):
        vec_sent[i - 1].wait_recv()
    small = mm(jnp.concatenate([vec_all[i] for i in range(8)], axis=1), place_m[...])
    half = j // 2
    pieces = [vec_all[2 * (i // 2) + half][8 + i % 2 : 9 + i % 2] for i in range(8)]
    fc_bias = mm(jnp.concatenate(pieces, axis=1), place_m[...])
    params[0:8] = small[0:8]
    params[8:9] = fc_bias
    nf[j] = (unit * params[0:1] + params[1:2]).astype(LOW)
    nf_base = links.take(4)
    to_peers(lambda k: nf.at[j], nf, nf_base)
    cot_base = links.take(4)
    to_peers(lambda k: cot, cots, cot_base)
    cots[j] = cot[...]

    out_sent.wait_recv()
    mine = wo_in[pl.ds(pl.multiple_of((THIRD * j + BLOCK * c) % 384, 16), BLOCK)]
    out_own[...] = jnp.where(c == half, mine, out_got[...])

    def of_heads(index):
        lane = lax.broadcasted_iota(jnp.int32, (D, THIRD), 0)
        out = lax.broadcasted_iota(jnp.int32, (D, THIRD), 1)
        return mm(params[index : index + 1].astype(LOW), jnp.where(lane == out + THIRD * j, 1.0, 0.0).astype(LOW))

    q_bias, v_bias = of_heads(2), of_heads(3)

    gq.step1()
    gp.start()
    gq.step2()
    gq.step3()
    gp.step1()
    gf.start()
    gq.finish()

    att_base = links.take(4)

    def attend(k, carry):
        r = xor(j, k)

        @pl.when(k > 0)
        def _():
            await_peer(nf, nf_base, k)
            await_peer(mk, mask_base, k)

        made = mm(nf[r], wq[...])
        query = (made[:, :THIRD] + q_bias).astype(LOW)
        keys = made[:, THIRD : 2 * THIRD].astype(LOW)
        values = (made[:, 2 * THIRD :] + v_bias).astype(LOW)
        qkv[r, :, 0:THIRD] = query
        qkv[r, :, 256 : 256 + THIRD] = keys
        qkv[r, :, 512 : 512 + THIRD] = values
        allowed = mk[r].astype(WIDE)
        allowed = jnp.concatenate([allowed] * 3, axis=0) > 0.5
        scores = jnp.where(allowed, mm_t(heads_of(query), keys) * (1.0 / math.sqrt(HD)), NEG)
        raised = jnp.exp(scores - jnp.max(scores, axis=-1, keepdims=True))
        probs = raised / jnp.sum(raised, axis=-1, keepdims=True)
        weights[r] = probs
        att[r] = heads_join(mm(probs.astype(LOW), values)).astype(LOW)

        @pl.when(k > 0)
        def _():
            links.copy(att.at[r], att_rx.at[j], att_base + k, p.peer(k)).start()

        return carry

    lax.fori_loop(0, 2, attend, 0)
    gp.step2()
    gp.step3()
    gf.step1()
    go.start()
    lax.fori_loop(2, 4, attend, 0)
    att_rx[j] = att[j]
    gf.step2()
    gf.step3()
    go.step1()
    gp.finish()

    total = tokens + params[4:5]
    for k in (0, 1, 2, 3):
        if k > 0:
            await_peer(att_rx, att_base, k)
        r = xor(j, k)
        total = total + mm(att_rx[r], wp[pl.ds(pl.multiple_of(r * THIRD, 16), THIRD)])
    res[...] = total
    unit, scale2 = normalize(total)
    unit2[...] = unit
    scales[:, 0:1] = scale1
    scales[:, 1:2] = scale2
    ns[j] = (unit * params[5:6] + params[6:7]).astype(LOW)
    ns_base = links.take(4)
    to_peers(lambda k: ns.at[j], ns, ns_base)

    go.step2()
    go.step3()
    gf.finish()
    go.finish()

    gns_base = links.take(4)
    acc[...] = jnp.zeros_like(acc)
    root = math.sqrt(2.0 / math.pi)

    def feed(k, carry):
        r = xor(j, k)

        @pl.when(k > 0)
        def _():
            await_peer(cots, cot_base, k)
            await_peer(ns, ns_base, k)

        grad_hidden = mm_t(cots[r], wo[...])
        pre = mm(ns[r], wf[...]) + params[8:9]
        square = pre * pre
        tanh = jnp.tanh(root * pre * (1.0 + 0.044715 * square))
        hid[r] = (0.5 * pre * (1.0 + tanh)).astype(LOW)
        slope = 0.5 * (1.0 + tanh) + 0.5 * pre * (1.0 - tanh * tanh) * (root * (1.0 + 3 * 0.044715 * square))
        grad_pre = grad_hidden * slope
        acc[0:1, :] += jnp.sum(grad_pre, axis=0, keepdims=True)
        gpl[r] = grad_pre.astype(LOW)
        gns_tx[r] = mm_t(gpl[r], wf[...]).astype(LOW)

        @pl.when(k > 0)
        def _():
            links.copy(gns_tx.at[r], gns_rx.at[j], gns_base + k, p.peer(k)).start()

        return carry

    lax.fori_loop(0, 4, feed, 0)
    op_base = links.take(4)

    def project(k, carry):
        r = xor(j, k)
        op_tx[r] = mm(hid[r], wo[...]).astype(LOW)

        @pl.when(k > 0)
        def _():
            links.copy(op_tx.at[r], op_rx.at[j], op_base + k, p.peer(k)).start()

        return carry

    lax.fori_loop(0, 4, project, 0)

    def whole(ref):
        return ref[...].reshape(4 * ROWS, -1)

    ro.fill(t_mm(whole(hid), whole(cots)))
    ro.pair()
    rf.fill(t_mm(whole(ns), whole(gpl)))
    rf.pair()
    ro.step1()

    grad = gns_tx[j].astype(WIDE)
    for k in (1, 2, 3):
        await_peer(gns_rx, gns_base, k)
        grad = grad + gns_rx[xor(j, k)].astype(WIDE)
    cot_own = cot[...].astype(WIDE)
    sums[5:6] = jnp.sum(grad * unit2[...], axis=0, keepdims=True)
    sums[6:7] = jnp.sum(grad, axis=0, keepdims=True)
    sums[7:8] = jnp.sum(cot_own, axis=0, keepdims=True)
    grad_res = cot_own + normalize_back(grad, unit2[...], scales[:, 1:2], params[5:6])
    gr[...] = grad_res
    sums[4:5] = jnp.sum(grad_res, axis=0, keepdims=True)
    grad_low = grad_res.astype(LOW)
    ga_base = links.take(4)
    for k in (1, 2, 3, 0):
        r = xor(j, k)
        ga_tx[r] = mm_t(grad_low, wp[pl.ds(pl.multiple_of(r * THIRD, 16), THIRD)]).astype(LOW)
        if k > 0:
            links.send(ga_tx.at[r], ga_rx.at[j], ga_base + k, p.peer(k))
    ga_rx[j] = ga_tx[j]
    rf.step1()
    ro.step2()
    for r in range(4):
        made = t_mm(att_rx[r], grad_low)
        for c_at in range(2):
            rp.part[r, c_at] = made[c_at * BLOCK : (c_at + 1) * BLOCK].astype(LOW)
    rp.pair()

    gnf_base = links.take(4)
    acc[8:9, :] = jnp.zeros((1, D), WIDE)

    def attend_back(k, carry):
        r = xor(j, k)

        @pl.when(k > 0)
        def _():
            await_peer(ga_rx, ga_base, k)

        grad_att = ga_rx[r]
        query = qkv[r, :, 0:THIRD]
        keys = qkv[r, :, 256 : 256 + THIRD]
        values = qkv[r, :, 512 : 512 + THIRD]
        probs = weights[r]
        stacked = heads_of(grad_att)
        grad_values = t_mm(probs.astype(LOW), stacked)
        grad_probs = mm_t(stacked, values)
        delta = jnp.sum(heads_of(grad_att.astype(WIDE) * att[r].astype(WIDE)), axis=-1, keepdims=True)
        grad_scores = (probs * (grad_probs - delta) * (1.0 / math.sqrt(HD))).astype(LOW)
        grad_query = heads_join(mm(grad_scores, keys))
        grad_keys = t_mm(grad_scores, heads_of(query))
        acc[8:9, 0:THIRD] += jnp.sum(grad_query, axis=0, keepdims=True)
        acc[8:9, 256 : 256 + THIRD] += jnp.sum(grad_values, axis=0, keepdims=True)
        made = jnp.concatenate([grad_query, grad_keys, grad_values], axis=1).astype(LOW)
        gproj[r] = made
        gnf_tx[r] = mm_t(made, wq[...]).astype(LOW)

        @pl.when(k > 0)
        def _():
            links.copy(gnf_tx.at[r], gnf_rx.at[j], gnf_base + k, p.peer(k)).start()

        return carry

    lax.fori_loop(0, 4, attend_back, 0)
    rq.fill(t_mm(whole(nf), whole(gproj)))
    rq.pair()
    rp.step1()
    rf.step2()

    def to_groups(final, dst):
        base = links.take(4)
        for k in (1, 2, 3):
            links.send(final, dst.at[j], base + k, p.peer(k))
        dst[j] = final[...]
        return base

    ro.finish(factor)
    do_base = links.take(4)
    do_recv = links.take(4)
    slot = (2 * j + c) % 4
    for k in (1, 2, 3):
        links.send(ro.final, do_ref.at[slot], do_base + k, (xor(j, k), 2 * z + half), do_recv + slot)
    across = links.copy(ro.final, do_ref.at[slot], do_base, p.mate, do_recv + slot)

    @pl.when(c == half)
    def _():
        do_ref[slot] = ro.final[...]

    @pl.when(c != half)
    def _():
        across.start()
        across.wait_send()

    rq.step1()
    rp.step2()
    rf.finish(factor)
    df_base = to_groups(rf.final, df_ref)

    grad = gnf_tx[j].astype(WIDE)
    for k in (1, 2, 3):
        await_peer(gnf_rx, gnf_base, k)
        grad = grad + gnf_rx[xor(j, k)].astype(WIDE)
    sums[0:1] = jnp.sum(grad * unit1[...], axis=0, keepdims=True)
    sums[1:2] = jnp.sum(grad, axis=0, keepdims=True)
    gt_ref[...] = gr[...] + normalize_back(grad, unit1[...], scales[:, 0:1], params[0:1])

    out = lax.broadcasted_iota(jnp.int32, (THIRD, D), 1)
    lane = lax.broadcasted_iota(jnp.int32, (THIRD, D), 0)
    spot = jnp.where(out == lane + THIRD * j, 1.0, 0.0).astype(LOW)
    for row_at, lane_at in ((2, 0), (3, 256)):
        parts = three(acc[8:9, lane_at : lane_at + THIRD])
        sums[row_at : row_at + 1] = mm(parts[0], spot) + mm(parts[1], spot) + mm(parts[2], spot)
    sums[8:16] = jnp.broadcast_to(acc[0:1, :], (8, D))
    parts = three(sums[...])
    spread_out = mm_t(parts[0], place_m[...]) + mm_t(parts[1], place_m[...]) + mm_t(parts[2], place_m[...])
    line = lax.broadcasted_iota(jnp.int32, (8, 128), 0)
    own_lines = (line >= 2 * (j % 2)) & (line < 2 * (j % 2) + 2)
    for i in range(8):
        vt[i, 0:8] = spread_out[0:8, 128 * i : 128 * i + 128]
        at = 256 * (i // 2)
        even, odd = spread_out[8:16, at : at + 128], spread_out[8:16, at + 128 : at + 256]
        picked = jnp.where((line & 1) == 0, even, odd)
        vt[i, 8:16] = jnp.where(own_lines & (half == i % 2), picked, 0.0)
    vt_base = links.take(8)
    vt_sent = []
    for i in range(1, 8):
        device = p.at(i // 2, i % 2)
        vt_sent.append(links.send(vt.at[device[1]], vr.at[i], vt_base + i, device))

    rp.finish(factor)
    dp_base = links.take(4)
    for k in (1, 2, 3):
        links.send(rp.final, dp_got.at[j], dp_base + k, p.peer(k))

    rq.step2()

    mine = vt[s]
    for i in range(1, 8):
        vt_sent[i - 1].wait_recv()
        mine = mine + vr[i]
    v2[...] = mine
    v2_base = links.take(4)
    to_peers(lambda k: v2, vr2, v2_base)

    made = res[...] + params[7:8] + op_tx[j].astype(WIDE)
    for k in (1, 2, 3):
        await_peer(op_rx, op_base, k)
        made = made + op_rx[xor(j, k)].astype(WIDE)
    y_ref[...] = made.astype(LOW)

    rq.finish(factor)
    dq_base = to_groups(rq.final, dq_ref)

    mine = rp.final[...].astype(WIDE)
    for k in (1, 2, 3):
        await_peer(dp_got, dp_base, k)
        mine = mine + dp_got[xor(j, k)].astype(WIDE)
    dp_ref[...] = mine.astype(LOW)
    mine = v2[...]
    for k in (1, 2, 3):
        await_peer(vr2, v2_base, k)
        mine = mine + vr2[xor(j, k)]
    dv_ref[...] = mine * factor

    for i in range(4):
        local = (2 * c + i // 2 == j) & (c == i % 2)

        @pl.when(jnp.logical_not(local))
        def _():
            links.copy(do_ref.at[i], do_ref.at[i], do_base, p.here, do_recv + i).wait_recv()

    for k in (1, 2, 3):
        await_peer(df_ref, df_base, k)
        await_peer(dq_ref, dq_base, k)
    for buf_of, dst, base in ((att, att_rx, att_base), (gns_tx, gns_rx, gns_base), (op_tx, op_rx, op_base), (gnf_tx, gnf_rx, gnf_base)):
        for k in (1, 2, 3):
            links.copy(buf_of.at[xor(j, k)], dst.at[j], base + k, p.peer(k)).wait_send()
    links.drain()


def vmem(*shape, kind=LOW):
    return pltpu.VMEM(shape, kind)


def fused_device(
    tokens,
    segment_ids,
    first_gain,
    first_shift,
    qkv_weight,
    qv_bias,
    proj_weight,
    proj_bias,
    second_gain,
    second_shift,
    fc_weight,
    fc_bias,
    out_weight,
    out_bias,
    cotangent,
):
    shards, reps = lax.axis_size("shard"), lax.axis_size("rep")
    factor = 1.0 / math.sqrt(ROWS * reps * shards)
    j = lax.axis_index("rep")
    segments = segment_ids[0]
    position = lax.iota(jnp.int32, ROWS)
    mask = ((segments[:, None] == segments[None, :]) & (position[None, :] <= position[:, None])).astype(LOW)
    fc_half = lax.dynamic_slice(fc_bias, (THIRD * (j % 2),), (THIRD,)).reshape(2, BLOCK)
    small = jnp.stack(
        [first_gain, first_shift, qv_bias[0], qv_bias[1], proj_bias, second_gain, second_shift, out_bias]
    )
    vec = jnp.pad(jnp.concatenate([small, fc_half]), ((0, 6), (0, 32)))
    wq = lax.dynamic_index_in_dim(qkv_weight.reshape(BLOCK, 3, 4, THIRD), j, 2, False).reshape(BLOCK, 3 * THIRD)
    wf = lax.dynamic_index_in_dim(fc_weight.reshape(BLOCK, 4, 4, THIRD), j, 2, False).reshape(BLOCK, D)

    def reduce_bufs(width):
        return [
            vmem(4, 2, BLOCK, width),
            vmem(4, BLOCK, width),
            vmem(4, BLOCK, width),
            vmem(2, BLOCK, width),
            vmem(BLOCK, width),
            vmem(BLOCK, width),
            vmem(BLOCK, width),
        ]

    blocks = lambda width, kind=LOW: vmem(4, ROWS, width, kind=kind)
    scratch = [
        pltpu.SemaphoreType.DMA((160,)),
        pltpu.SemaphoreType.DMA((160,)),
        vmem(8, 16, 128),
        blocks(D),
        blocks(128),
        blocks(D),
        vmem(D, 3 * THIRD),
        vmem(D, D),
        vmem(D, D),
        vmem(D, D),
        vmem(BLOCK, D),
        vmem(BLOCK, D),
        vmem(1024, D),
        vmem(16, D, kind=WIDE),
        blocks(D),
        vmem(4, 3 * ROWS, 128, kind=WIDE),
        blocks(THIRD),
        blocks(THIRD),
        vmem(ROWS, D, kind=WIDE),
        vmem(ROWS, D, kind=WIDE),
        vmem(ROWS, D, kind=WIDE),
        vmem(ROWS, 128, kind=WIDE),
        blocks(D),
        blocks(D),
        blocks(D),
        blocks(D),
        blocks(D),
        blocks(D),
        blocks(D),
        blocks(THIRD),
        blocks(THIRD),
        blocks(D),
        blocks(D),
        blocks(3 * THIRD),
        vmem(ROWS, D, kind=WIDE),
        vmem(16, D, kind=WIDE),
        vmem(16, D, kind=WIDE),
        vmem(8, 16, 128, kind=WIDE),
        vmem(8, 16, 128, kind=WIDE),
        vmem(16, 128, kind=WIDE),
        vmem(4, 16, 128, kind=WIDE),
        vmem(BLOCK, D),
        vmem(4, BLOCK, D),
    ]
    for width in (3 * THIRD, D, D, D):
        scratch += reduce_bufs(width)
    in_vmem = pl.BlockSpec(memory_space=pltpu.VMEM)
    y, grad_tokens, dq, dp, df, do, dv = pl.pallas_call(
        functools.partial(layer_kernel, factor),
        out_shape=(
            jax.ShapeDtypeStruct((ROWS, D), LOW),
            jax.ShapeDtypeStruct((ROWS, D), WIDE),
            jax.ShapeDtypeStruct((4, BLOCK, 3 * THIRD), LOW),
            jax.ShapeDtypeStruct((BLOCK, D), LOW),
            jax.ShapeDtypeStruct((4, BLOCK, D), LOW),
            jax.ShapeDtypeStruct((4, BLOCK, D), LOW),
            jax.ShapeDtypeStruct((16, 128), WIDE),
        ),
        in_specs=[in_vmem] * 8,
        out_specs=(in_vmem,) * 7,
        scratch_shapes=scratch,
        compiler_params=pltpu.CompilerParams(
            collective_id=0, has_side_effects=True, vmem_limit_bytes=56 * 1024 * 1024
        ),
    )(tokens, cotangent, mask, vec, wq, proj_weight, wf, out_weight)
    qkv_grad = dq.reshape(4, BLOCK, 3, THIRD).transpose(1, 2, 0, 3).reshape(BLOCK, 3 * D).astype(WIDE)
    fc_grad = df.reshape(4, BLOCK, 4, THIRD).transpose(1, 2, 0, 3).reshape(BLOCK, FF).astype(WIDE)
    out_grad = do.reshape(4 * BLOCK, D).astype(WIDE)
    sums = dv[:, :BLOCK]
    return (
        y,
        grad_tokens,
        sums[0],
        sums[1],
        qkv_grad,
        sums[2:4],
        dp.astype(WIDE),
        sums[4],
        sums[5],
        sums[6],
        fc_grad,
        sums[8:12].reshape(4 * BLOCK),
        out_grad,
        sums[7],
    )


def solution(mesh):
    return jax.shard_map(
        fused_device if dict(mesh.shape) == {"rep": 4, "shard": 8} else per_device,
        mesh=mesh,
        in_specs=(
            P(("rep", "shard"), None),
            P(("rep", "shard"), None),
            P("shard"),
            P("shard"),
            P("shard", None),
            P(None, "shard"),
            P("shard", None),
            P("shard"),
            P("shard"),
            P("shard"),
            P("shard", None),
            P("shard"),
            P("shard", None),
            P("shard"),
            P(("rep", "shard"), None),
        ),
        out_specs=(
            P(("rep", "shard"), None),
            P(("rep", "shard"), None),
            P("shard"),
            P("shard"),
            P("shard", None),
            P(None, "shard"),
            P("shard", None),
            P("shard"),
            P("shard"),
            P("shard"),
            P("shard", None),
            P("shard"),
            P("shard", None),
            P("shard"),
        ),
        check_vma=False,
    )
```

```python
import functools
import math

import jax
import jax.numpy as jnp
from jax import lax
from jax.experimental import pallas as pl
from jax.experimental.pallas import tpu as pltpu
from jax.sharding import PartitionSpec as P

D = 768
HEADS = 12
HD = 64
FF = 3072


EPSILON = 1e-05


def layer_norm(field, norm_gain, norm_shift):
    center = field - jnp.mean(field, axis=-1, keepdims=True)
    spread = jnp.mean(center * center, axis=-1, keepdims=True)
    return center * lax.rsqrt(spread + EPSILON) * norm_gain + norm_shift


def gelu_tanh(field):
    return jax.nn.gelu(field, approximate=True)


def head_split(matrix):
    return matrix.reshape(matrix.shape[0], HEADS, HD)


def masked_scores(query, keys, segments):
    rows = query.shape[0]
    scores = jnp.einsum(
        "qhd,khd->hqk", head_split(query), head_split(keys), preferred_element_type=jnp.float32
    ) * (1.0 / math.sqrt(HD))
    position = lax.iota(jnp.int32, rows)
    allowed = (segments[:, None] == segments[None, :]) & (position[None, :] <= position[:, None])
    return jnp.where(allowed[None], scores, -1e30)


def attend_forward(query, keys, values, segments):
    rows = query.shape[0]
    scores = masked_scores(query, keys, segments)
    row_max = jnp.max(scores, axis=-1, keepdims=True)
    row_total = jnp.sum(jnp.exp(scores - row_max), axis=-1, keepdims=True)
    logsum = row_max + jnp.log(row_total)
    probs = jnp.exp(scores - logsum).astype(jnp.bfloat16)
    attended = jnp.einsum(
        "hqk,khd->qhd", probs, head_split(values), preferred_element_type=jnp.float32
    )
    return (attended.reshape(rows, D).astype(jnp.bfloat16), logsum)


def attend_backward(query, keys, values, segments, attended, logsum, grad_attended):
    rows = query.shape[0]
    scores = masked_scores(query, keys, segments)
    weights = jnp.exp(scores - logsum)
    grad_heads = head_split(grad_attended)
    grad_values = jnp.einsum(
        "hqk,qhd->khd", weights.astype(jnp.bfloat16), grad_heads, preferred_element_type=jnp.float32
    )
    grad_probs = jnp.einsum(
        "qhd,khd->hqk", grad_heads, head_split(values), preferred_element_type=jnp.float32
    )
    delta = jnp.einsum(
        "qhd,qhd->hq", grad_heads, head_split(attended), preferred_element_type=jnp.float32
    )
    grad_scores = (weights * (grad_probs - delta[..., None]) * (1.0 / math.sqrt(HD))).astype(
        jnp.bfloat16
    )
    grad_query = jnp.einsum(
        "hqk,khd->qhd", grad_scores, head_split(keys), preferred_element_type=jnp.float32
    )
    grad_keys = jnp.einsum(
        "hqk,qhd->khd", grad_scores, head_split(query), preferred_element_type=jnp.float32
    )
    return (grad_query.reshape(rows, D), grad_keys.reshape(rows, D), grad_values.reshape(rows, D))


def exchange(field, axis, split, concat):
    return lax.all_to_all(field, axis, split_axis=split, concat_axis=concat, tiled=True)


def spread(field, axis):
    parts = lax.axis_size(axis)
    return exchange(jnp.broadcast_to(field[None], (parts,) + field.shape), axis, 0, 0)


def by_replica(field, shards, reps):
    rows = field.shape[0]
    return (
        field.reshape(shards, reps, rows // (shards * reps), -1).swapaxes(0, 1).reshape(rows, -1)
    )


def per_device(
    tokens,
    segment_ids,
    first_gain,
    first_shift,
    qkv_weight,
    qv_bias,
    proj_weight,
    proj_bias,
    second_gain,
    second_shift,
    fc_weight,
    fc_bias,
    out_weight,
    out_bias,
    cotangent,
):
    low = jnp.bfloat16
    segments = segment_ids[0]
    own_rows = tokens.shape[0]
    shards = lax.axis_size("shard")
    reps = lax.axis_size("rep")
    factor = 1.0 / math.sqrt(own_rows * reps * shards)
    small = jnp.stack(
        [first_gain, first_shift, qv_bias[0], qv_bias[1], proj_bias, second_gain, second_shift, out_bias]
    )
    small_full = lax.all_gather(small, "shard", axis=1, tiled=True).astype(jnp.float32)
    gain_one, shift_one, q_bias, v_bias, proj_bias_full, gain_two, shift_two, out_bias_full = (
        small_full[i] for i in range(8)
    )
    qkv_full = lax.all_gather(qkv_weight, "shard", axis=0, tiled=True)
    proj_full = lax.all_gather(proj_weight, "shard", axis=0, tiled=True)
    fc_cols = exchange(fc_weight, "shard", 1, 0)
    inputs = tokens.astype(jnp.float32)
    normed_f, first_back = jax.vjp(layer_norm, inputs, gain_one, shift_one)
    normed_first = normed_f.astype(low)
    projected = jnp.dot(normed_first, qkv_full, preferred_element_type=jnp.float32)
    query = (projected[:, :D] + q_bias).astype(low)
    keys = projected[:, D : 2 * D].astype(low)
    values = (projected[:, 2 * D :] + v_bias).astype(low)
    attended, logsum = attend_forward(query, keys, values, segments)
    residual = (
        inputs + jnp.dot(attended, proj_full, preferred_element_type=jnp.float32) + proj_bias_full
    )
    cot_f = cotangent.astype(jnp.float32)
    normed_s, second_back = jax.vjp(layer_norm, residual, gain_two, shift_two)
    normed_all = lax.all_gather(normed_s.astype(low), "shard", axis=0, tiled=True)
    cot_later, normed_all = lax.optimization_barrier((cotangent, normed_all))
    cot_all = lax.all_gather(cot_later, "shard", axis=0, tiled=True)
    pre_act = jnp.dot(normed_all, fc_cols, preferred_element_type=jnp.float32) + fc_bias.astype(
        jnp.float32
    )
    activated, gelu_back = jax.vjp(gelu_tanh, pre_act)
    hidden = activated.astype(low)
    grad_hidden = jnp.dot(cot_all, out_weight.T, preferred_element_type=jnp.float32)
    (grad_pre,) = gelu_back(grad_hidden)
    grad_pre_low = grad_pre.astype(low)
    grad_normed_part = jnp.dot(grad_pre_low, fc_cols.T, preferred_element_type=jnp.float32).astype(low)
    grad_normed_low = lax.psum_scatter(grad_normed_part, "shard", scatter_dimension=0, tiled=True)
    term_out_weight = jnp.dot(hidden.T, cot_all, preferred_element_type=jnp.float32) * factor
    term_fc_weight = jnp.dot(normed_all.T, grad_pre_low, preferred_element_type=jnp.float32) * factor
    out_part = jnp.dot(hidden, out_weight, preferred_element_type=jnp.float32).astype(low)
    ff_terms = jnp.concatenate(
        [
            term_out_weight.astype(low).reshape(reps, -1, D),
            by_replica(term_fc_weight.astype(low), shards, reps).reshape(reps, -1, D),
        ],
        axis=1,
    )
    ff_sum = jnp.sum(exchange(ff_terms, "rep", 0, 0).astype(jnp.float32), axis=0).astype(low)
    first_later, attended_later, grad_normed_low, ff_sum = lax.optimization_barrier(
        (normed_first, attended, grad_normed_low, ff_sum)
    )
    first_all = lax.all_gather(first_later, "shard", axis=0, tiled=True)
    grad_normed_second = grad_normed_low.astype(jnp.float32)

    grad_from_norm, second_gain_sum, second_shift_sum = second_back(grad_normed_second)
    grad_residual = cot_f + grad_from_norm
    grad_residual_low = grad_residual.astype(low)
    grad_residual_all = lax.all_gather(grad_residual_low, "shard", axis=0, tiled=True)
    attended_cols = exchange(attended_later, "shard", 1, 0)
    grad_attended = jnp.dot(
        grad_residual_low, proj_full.T, preferred_element_type=jnp.float32
    ).astype(low)
    out_rows = out_weight.shape[0] // reps
    out_piece = ff_sum[:out_rows]
    fc_piece = ff_sum[out_rows:].reshape(D // reps, -1)
    fc_piece = exchange(fc_piece, "shard", 0, 1)
    ff_all = spread(jnp.concatenate([out_piece, fc_piece.reshape(-1, D)]), "rep").astype(jnp.float32)

    grad_query, grad_keys, grad_values = attend_backward(
        query, keys, values, segments, attended, logsum, grad_attended
    )
    grad_projected = jnp.concatenate([grad_query, grad_keys, grad_values], axis=1).astype(low)
    grad_projected, ff_all = lax.optimization_barrier((grad_projected, ff_all))
    out_grad = ff_all[:, :out_rows].reshape(-1, D)
    fc_grad = ff_all[:, out_rows:].reshape(-1, FF)
    grad_cols = exchange(grad_projected, "shard", 1, 0)
    grad_normed_first = jnp.dot(grad_projected, qkv_full.T, preferred_element_type=jnp.float32)
    out_later, grad_cols = lax.optimization_barrier((out_part, grad_cols))
    out_sum = lax.psum_scatter(out_later, "shard", scatter_dimension=0, tiled=True)
    result = (residual + out_sum.astype(jnp.float32) + out_bias_full).astype(low)
    term_qkv_weight = jnp.dot(first_all.T, grad_cols, preferred_element_type=jnp.float32) * factor
    term_proj_weight = (
        jnp.dot(attended_cols.T, grad_residual_all, preferred_element_type=jnp.float32) * factor
    )
    attn_terms = jnp.concatenate(
        [
            term_proj_weight.astype(low).reshape(reps, -1, D),
            by_replica(term_qkv_weight.astype(low), shards, reps).reshape(reps, -1, D),
        ],
        axis=1,
    )
    attn_sum = jnp.sum(exchange(attn_terms, "rep", 0, 0).astype(jnp.float32), axis=0).astype(low)
    proj_rows = proj_weight.shape[0] // reps
    proj_piece = attn_sum[:proj_rows]
    qkv_piece = attn_sum[proj_rows:].reshape(D // reps, -1)
    qkv_piece = exchange(qkv_piece, "shard", 0, 1)
    attn_all = spread(jnp.concatenate([proj_piece, qkv_piece.reshape(-1, D)]), "rep").astype(
        jnp.float32
    )
    proj_grad = attn_all[:, :proj_rows].reshape(-1, D)
    qkv_grad = attn_all[:, proj_rows:].reshape(-1, 3 * D)

    grad_input_norm, first_gain_sum, first_shift_sum = first_back(grad_normed_first)
    grad_inputs = grad_residual + grad_input_norm
    terms = jnp.stack(
        [
            first_gain_sum,
            first_shift_sum,
            jnp.sum(grad_query, axis=0),
            jnp.sum(grad_values, axis=0),
            jnp.sum(grad_residual, axis=0),
            second_gain_sum,
            second_shift_sum,
            jnp.sum(cot_f, axis=0),
        ]
    )
    count = terms.shape[0]
    terms = terms.reshape(count, shards, -1).swapaxes(0, 1).reshape(shards, -1)
    own_terms = jnp.concatenate(
        [jnp.sum(exchange(terms, "shard", 0, 0), axis=0), jnp.sum(grad_pre, axis=0)]
    )
    sums = jnp.sum(spread(own_terms, "rep"), axis=0) * factor
    own_cols = D // shards
    fc_bias_grad = sums[count * own_cols :]
    sums = sums[: count * own_cols].reshape(count, own_cols)
    return (
        result,
        grad_inputs,
        sums[0],
        sums[1],
        qkv_grad,
        sums[2:4],
        proj_grad,
        sums[4],
        sums[5],
        sums[6],
        fc_grad,
        fc_bias_grad,
        out_grad,
        sums[7],
    )

MESH = pl.DeviceIdType.MESH
LOW = jnp.bfloat16
WIDE = jnp.float32
ROWS = 128
BLOCK = 96
THIRD = 192
NEG = -1e30


def xor(a, b):
    return (a // 2 + b // 2) % 2 * 2 + (a + b) % 2


def mm(a, b):
    return jnp.dot(a, b, preferred_element_type=WIDE)


def mm_t(a, b):
    return lax.dot_general(a, b, (((1,), (1,)), ((), ())), preferred_element_type=WIDE)


def t_mm(a, b):
    return lax.dot_general(a, b, (((0,), (0,)), ((), ())), preferred_element_type=WIDE)


def three(field):
    first = field.astype(LOW)
    rest = field - first.astype(WIDE)
    second = rest.astype(LOW)
    return first, second, (rest - second.astype(WIDE)).astype(LOW)


def normalize(field):
    center = field - jnp.mean(field, axis=-1, keepdims=True)
    scale = lax.rsqrt(jnp.mean(center * center, axis=-1, keepdims=True) + EPSILON)
    return center * scale, scale


def normalize_back(grad, unit, scale, gain):
    inner = grad * gain
    mean = jnp.mean(inner, axis=-1, keepdims=True)
    along = jnp.mean(inner * unit, axis=-1, keepdims=True)
    return scale * (inner - mean - unit * along)


def heads_of(field):
    lane = lax.broadcasted_iota(jnp.int32, field.shape, 1)
    zero = jnp.zeros_like(field)
    return jnp.concatenate(
        [jnp.where((lane >= h * HD) & (lane < (h + 1) * HD), field, zero) for h in range(3)], axis=0
    )


def heads_join(stacked):
    lane = lax.broadcasted_iota(jnp.int32, (ROWS, THIRD), 1)
    return jnp.where(
        lane < HD, stacked[:ROWS], jnp.where(lane < 2 * HD, stacked[ROWS : 2 * ROWS], stacked[2 * ROWS :])
    )


class Links:
    def __init__(self, sends, recvs):
        self.sends, self.recvs, self.used, self.open, self.later = sends, recvs, 0, [], []

    def take(self, count=1):
        self.used += count
        return self.used - count

    def copy(self, src, dst, index, device, recv_index=None):
        recv_index = index if recv_index is None else recv_index
        return pltpu.make_async_remote_copy(
            src_ref=src,
            dst_ref=dst,
            send_sem=self.sends.at[index],
            recv_sem=self.recvs.at[recv_index],
            device_id=device,
            device_id_type=MESH,
        )

    def send(self, src, dst, index, device, recv_index=None):
        made = self.copy(src, dst, index, device, recv_index)
        made.start()
        self.open.append(made)
        return made

    def drain(self):
        for made in self.open:
            made.wait_send()
        for copies in self.later:
            for made in copies():
                made.wait_send()


class Gather:
    def __init__(self, links, place, own, full):
        self.links, self.place, self.own, self.full = links, place, own, full
        self.base = links.take(7)

    def slot(self, z, c):
        return self.full.at[pl.ds(pl.multiple_of((2 * z + c) * BLOCK, 16), BLOCK)]

    def arrived(self, which, slot):
        self.links.copy(slot, slot, self.base + which, self.place.here).wait_recv()

    def pass_on(self, which, slot, device):
        self.links.send(slot, slot, self.base + which, device)

    def two(self):
        p = self.place
        self.links.send(self.own, self.slot(p.z, p.c), self.base, p.two)

    def one(self):
        p = self.place
        mine = self.slot(p.z, p.c)
        self.links.send(self.own, mine, self.base + 1, p.one)
        self.links.send(self.own, mine, self.base + 2, p.mate)
        mine[...] = self.own[...]

    def step1(self):
        p = self.place
        slot = self.slot(xor(p.z, 2), p.c)
        self.arrived(0, slot)
        self.pass_on(3, slot, p.one)
        self.pass_on(4, slot, p.mate)

    def step2(self):
        p = self.place
        slot = self.slot(xor(p.z, 1), p.c)
        self.arrived(1, slot)
        self.pass_on(5, slot, p.mate)

    def step3(self):
        p = self.place
        slot = self.slot(xor(p.z, 3), p.c)
        self.arrived(3, slot)
        self.pass_on(6, slot, p.mate)

    def finish(self):
        p = self.place
        for which, flip in ((2, 0), (4, 2), (5, 1), (6, 3)):
            self.arrived(which, self.slot(xor(p.z, flip), 1 - p.c))


class Across:
    def __init__(self, links, place, buf, cut):
        self.links, self.place, self.buf, self.cut = links, place, buf, cut
        self.base = links.take(4)
        links.later.append(self.copies)

    def part(self, k, second):
        slot = self.buf.at[xor(self.place.j, k)]
        rows = self.buf.shape[1]
        return slot.at[self.cut : rows] if second else slot.at[0 : self.cut]

    def copy(self, which):
        p, links = self.place, self.links
        src = self.buf.at[p.j] if which < 2 else self.part(which - 1, which == 3)
        return links.copy(src, src, self.base + which, p.peer((1, 2, 2, 1)[which]))

    def copies(self):
        return [self.copy(which) for which in range(4)]

    def arrived(self, which, slot):
        self.links.copy(slot, slot, self.base + which, self.place.here).wait_recv()

    def start(self):
        self.copy(0).start()
        self.copy(1).start()

    def step1(self):
        self.arrived(0, self.buf.at[xor(self.place.j, 1)])
        self.copy(2).start()

    def step2(self):
        self.arrived(1, self.buf.at[xor(self.place.j, 2)])
        self.copy(3).start()

    def finish(self):
        self.arrived(2, self.part(3, False))
        self.arrived(3, self.part(3, True))

    def step(self, k):
        pl.when(k == 1)(self.step1)
        pl.when(k == 2)(self.step2)
        pl.when(k == 3)(self.finish)


class Reduce:
    def __init__(self, links, place, bufs):
        self.links, self.place = links, place
        self.part, self.got, self.total, self.near, self.second, self.far, self.final = bufs
        self.base = links.take(4)

    def fill(self, full):
        for z in range(4):
            for c in range(2):
                at = (2 * z + c) * BLOCK
                self.part[z, c] = full[at : at + BLOCK].astype(LOW)

    def pair(self):
        p = self.place
        self.sent = self.links.send(self.part.at[:, 1 - p.c], self.got, self.base, p.mate)

    def step1(self):
        p = self.place
        self.sent.wait_recv()
        for z in range(4):
            self.total[z] = (self.part[z, p.c].astype(WIDE) + self.got[z].astype(WIDE)).astype(LOW)
        self.first = [
            self.links.send(self.total.at[xor(p.z, 3)], self.near.at[1], self.base + 1, p.one),
            self.links.send(self.total.at[xor(p.z, 1)], self.near.at[0], self.base + 2, p.one),
        ]

    def step2(self):
        p = self.place
        self.first[0].wait_recv()
        self.second[...] = (self.total[xor(p.z, 2)].astype(WIDE) + self.near[1].astype(WIDE)).astype(LOW)
        self.last = self.links.send(self.second, self.far, self.base + 3, p.two)

    def finish(self, factor):
        p = self.place
        self.first[1].wait_recv()
        self.last.wait_recv()
        whole = self.total[p.z].astype(WIDE) + self.near[0].astype(WIDE) + self.far[...].astype(WIDE)
        self.final[...] = (whole * factor).astype(LOW)


class Place:
    def __init__(self):
        self.j, self.s = lax.axis_index("rep"), lax.axis_index("shard")
        self.z, self.c = self.s // 2, self.s % 2
        self.here = (self.j, self.s)
        self.mate = self.at(0, 1)
        self.one = self.at(1, 0)
        self.two = self.at(2, 0)

    def at(self, flip_z, flip_c):
        return (self.j, 2 * xor(self.z, flip_z) + (self.c + flip_c) % 2)

    def peer(self, k):
        return (xor(self.j, k), self.s)


TILES = tuple(
    (t, max(96 * t, 144 * q) - 144 * q, min(96 * t + 96, 144 * q + 144) - 144 * q, q, max(96 * t, 144 * q) - 96 * t)
    for t in range(6)
    for q in range(4)
    if max(96 * t, 144 * q) < min(96 * t + 96, 144 * q + 144)
)


def layer_kernel(
    factor,
    tok_hbm, cot_hbm, seg_in, g1_in, s1_in, qvb_in, pb_in, g2_in, s2_in, fb_in, ob_in, qkv_hbm, wp_hbm, fc_hbm, wo_hbm,
    y_hbm, gt_hbm, dq_hbm, dp_hbm, df_hbm, do_hbm, dv_hbm,
    sends, recvs, locals_,
    tok, qkv_in, wp_in, fc_in, wo_in, y_ref, gt_ref, dq_ref, dp_ref, df_ref, do_ref, dv_ref,
    vec_wide, vec_in, vec_all, nf, seg, cots, wq_in, wf_in, wq, wp, wf, wo, out_own, out_got, place_m, params,
    qkv, weights, att, att_rx, res, unit1, unit2, scales,
    ns, hid, slope, gpl, gns_tx, gns_rx, op_tx, op_rx, ga_tx, ga_rx, gnf_tx, gnf_rx, gproj, gr,
    sums, acc, vt, vr, v2, vr2, dq_all, df_all,
    pt_own, pq, pp, pp_got, pp_sum, pp_rx, pz, pz_near, pz_second, pz_far, pp_all,
    *reduce_bufs,
):
    p = Place()
    j, s, z, c = p.j, p.s, p.z, p.c
    half = j // 2
    odd = j % 2 == 1
    links = Links(sends, recvs)

    def local(src, dst, index):
        made = pltpu.make_async_copy(src, dst, locals_.at[index])
        made.start()
        return made

    load_qkv = local(qkv_hbm, qkv_in, 0)
    load_wp = local(wp_hbm, wp_in, 1)
    load_cot = local(cot_hbm, cots.at[j], 2)
    load_fc = local(fc_hbm, fc_in, 3)
    load_wo = local(wo_hbm, wo_in, 4)
    load_tok = local(tok_hbm, tok, 5)

    partners = [p.at(fz, fc) for fz in range(4) for fc in range(2) if (fz, fc) != (0, 0)]
    partners += [p.peer(k) for k in (1, 2, 3)]
    partners += [(xor(j, k), 2 * z + 1 - c) for k in (1, 2, 3)]
    barrier = pltpu.get_barrier_semaphore()
    for device in partners:
        pl.semaphore_signal(barrier, inc=1, device_id=device, device_id_type=MESH)

    def columns(src, dst, count):
        for i in range(count):
            wide = src[:, pl.ds(pl.multiple_of(D * i + 128 * (3 * j // 2), 128), 256)]
            dst[:, THIRD * i : THIRD * (i + 1)] = jnp.where(odd, wide[:, 64:], wide[:, :THIRD])

    vec_wide[...] = jnp.zeros_like(vec_wide)
    for i, ref in enumerate((g1_in, s1_in, None, None, pb_in, g2_in, s2_in, ob_in)):
        if ref is not None:
            vec_wide[i : i + 1, 0:BLOCK] = ref[...].astype(WIDE)
    vec_wide[2:4, 0:BLOCK] = qvb_in[...].astype(WIDE)
    bias_row = fb_in[...].astype(WIDE)
    for i in range(2):
        low_part, high_part = (bias_row[:, THIRD * h + BLOCK * i : THIRD * h + BLOCK * (i + 1)] for h in range(2))
        vec_wide[8 + i : 9 + i, 0:BLOCK] = jnp.where(odd, high_part, low_part)
    vec_in[...] = vec_wide[...].astype(LOW)
    seg[j] = jnp.broadcast_to(seg_in[...].astype(WIDE), (8, ROWS))
    load_qkv.wait()
    columns(qkv_in, wq_in, 3)
    load_wp.wait()
    for t in range(6):
        pt_own[BLOCK * t : BLOCK * (t + 1)] = wp_in[:, 128 * t : 128 * (t + 1)]

    gq = Gather(links, p, wq_in, wq)
    gf = Gather(links, p, wf_in, wf)
    go = Gather(links, p, out_own, wo)
    rq, rf, ro = (Reduce(links, p, reduce_bufs[7 * i : 7 * i + 7]) for i in range(3))
    across_nf = Across(links, p, nf, ROWS // 2)
    across_cot = Across(links, p, cots, ROWS // 2)
    across_ns = Across(links, p, ns, ROWS // 2)
    across_df = Across(links, p, df_all, BLOCK // 2)
    across_dq = Across(links, p, dq_all, BLOCK // 2)
    load_cot.wait()
    pl.semaphore_wait(barrier, len(partners))

    vec_base = links.take(8)
    vec_sent = []
    for i in range(1, 8):
        vec_sent.append(links.send(vec_in, vec_all.at[s], vec_base + i, p.at(i // 2, i % 2)))
    gq.two()
    gq.one()

    def to_peers(src_of, dst, base):
        return [links.send(src_of(k), dst.at[j], base + k, p.peer(k)) for k in (1, 2, 3)]

    def await_peer(dst, base, k):
        slot = dst.at[xor(j, k)]
        links.copy(slot, slot, base + k, p.here).wait_recv()

    quarter = pt_own.at[pl.ds(pl.multiple_of(144 * j, 16), 144)]
    pq_base = links.take(3)
    pq[j, c, z] = pt_own[pl.ds(pl.multiple_of(144 * j, 16), 144)]
    links.send(quarter, pq.at[j, c, z], pq_base, p.two)
    links.send(quarter, pq.at[j, c, z], pq_base + 1, p.one)

    def await_quarter(which, flip):
        slot = pq.at[j, c, xor(z, flip)]
        links.copy(slot, slot, pq_base + which, p.here).wait_recv()

    seg_base = links.take(4)
    to_peers(lambda k: seg.at[j], seg, seg_base)
    across_cot.start()
    load_wo.wait()
    out_base = links.take(1)
    out_sent = links.send(
        wo_in.at[pl.ds(pl.multiple_of((THIRD * j + BLOCK * (1 - c)) % 384, 16), BLOCK)], out_got, out_base, p.mate
    )
    load_fc.wait()
    columns(fc_in, wf_in, 4)
    gf.two()
    vec_all[s] = vec_in[...]

    row = lax.broadcasted_iota(jnp.int32, (1024, D), 0)
    col = lax.broadcasted_iota(jnp.int32, (1024, D), 1)
    inside = (row & 127) < BLOCK
    place_m[...] = jnp.where(inside & (col == BLOCK * (row >> 7) + (row & 127)), 1.0, 0.0).astype(LOW)

    load_tok.wait()
    tokens = tok[...].astype(WIDE)
    unit, scale1 = normalize(tokens)
    unit1[...] = unit
    for i in range(1, 8):
        vec_sent[i - 1].wait_recv()
    small = mm(jnp.concatenate([vec_all[i] for i in range(8)], axis=1), place_m[...])
    pieces = [vec_all[2 * (i // 2) + half][8 + i % 2 : 9 + i % 2] for i in range(8)]
    fc_bias = mm(jnp.concatenate(pieces, axis=1), place_m[...])
    params[0:8] = small[0:8]
    params[8:9] = fc_bias
    nf[j] = (unit * params[0:1] + params[1:2]).astype(LOW)
    across_nf.start()

    out_sent.wait_recv()
    mine = wo_in[pl.ds(pl.multiple_of((THIRD * j + BLOCK * c) % 384, 16), BLOCK)]
    out_own[...] = jnp.where(c == half, mine, out_got[...])

    def of_heads(index):
        lane = lax.broadcasted_iota(jnp.int32, (D, THIRD), 0)
        out = lax.broadcasted_iota(jnp.int32, (D, THIRD), 1)
        return mm(params[index : index + 1].astype(LOW), jnp.where(lane == out + THIRD * j, 1.0, 0.0).astype(LOW))

    q_bias, v_bias = of_heads(2), of_heads(3)

    gq.step1()
    await_quarter(0, 2)
    links.send(pq.at[j, c, xor(z, 2)], pq.at[j, c, xor(z, 2)], pq_base + 2, p.one)
    gf.one()
    go.two()
    gq.step2()
    await_quarter(1, 1)
    across_cot.step1()
    across_cot.step2()
    gq.step3()
    await_quarter(2, 3)
    plane_base = links.take(4)
    for k in (1, 2):
        links.send(pq.at[j, c], pq.at[j, c], plane_base + k, p.peer(k))
    gq.finish()

    att_base = links.take(4)

    def attend(k, carry):
        r = xor(j, k)
        across_nf.step(k)

        @pl.when(k > 0)
        def _():
            await_peer(seg, seg_base, k)

        made = mm(nf[r], wq[...])
        query = (made[:, :THIRD] + q_bias).astype(LOW)
        keys = made[:, THIRD : 2 * THIRD].astype(LOW)
        values = (made[:, 2 * THIRD :] + v_bias).astype(LOW)
        qkv[r, :, 0:THIRD] = query
        qkv[r, :, 256 : 256 + THIRD] = keys
        qkv[r, :, 512 : 512 + THIRD] = values
        across = jnp.broadcast_to(seg[r, 0:1], (ROWS, ROWS))
        row_at = lax.broadcasted_iota(jnp.int32, (ROWS, ROWS), 0)
        col_at = lax.broadcasted_iota(jnp.int32, (ROWS, ROWS), 1)
        allowed = jnp.where((across == across.T) & (col_at <= row_at), 1.0, 0.0)
        scores = jnp.where(
            jnp.concatenate([allowed] * 3, axis=0) > 0.5, mm_t(heads_of(query), keys) * (1.0 / math.sqrt(HD)), NEG
        )
        raised = jnp.exp(scores - jnp.max(scores, axis=-1, keepdims=True))
        probs = raised / jnp.sum(raised, axis=-1, keepdims=True)
        weights[r] = probs
        att[r] = heads_join(mm(probs.astype(LOW), values)).astype(LOW)

        @pl.when(k > 0)
        def _():
            links.copy(att.at[r], att_rx.at[j], att_base + k, p.peer(k)).start()

        return carry

    lax.fori_loop(0, 3, attend, 0)
    gf.step1()
    go.one()
    lax.fori_loop(3, 4, attend, 0)
    att_rx[j] = att[j]

    def await_plane(k, which):
        slot = pq.at[xor(j, k), c]
        part = slot.at[0:2] if which == 0 else slot.at[2:4] if which == 1 else slot
        return part, plane_base + (k if which == 2 else 3 * which)

    for k, part in ((1, 0), (2, 1)):
        slot, index = await_plane(k, 2)
        links.copy(slot, slot, index, p.here).wait_recv()
        slot, _ = await_plane(k, part)
        links.send(slot, slot, plane_base + 3 * part, p.peer(3 - k))
    for part in (0, 1):
        slot, index = await_plane(3, part)
        links.copy(slot, slot, index, p.here).wait_recv()
    mate_base = links.take(1)
    links.send(pq.at[:, c], pq.at[:, c], mate_base, p.mate)
    go.step1()
    links.copy(pq.at[:, 1 - c], pq.at[:, 1 - c], mate_base, p.here).wait_recv()

    def assemble(i, carry):
        for t, a, b, at, to in TILES:
            top = pl.multiple_of(BLOCK * i + to, 16)
            wp[pl.ds(top, b - a), 128 * t : 128 * (t + 1)] = pq[at, i % 2, i // 2, a:b]
        return carry

    lax.fori_loop(0, 8, assemble, 0)

    total = tokens + params[4:5]
    for k in (0, 1, 2, 3):
        if k > 0:
            await_peer(att_rx, att_base, k)
        r = xor(j, k)
        total = total + mm(att_rx[r], wp[pl.ds(pl.multiple_of(r * THIRD, 16), THIRD)])
    res[...] = total
    unit, scale2 = normalize(total)
    unit2[...] = unit
    scales[:, 0:1] = scale1
    scales[:, 1:2] = scale2
    ns[j] = (unit * params[5:6] + params[6:7]).astype(LOW)
    across_ns.start()
    gf.step2()
    gf.step3()
    gf.finish()

    op_base = links.take(4)
    acc[...] = jnp.zeros_like(acc)
    root = math.sqrt(2.0 / math.pi)

    def prepare(k, carry):
        r = xor(j, k)
        across_ns.step(k)
        pre = mm(ns[r], wf[...]) + params[8:9]
        square = pre * pre
        tanh = jnp.tanh(root * pre * (1.0 + 0.044715 * square))
        hid[r] = (0.5 * pre * (1.0 + tanh)).astype(LOW)
        slope[r] = 0.5 * (1.0 + tanh) + 0.5 * pre * (1.0 - tanh * tanh) * (root * (1.0 + 3 * 0.044715 * square))
        return carry

    def project(k, carry):
        r = xor(j, k)
        op_tx[r] = mm(hid[r], wo[...]).astype(LOW)

        @pl.when(k > 0)
        def _():
            links.copy(op_tx.at[r], op_rx.at[j], op_base + k, p.peer(k)).start()

        return carry

    lax.fori_loop(0, 1, prepare, 0)
    go.step2()
    go.step3()
    go.finish()
    lax.fori_loop(1, 3, lambda k, carry: project(k, prepare(k, carry)), 0)
    lax.fori_loop(3, 4, prepare, 0)
    across_cot.finish()

    def whole(ref):
        return ref[...].reshape(4 * ROWS, -1)

    ro.fill(t_mm(whole(hid), whole(cots)))
    ro.pair()
    gns_base = links.take(4)

    def feed(i, carry):
        k = (i + 1) % 4
        r = xor(j, k)
        grad_pre = mm_t(cots[r], wo[...]) * slope[r]
        acc[0:1, :] += jnp.sum(grad_pre, axis=0, keepdims=True)
        gpl[r] = grad_pre.astype(LOW)
        gns_tx[r] = mm_t(gpl[r], wf[...]).astype(LOW)

        @pl.when(k > 0)
        def _():
            links.copy(gns_tx.at[r], gns_rx.at[j], gns_base + k, p.peer(k)).start()

        return carry

    lax.fori_loop(0, 4, feed, 0)
    ro.step1()
    rf.fill(t_mm(whole(ns), whole(gpl)))
    rf.pair()
    lax.fori_loop(3, 4, project, 0)
    rf.step1()
    ro.step2()

    grad = gns_tx[j].astype(WIDE)
    for k in (1, 2, 3):
        await_peer(gns_rx, gns_base, k)
        grad = grad + gns_rx[xor(j, k)].astype(WIDE)
    cot_own = cots[j].astype(WIDE)
    sums[5:6] = jnp.sum(grad * unit2[...], axis=0, keepdims=True)
    sums[6:7] = jnp.sum(grad, axis=0, keepdims=True)
    sums[7:8] = jnp.sum(cot_own, axis=0, keepdims=True)
    grad_res = cot_own + normalize_back(grad, unit2[...], scales[:, 1:2], params[5:6])
    gr[...] = grad_res
    sums[4:5] = jnp.sum(grad_res, axis=0, keepdims=True)
    grad_low = grad_res.astype(LOW)
    ga_base = links.take(4)
    for k in (3, 1, 2, 0):
        r = xor(j, k)
        ga_tx[r] = mm_t(grad_low, wp[pl.ds(pl.multiple_of(r * THIRD, 16), THIRD)]).astype(LOW)
        if k > 0:
            links.send(ga_tx.at[r], ga_rx.at[j], ga_base + k, p.peer(k))
    ga_rx[j] = ga_tx[j]
    lax.fori_loop(0, 1, project, 0)
    for r in range(4):
        made = t_mm(att_rx[r], grad_low)
        for c_at in range(2):
            for t, a, b, at, to in TILES:
                top = BLOCK * c_at + to
                pp[c_at, at, r, a:b] = made[top : top + b - a, 128 * t : 128 * (t + 1)].astype(LOW)
    pp_base = links.take(1)
    pp_sent = links.send(pp.at[1 - c], pp_got, pp_base, p.mate)
    rf.step2()

    gnf_base = links.take(4)
    acc[8:9, :] = jnp.zeros((1, D), WIDE)

    def attend_back(k, carry):
        r = xor(j, k)

        @pl.when(k > 0)
        def _():
            await_peer(ga_rx, ga_base, k)

        grad_att = ga_rx[r]
        query = qkv[r, :, 0:THIRD]
        keys = qkv[r, :, 256 : 256 + THIRD]
        values = qkv[r, :, 512 : 512 + THIRD]
        probs = weights[r]
        stacked = heads_of(grad_att)
        grad_values = t_mm(probs.astype(LOW), stacked)
        grad_probs = mm_t(stacked, values)
        delta = jnp.sum(heads_of(grad_att.astype(WIDE) * att[r].astype(WIDE)), axis=-1, keepdims=True)
        grad_scores = (probs * (grad_probs - delta) * (1.0 / math.sqrt(HD))).astype(LOW)
        grad_query = heads_join(mm(grad_scores, keys))
        grad_keys = t_mm(grad_scores, heads_of(query))
        acc[8:9, 0:THIRD] += jnp.sum(grad_query, axis=0, keepdims=True)
        acc[8:9, 256 : 256 + THIRD] += jnp.sum(grad_values, axis=0, keepdims=True)
        made = jnp.concatenate([grad_query, grad_keys, grad_values], axis=1).astype(LOW)
        gproj[r] = made
        gnf_tx[r] = mm_t(made, wq[...]).astype(LOW)

        @pl.when(k > 0)
        def _():
            links.copy(gnf_tx.at[r], gnf_rx.at[j], gnf_base + k, p.peer(k)).start()

        return carry

    lax.fori_loop(0, 4, attend_back, 0)
    rq.fill(t_mm(whole(nf), whole(gproj)))
    rq.pair()
    pp_sent.wait_recv()
    pp_sum[...] = (pp[c].astype(WIDE) + pp_got[...].astype(WIDE)).astype(LOW)
    prx_base = links.take(4)
    for k in (1, 2, 3):
        links.send(pp_sum.at[xor(j, k)], pp_rx.at[j], prx_base + k, p.peer(k))
    rq.step1()

    ro.finish(factor)
    do_base = links.take(4)
    do_recv = links.take(4)
    slot = (2 * j + c) % 4
    for k in (1, 2, 3):
        links.send(ro.final, do_ref.at[slot], do_base + k, (xor(j, k), 2 * z + half), do_recv + slot)
    across = links.copy(ro.final, do_ref.at[slot], do_base, p.mate, do_recv + slot)

    @pl.when(c == half)
    def _():
        do_ref[slot] = ro.final[...]

    @pl.when(c != half)
    def _():
        across.start()
        across.wait_send()

    rf.finish(factor)
    df_all[j] = rf.final[...]
    across_df.start()

    made = pp_sum[j].astype(WIDE)
    for k in (1, 2, 3):
        await_peer(pp_rx, prx_base, k)
        made = made + pp_rx[xor(j, k)].astype(WIDE)
    pz[...] = made.astype(LOW)
    pz_base = links.take(3)
    pz_sent = [
        links.send(pz.at[xor(z, 3)], pz_near.at[1], pz_base, p.one),
        links.send(pz.at[xor(z, 1)], pz_near.at[0], pz_base + 1, p.one),
    ]
    rq.step2()

    grad = gnf_tx[j].astype(WIDE)
    for k in (1, 2, 3):
        await_peer(gnf_rx, gnf_base, k)
        grad = grad + gnf_rx[xor(j, k)].astype(WIDE)
    sums[0:1] = jnp.sum(grad * unit1[...], axis=0, keepdims=True)
    sums[1:2] = jnp.sum(grad, axis=0, keepdims=True)
    gt_ref[...] = gr[...] + normalize_back(grad, unit1[...], scales[:, 0:1], params[0:1])
    stores = [local(gt_ref, gt_hbm, 0)]

    out = lax.broadcasted_iota(jnp.int32, (THIRD, D), 1)
    lane = lax.broadcasted_iota(jnp.int32, (THIRD, D), 0)
    spot = jnp.where(out == lane + THIRD * j, 1.0, 0.0).astype(LOW)
    for row_at, lane_at in ((2, 0), (3, 256)):
        parts = three(acc[8:9, lane_at : lane_at + THIRD])
        sums[row_at : row_at + 1] = mm(parts[0], spot) + mm(parts[1], spot) + mm(parts[2], spot)
    sums[8:16] = jnp.broadcast_to(acc[0:1, :], (8, D))
    parts = three(sums[...])
    spread_out = mm_t(parts[0], place_m[...]) + mm_t(parts[1], place_m[...]) + mm_t(parts[2], place_m[...])
    line = lax.broadcasted_iota(jnp.int32, (8, 128), 0)
    own_lines = (line >= 2 * (j % 2)) & (line < 2 * (j % 2) + 2)
    for i in range(8):
        vt[i, 0:8] = spread_out[0:8, 128 * i : 128 * i + 128]
        at = 256 * (i // 2)
        even, more = spread_out[8:16, at : at + 128], spread_out[8:16, at + 128 : at + 256]
        picked = jnp.where((line & 1) == 0, even, more)
        vt[i, 8:16] = jnp.where(own_lines & (half == i % 2), picked, 0.0)
    vt_base = links.take(8)
    vt_sent = []
    for i in range(1, 8):
        device = p.at(i // 2, i % 2)
        vt_sent.append(links.send(vt.at[device[1]], vr.at[i], vt_base + i, device))

    pz_sent[0].wait_recv()
    pz_second[...] = (pz[xor(z, 2)].astype(WIDE) + pz_near[1].astype(WIDE)).astype(LOW)
    pz_last = links.send(pz_second, pz_far, pz_base + 2, p.two)
    rq.finish(factor)
    dq_all[j] = rq.final[...]
    across_dq.start()

    mine = vt[s]
    for i in range(1, 8):
        vt_sent[i - 1].wait_recv()
        mine = mine + vr[i]
    v2[...] = mine
    v2_base = links.take(4)
    to_peers(lambda k: v2, vr2, v2_base)

    pz_sent[1].wait_recv()
    pz_last.wait_recv()
    made = pz[z].astype(WIDE) + pz_near[0].astype(WIDE) + pz_far[...].astype(WIDE)
    pp_all[j] = (made * factor).astype(LOW)
    dp_base = links.take(4)
    to_peers(lambda k: pp_all.at[j], pp_all, dp_base)
    across_df.step1()
    across_df.step2()

    made = res[...] + params[7:8] + op_tx[j].astype(WIDE)
    for k in (1, 2, 3):
        await_peer(op_rx, op_base, k)
        made = made + op_rx[xor(j, k)].astype(WIDE)
    y_ref[...] = made.astype(LOW)
    stores.append(local(y_ref, y_hbm, 1))
    for i in range(4):
        here = (2 * c + i // 2 == j) & (c == i % 2)

        @pl.when(jnp.logical_not(here))
        def _():
            links.copy(do_ref.at[i], do_ref.at[i], do_base, p.here, do_recv + i).wait_recv()

    stores.append(local(do_ref, do_hbm, 2))
    across_dq.step1()
    across_dq.step2()
    across_df.finish()

    def into(dst, src, count):
        for r in range(4):
            for i in range(count):
                at = D * i + THIRD * r
                dst[:, at : at + THIRD] = src[r, :, THIRD * i : THIRD * (i + 1)]

    into(df_ref, df_all, 4)
    stores.append(local(df_ref, df_hbm, 3))
    for k in (1, 2, 3):
        await_peer(pp_all, dp_base, k)
    for t, a, b, at, to in TILES:
        dp_ref[to : to + b - a, 128 * t : 128 * (t + 1)] = pp_all[at, a:b]
    stores.append(local(dp_ref, dp_hbm, 4))
    mine = v2[...]
    for k in (1, 2, 3):
        await_peer(vr2, v2_base, k)
        mine = mine + vr2[xor(j, k)]
    dv_ref[...] = mine * factor
    stores.append(local(dv_ref, dv_hbm, 5))
    across_dq.finish()
    into(dq_ref, dq_all, 3)
    stores.append(local(dq_ref, dq_hbm, 6))

    for buf_of, dst, base in (
        (att, att_rx, att_base),
        (gns_tx, gns_rx, gns_base),
        (op_tx, op_rx, op_base),
        (gnf_tx, gnf_rx, gnf_base),
    ):
        for k in (1, 2, 3):
            links.copy(buf_of.at[xor(j, k)], dst.at[j], base + k, p.peer(k)).wait_send()
    links.drain()
    for made in stores:
        made.wait()


def widen_kernel(
    y, gt, dq, dp, df, do, dv,
    y_out, gt_out, dq_out, dp_out, df_out, do_out, qv_out, fb_out, g1_out, s1_out, pb_out, g2_out, s2_out, ob_out,
    ins, outs, y_low, gt_low, dq_low, dp_low, df_low, do_low, dq_wide, dp_wide, df_wide, do_wide,
):
    def local(src, dst, sems, index):
        made = pltpu.make_async_copy(src, dst, sems.at[index])
        made.start()
        return made

    work = ((dq, dq_low, dq_wide, dq_out), (df, df_low, df_wide, df_out), (do, do_low, do_wide, do_out), (dp, dp_low, dp_wide, dp_out))
    loads = [local(src, low, ins, i) for i, (src, low, _, _) in enumerate(work)]
    plain = ((y, y_low, y_out), (gt, gt_low, gt_out))
    passing = [local(src, low, ins, 4 + i) for i, (src, low, _) in enumerate(plain)]
    done = []
    qv_out[...] = dv[2:4, 0:BLOCK]
    for i in range(4):
        fb_out[:, BLOCK * i : BLOCK * (i + 1)] = dv[8 + i : 9 + i, 0:BLOCK]
    for ref, i in zip((g1_out, s1_out, pb_out, g2_out, s2_out, ob_out), (0, 1, 4, 5, 6, 7)):
        ref[...] = dv[i : i + 1, 0:BLOCK]
    for i, (_, low, wide, out) in enumerate(work):
        loads[i].wait()
        wide[...] = low[...].reshape(wide.shape).astype(WIDE)
        done.append(local(wide, out, outs, i))
    for i, (_, low, out) in enumerate(plain):
        passing[i].wait()
        done.append(local(low, out, outs, 4 + i))
    for made in done:
        made.wait()


def vmem(*shape, kind=LOW):
    return pltpu.VMEM(shape, kind)


def fused_device(
    tokens,
    segment_ids,
    first_gain,
    first_shift,
    qkv_weight,
    qv_bias,
    proj_weight,
    proj_bias,
    second_gain,
    second_shift,
    fc_weight,
    fc_bias,
    out_weight,
    out_bias,
    cotangent,
):
    shards, reps = lax.axis_size("shard"), lax.axis_size("rep")
    factor = 1.0 / math.sqrt(ROWS * reps * shards)

    def reduce_bufs(width):
        return [
            vmem(4, 2, BLOCK, width),
            vmem(4, BLOCK, width),
            vmem(4, BLOCK, width),
            vmem(2, BLOCK, width),
            vmem(BLOCK, width),
            vmem(BLOCK, width),
            vmem(BLOCK, width),
        ]

    blocks = lambda width, kind=LOW: vmem(4, ROWS, width, kind=kind)
    scratch = [
        pltpu.SemaphoreType.DMA((160,)),
        pltpu.SemaphoreType.DMA((160,)),
        pltpu.SemaphoreType.DMA((8,)),
        vmem(ROWS, D),
        vmem(BLOCK, 3 * D),
        vmem(BLOCK, D),
        vmem(BLOCK, FF),
        vmem(4 * BLOCK, D),
        vmem(ROWS, D),
        vmem(ROWS, D, kind=WIDE),
        vmem(BLOCK, 3 * D),
        vmem(BLOCK, D),
        vmem(BLOCK, FF),
        vmem(4, BLOCK, D),
        vmem(16, 128, kind=WIDE),
        vmem(16, 128, kind=WIDE),
        vmem(16, 128),
        vmem(8, 16, 128),
        blocks(D),
        vmem(4, 8, ROWS, kind=WIDE),
        blocks(D),
        vmem(BLOCK, 3 * THIRD),
        vmem(BLOCK, D),
        vmem(D, 3 * THIRD),
        vmem(D, D),
        vmem(D, D),
        vmem(D, D),
        vmem(BLOCK, D),
        vmem(BLOCK, D),
        vmem(1024, D),
        vmem(16, D, kind=WIDE),
        blocks(D),
        vmem(4, 3 * ROWS, 128, kind=WIDE),
        blocks(THIRD),
        blocks(THIRD),
        vmem(ROWS, D, kind=WIDE),
        vmem(ROWS, D, kind=WIDE),
        vmem(ROWS, D, kind=WIDE),
        vmem(ROWS, 128, kind=WIDE),
        blocks(D),
        blocks(D),
        blocks(D, WIDE),
        blocks(D),
        blocks(D),
        blocks(D),
        blocks(D),
        blocks(D),
        blocks(THIRD),
        blocks(THIRD),
        blocks(D),
        blocks(D),
        blocks(3 * THIRD),
        vmem(ROWS, D, kind=WIDE),
        vmem(16, D, kind=WIDE),
        vmem(16, D, kind=WIDE),
        vmem(8, 16, 128, kind=WIDE),
        vmem(8, 16, 128, kind=WIDE),
        vmem(16, 128, kind=WIDE),
        vmem(4, 16, 128, kind=WIDE),
        vmem(4, BLOCK, 3 * THIRD),
        vmem(4, BLOCK, D),
        vmem(576, 128),
        vmem(4, 2, 4, 144, 128),
        vmem(2, 4, 4, 144, 128),
        vmem(4, 4, 144, 128),
        vmem(4, 4, 144, 128),
        vmem(4, 4, 144, 128),
        vmem(4, 144, 128),
        vmem(2, 144, 128),
        vmem(144, 128),
        vmem(144, 128),
        vmem(4, 144, 128),
    ]
    for width in (3 * THIRD, D, D):
        scratch += reduce_bufs(width)
    in_vmem = pl.BlockSpec(memory_space=pltpu.VMEM)
    anywhere = pl.BlockSpec(memory_space=pl.ANY)
    partial = pl.pallas_call(
        functools.partial(layer_kernel, factor),
        out_shape=(
            jax.ShapeDtypeStruct((ROWS, D), LOW),
            jax.ShapeDtypeStruct((ROWS, D), WIDE),
            jax.ShapeDtypeStruct((BLOCK, 3 * D), LOW),
            jax.ShapeDtypeStruct((BLOCK, D), LOW),
            jax.ShapeDtypeStruct((BLOCK, FF), LOW),
            jax.ShapeDtypeStruct((4, BLOCK, D), LOW),
            jax.ShapeDtypeStruct((16, 128), WIDE),
        ),
        in_specs=[anywhere] * 2 + [in_vmem] * 9 + [anywhere] * 4,
        out_specs=(anywhere,) * 7,
        scratch_shapes=scratch,
        compiler_params=pltpu.CompilerParams(
            collective_id=0, has_side_effects=True, vmem_limit_bytes=56 * 1024 * 1024
        ),
    )(
        tokens,
        cotangent,
        segment_ids,
        first_gain[None],
        first_shift[None],
        qv_bias,
        proj_bias[None],
        second_gain[None],
        second_shift[None],
        fc_bias[None],
        out_bias[None],
        qkv_weight,
        proj_weight,
        fc_weight,
        out_weight,
    )
    rows = [jax.ShapeDtypeStruct((1, BLOCK), WIDE)] * 6
    y, grad_tokens, qkv_grad, proj_grad, fc_grad, out_grad, qv_grad, fc_bias_grad, *sums = pl.pallas_call(
        widen_kernel,
        out_shape=(
            jax.ShapeDtypeStruct((ROWS, D), LOW),
            jax.ShapeDtypeStruct((ROWS, D), WIDE),
            jax.ShapeDtypeStruct((BLOCK, 3 * D), WIDE),
            jax.ShapeDtypeStruct((BLOCK, D), WIDE),
            jax.ShapeDtypeStruct((BLOCK, FF), WIDE),
            jax.ShapeDtypeStruct((4 * BLOCK, D), WIDE),
            jax.ShapeDtypeStruct((2, BLOCK), WIDE),
            jax.ShapeDtypeStruct((1, 4 * BLOCK), WIDE),
            *rows,
        ),
        in_specs=[anywhere] * 6 + [in_vmem],
        out_specs=(anywhere,) * 6 + (in_vmem,) * 8,
        scratch_shapes=[
            pltpu.SemaphoreType.DMA((6,)),
            pltpu.SemaphoreType.DMA((6,)),
            vmem(ROWS, D),
            vmem(ROWS, D, kind=WIDE),
            vmem(BLOCK, 3 * D),
            vmem(BLOCK, D),
            vmem(BLOCK, FF),
            vmem(4, BLOCK, D),
            vmem(BLOCK, 3 * D, kind=WIDE),
            vmem(BLOCK, D, kind=WIDE),
            vmem(BLOCK, FF, kind=WIDE),
            vmem(4 * BLOCK, D, kind=WIDE),
        ],
        compiler_params=pltpu.CompilerParams(vmem_limit_bytes=56 * 1024 * 1024),
    )(*partial)
    first_gain_grad, first_shift_grad, proj_bias_grad, second_gain_grad, second_shift_grad, out_bias_grad = (
        row.reshape(BLOCK) for row in sums
    )
    return (
        y,
        grad_tokens,
        first_gain_grad,
        first_shift_grad,
        qkv_grad,
        qv_grad,
        proj_grad,
        proj_bias_grad,
        second_gain_grad,
        second_shift_grad,
        fc_grad,
        fc_bias_grad.reshape(4 * BLOCK),
        out_grad,
        out_bias_grad,
    )


def solution(mesh):
    return jax.shard_map(
        fused_device if dict(mesh.shape) == {"rep": 4, "shard": 8} else per_device,
        mesh=mesh,
        in_specs=(
            P(("rep", "shard"), None),
            P(("rep", "shard"), None),
            P("shard"),
            P("shard"),
            P("shard", None),
            P(None, "shard"),
            P("shard", None),
            P("shard"),
            P("shard"),
            P("shard"),
            P("shard", None),
            P("shard"),
            P("shard", None),
            P("shard"),
            P(("rep", "shard"), None),
        ),
        out_specs=(
            P(("rep", "shard"), None),
            P(("rep", "shard"), None),
            P("shard"),
            P("shard"),
            P("shard", None),
            P(None, "shard"),
            P("shard", None),
            P("shard"),
            P("shard"),
            P("shard"),
            P("shard", None),
            P("shard"),
            P("shard", None),
            P("shard"),
        ),
        check_vma=False,
    )
```

```python
import functools
import math

import jax
import jax.numpy as jnp
from jax import lax
from jax.experimental import pallas as pl
from jax.experimental.pallas import tpu as pltpu
from jax.sharding import PartitionSpec as P

D = 768
HEADS = 12
HD = 64
FF = 3072


EPSILON = 1e-05


def layer_norm(field, norm_gain, norm_shift):
    center = field - jnp.mean(field, axis=-1, keepdims=True)
    spread = jnp.mean(center * center, axis=-1, keepdims=True)
    return center * lax.rsqrt(spread + EPSILON) * norm_gain + norm_shift


def gelu_tanh(field):
    return jax.nn.gelu(field, approximate=True)


def head_split(matrix):
    return matrix.reshape(matrix.shape[0], HEADS, HD)


def masked_scores(query, keys, segments):
    rows = query.shape[0]
    scores = jnp.einsum(
        "qhd,khd->hqk", head_split(query), head_split(keys), preferred_element_type=jnp.float32
    ) * (1.0 / math.sqrt(HD))
    position = lax.iota(jnp.int32, rows)
    allowed = (segments[:, None] == segments[None, :]) & (position[None, :] <= position[:, None])
    return jnp.where(allowed[None], scores, -1e30)


def attend_forward(query, keys, values, segments):
    rows = query.shape[0]
    scores = masked_scores(query, keys, segments)
    row_max = jnp.max(scores, axis=-1, keepdims=True)
    row_total = jnp.sum(jnp.exp(scores - row_max), axis=-1, keepdims=True)
    logsum = row_max + jnp.log(row_total)
    probs = jnp.exp(scores - logsum).astype(jnp.bfloat16)
    attended = jnp.einsum(
        "hqk,khd->qhd", probs, head_split(values), preferred_element_type=jnp.float32
    )
    return (attended.reshape(rows, D).astype(jnp.bfloat16), logsum)


def attend_backward(query, keys, values, segments, attended, logsum, grad_attended):
    rows = query.shape[0]
    scores = masked_scores(query, keys, segments)
    weights = jnp.exp(scores - logsum)
    grad_heads = head_split(grad_attended)
    grad_values = jnp.einsum(
        "hqk,qhd->khd", weights.astype(jnp.bfloat16), grad_heads, preferred_element_type=jnp.float32
    )
    grad_probs = jnp.einsum(
        "qhd,khd->hqk", grad_heads, head_split(values), preferred_element_type=jnp.float32
    )
    delta = jnp.einsum(
        "qhd,qhd->hq", grad_heads, head_split(attended), preferred_element_type=jnp.float32
    )
    grad_scores = (weights * (grad_probs - delta[..., None]) * (1.0 / math.sqrt(HD))).astype(
        jnp.bfloat16
    )
    grad_query = jnp.einsum(
        "hqk,khd->qhd", grad_scores, head_split(keys), preferred_element_type=jnp.float32
    )
    grad_keys = jnp.einsum(
        "hqk,qhd->khd", grad_scores, head_split(query), preferred_element_type=jnp.float32
    )
    return (grad_query.reshape(rows, D), grad_keys.reshape(rows, D), grad_values.reshape(rows, D))


def exchange(field, axis, split, concat):
    return lax.all_to_all(field, axis, split_axis=split, concat_axis=concat, tiled=True)


def spread(field, axis):
    parts = lax.axis_size(axis)
    return exchange(jnp.broadcast_to(field[None], (parts,) + field.shape), axis, 0, 0)


def by_replica(field, shards, reps):
    rows = field.shape[0]
    return (
        field.reshape(shards, reps, rows // (shards * reps), -1).swapaxes(0, 1).reshape(rows, -1)
    )


def per_device(
    tokens,
    segment_ids,
    first_gain,
    first_shift,
    qkv_weight,
    qv_bias,
    proj_weight,
    proj_bias,
    second_gain,
    second_shift,
    fc_weight,
    fc_bias,
    out_weight,
    out_bias,
    cotangent,
):
    low = jnp.bfloat16
    segments = segment_ids[0]
    own_rows = tokens.shape[0]
    shards = lax.axis_size("shard")
    reps = lax.axis_size("rep")
    factor = 1.0 / math.sqrt(own_rows * reps * shards)
    small = jnp.stack(
        [first_gain, first_shift, qv_bias[0], qv_bias[1], proj_bias, second_gain, second_shift, out_bias]
    )
    small_full = lax.all_gather(small, "shard", axis=1, tiled=True).astype(jnp.float32)
    gain_one, shift_one, q_bias, v_bias, proj_bias_full, gain_two, shift_two, out_bias_full = (
        small_full[i] for i in range(8)
    )
    qkv_full = lax.all_gather(qkv_weight, "shard", axis=0, tiled=True)
    proj_full = lax.all_gather(proj_weight, "shard", axis=0, tiled=True)
    fc_cols = exchange(fc_weight, "shard", 1, 0)
    inputs = tokens.astype(jnp.float32)
    normed_f, first_back = jax.vjp(layer_norm, inputs, gain_one, shift_one)
    normed_first = normed_f.astype(low)
    projected = jnp.dot(normed_first, qkv_full, preferred_element_type=jnp.float32)
    query = (projected[:, :D] + q_bias).astype(low)
    keys = projected[:, D : 2 * D].astype(low)
    values = (projected[:, 2 * D :] + v_bias).astype(low)
    attended, logsum = attend_forward(query, keys, values, segments)
    residual = (
        inputs + jnp.dot(attended, proj_full, preferred_element_type=jnp.float32) + proj_bias_full
    )
    cot_f = cotangent.astype(jnp.float32)
    normed_s, second_back = jax.vjp(layer_norm, residual, gain_two, shift_two)
    normed_all = lax.all_gather(normed_s.astype(low), "shard", axis=0, tiled=True)
    cot_later, normed_all = lax.optimization_barrier((cotangent, normed_all))
    cot_all = lax.all_gather(cot_later, "shard", axis=0, tiled=True)
    pre_act = jnp.dot(normed_all, fc_cols, preferred_element_type=jnp.float32) + fc_bias.astype(
        jnp.float32
    )
    activated, gelu_back = jax.vjp(gelu_tanh, pre_act)
    hidden = activated.astype(low)
    grad_hidden = jnp.dot(cot_all, out_weight.T, preferred_element_type=jnp.float32)
    (grad_pre,) = gelu_back(grad_hidden)
    grad_pre_low = grad_pre.astype(low)
    grad_normed_part = jnp.dot(grad_pre_low, fc_cols.T, preferred_element_type=jnp.float32).astype(low)
    grad_normed_low = lax.psum_scatter(grad_normed_part, "shard", scatter_dimension=0, tiled=True)
    term_out_weight = jnp.dot(hidden.T, cot_all, preferred_element_type=jnp.float32) * factor
    term_fc_weight = jnp.dot(normed_all.T, grad_pre_low, preferred_element_type=jnp.float32) * factor
    out_part = jnp.dot(hidden, out_weight, preferred_element_type=jnp.float32).astype(low)
    ff_terms = jnp.concatenate(
        [
            term_out_weight.astype(low).reshape(reps, -1, D),
            by_replica(term_fc_weight.astype(low), shards, reps).reshape(reps, -1, D),
        ],
        axis=1,
    )
    ff_sum = jnp.sum(exchange(ff_terms, "rep", 0, 0).astype(jnp.float32), axis=0).astype(low)
    first_later, attended_later, grad_normed_low, ff_sum = lax.optimization_barrier(
        (normed_first, attended, grad_normed_low, ff_sum)
    )
    first_all = lax.all_gather(first_later, "shard", axis=0, tiled=True)
    grad_normed_second = grad_normed_low.astype(jnp.float32)

    grad_from_norm, second_gain_sum, second_shift_sum = second_back(grad_normed_second)
    grad_residual = cot_f + grad_from_norm
    grad_residual_low = grad_residual.astype(low)
    grad_residual_all = lax.all_gather(grad_residual_low, "shard", axis=0, tiled=True)
    attended_cols = exchange(attended_later, "shard", 1, 0)
    grad_attended = jnp.dot(
        grad_residual_low, proj_full.T, preferred_element_type=jnp.float32
    ).astype(low)
    out_rows = out_weight.shape[0] // reps
    out_piece = ff_sum[:out_rows]
    fc_piece = ff_sum[out_rows:].reshape(D // reps, -1)
    fc_piece = exchange(fc_piece, "shard", 0, 1)
    ff_all = spread(jnp.concatenate([out_piece, fc_piece.reshape(-1, D)]), "rep").astype(jnp.float32)

    grad_query, grad_keys, grad_values = attend_backward(
        query, keys, values, segments, attended, logsum, grad_attended
    )
    grad_projected = jnp.concatenate([grad_query, grad_keys, grad_values], axis=1).astype(low)
    grad_projected, ff_all = lax.optimization_barrier((grad_projected, ff_all))
    out_grad = ff_all[:, :out_rows].reshape(-1, D)
    fc_grad = ff_all[:, out_rows:].reshape(-1, FF)
    grad_cols = exchange(grad_projected, "shard", 1, 0)
    grad_normed_first = jnp.dot(grad_projected, qkv_full.T, preferred_element_type=jnp.float32)
    out_later, grad_cols = lax.optimization_barrier((out_part, grad_cols))
    out_sum = lax.psum_scatter(out_later, "shard", scatter_dimension=0, tiled=True)
    result = (residual + out_sum.astype(jnp.float32) + out_bias_full).astype(low)
    term_qkv_weight = jnp.dot(first_all.T, grad_cols, preferred_element_type=jnp.float32) * factor
    term_proj_weight = (
        jnp.dot(attended_cols.T, grad_residual_all, preferred_element_type=jnp.float32) * factor
    )
    attn_terms = jnp.concatenate(
        [
            term_proj_weight.astype(low).reshape(reps, -1, D),
            by_replica(term_qkv_weight.astype(low), shards, reps).reshape(reps, -1, D),
        ],
        axis=1,
    )
    attn_sum = jnp.sum(exchange(attn_terms, "rep", 0, 0).astype(jnp.float32), axis=0).astype(low)
    proj_rows = proj_weight.shape[0] // reps
    proj_piece = attn_sum[:proj_rows]
    qkv_piece = attn_sum[proj_rows:].reshape(D // reps, -1)
    qkv_piece = exchange(qkv_piece, "shard", 0, 1)
    attn_all = spread(jnp.concatenate([proj_piece, qkv_piece.reshape(-1, D)]), "rep").astype(
        jnp.float32
    )
    proj_grad = attn_all[:, :proj_rows].reshape(-1, D)
    qkv_grad = attn_all[:, proj_rows:].reshape(-1, 3 * D)

    grad_input_norm, first_gain_sum, first_shift_sum = first_back(grad_normed_first)
    grad_inputs = grad_residual + grad_input_norm
    terms = jnp.stack(
        [
            first_gain_sum,
            first_shift_sum,
            jnp.sum(grad_query, axis=0),
            jnp.sum(grad_values, axis=0),
            jnp.sum(grad_residual, axis=0),
            second_gain_sum,
            second_shift_sum,
            jnp.sum(cot_f, axis=0),
        ]
    )
    count = terms.shape[0]
    terms = terms.reshape(count, shards, -1).swapaxes(0, 1).reshape(shards, -1)
    own_terms = jnp.concatenate(
        [jnp.sum(exchange(terms, "shard", 0, 0), axis=0), jnp.sum(grad_pre, axis=0)]
    )
    sums = jnp.sum(spread(own_terms, "rep"), axis=0) * factor
    own_cols = D // shards
    fc_bias_grad = sums[count * own_cols :]
    sums = sums[: count * own_cols].reshape(count, own_cols)
    return (
        result,
        grad_inputs,
        sums[0],
        sums[1],
        qkv_grad,
        sums[2:4],
        proj_grad,
        sums[4],
        sums[5],
        sums[6],
        fc_grad,
        fc_bias_grad,
        out_grad,
        sums[7],
    )

MESH = pl.DeviceIdType.MESH
LOW = jnp.bfloat16
WIDE = jnp.float32
ROWS = 128
BLOCK = 96
THIRD = 192
NEG = -1e30


def xor(a, b):
    return (a // 2 + b // 2) % 2 * 2 + (a + b) % 2


def mm(a, b):
    return jnp.dot(a, b, preferred_element_type=WIDE)


def mm_t(a, b):
    return lax.dot_general(a, b, (((1,), (1,)), ((), ())), preferred_element_type=WIDE)


def t_mm(a, b):
    return lax.dot_general(a, b, (((0,), (0,)), ((), ())), preferred_element_type=WIDE)


def three(field):
    first = field.astype(LOW)
    rest = field - first.astype(WIDE)
    second = rest.astype(LOW)
    return first, second, (rest - second.astype(WIDE)).astype(LOW)


def normalize(field):
    center = field - jnp.mean(field, axis=-1, keepdims=True)
    scale = lax.rsqrt(jnp.mean(center * center, axis=-1, keepdims=True) + EPSILON)
    return center * scale, scale


def normalize_back(grad, unit, scale, gain):
    inner = grad * gain
    mean = jnp.mean(inner, axis=-1, keepdims=True)
    along = jnp.mean(inner * unit, axis=-1, keepdims=True)
    return scale * (inner - mean - unit * along)


def heads_of(field):
    lane = lax.broadcasted_iota(jnp.int32, field.shape, 1)
    zero = jnp.zeros_like(field)
    return jnp.concatenate(
        [jnp.where((lane >= h * HD) & (lane < (h + 1) * HD), field, zero) for h in range(3)], axis=0
    )


def heads_join(stacked):
    lane = lax.broadcasted_iota(jnp.int32, (ROWS, THIRD), 1)
    return jnp.where(
        lane < HD, stacked[:ROWS], jnp.where(lane < 2 * HD, stacked[ROWS : 2 * ROWS], stacked[2 * ROWS :])
    )


class Links:
    def __init__(self, sends, recvs):
        self.sends, self.recvs, self.used, self.open, self.later = sends, recvs, 0, [], []

    def take(self, count=1):
        self.used += count
        return self.used - count

    def copy(self, src, dst, index, device, recv_index=None):
        recv_index = index if recv_index is None else recv_index
        return pltpu.make_async_remote_copy(
            src_ref=src,
            dst_ref=dst,
            send_sem=self.sends.at[index],
            recv_sem=self.recvs.at[recv_index],
            device_id=device,
            device_id_type=MESH,
        )

    def send(self, src, dst, index, device, recv_index=None):
        made = self.copy(src, dst, index, device, recv_index)
        made.start()
        self.open.append(made)
        return made

    def drain(self):
        for made in self.open:
            made.wait_send()
        for copies in self.later:
            for made in copies():
                made.wait_send()


class Gather:
    def __init__(self, links, place, own, full):
        self.links, self.place, self.own, self.full = links, place, own, full
        self.base = links.take(7)

    def slot(self, z, c):
        return self.full.at[pl.ds(pl.multiple_of((2 * z + c) * BLOCK, 16), BLOCK)]

    def arrived(self, which, slot):
        self.links.copy(slot, slot, self.base + which, self.place.here).wait_recv()

    def pass_on(self, which, slot, device):
        self.links.send(slot, slot, self.base + which, device)

    def two(self):
        p = self.place
        self.links.send(self.own, self.slot(p.z, p.c), self.base, p.two)

    def one(self):
        p = self.place
        mine = self.slot(p.z, p.c)
        self.links.send(self.own, mine, self.base + 1, p.one)
        self.links.send(self.own, mine, self.base + 2, p.mate)
        mine[...] = self.own[...]

    def step1(self):
        p = self.place
        slot = self.slot(xor(p.z, 2), p.c)
        self.arrived(0, slot)
        self.pass_on(3, slot, p.one)
        self.pass_on(4, slot, p.mate)

    def step2(self):
        p = self.place
        slot = self.slot(xor(p.z, 1), p.c)
        self.arrived(1, slot)
        self.pass_on(5, slot, p.mate)

    def step3(self):
        p = self.place
        slot = self.slot(xor(p.z, 3), p.c)
        self.arrived(3, slot)
        self.pass_on(6, slot, p.mate)

    def finish(self):
        p = self.place
        for which, flip in ((2, 0), (4, 2), (5, 1), (6, 3)):
            self.arrived(which, self.slot(xor(p.z, flip), 1 - p.c))


class Across:
    def __init__(self, links, place, buf, cut):
        self.links, self.place, self.buf, self.cut = links, place, buf, cut
        self.base = links.take(6)
        links.later.append(self.copies)

    def part(self, k, second):
        slot = self.buf.at[xor(self.place.j, k)]
        rows = self.buf.shape[1]
        return slot.at[self.cut : rows] if second else slot.at[0 : self.cut]

    def copy(self, which):
        p, links = self.place, self.links
        k, second = ((0, False), (0, True), (1, False), (2, True), (0, True), (0, False))[which]
        src = self.part(k, second)
        return links.copy(src, src, self.base + which, p.peer((1, 2, 2, 1, 1, 2)[which]))

    def copies(self):
        return [self.copy(which) for which in range(6)]

    def arrived(self, which, slot):
        self.links.copy(slot, slot, self.base + which, self.place.here).wait_recv()

    def start(self):
        for which in (0, 1, 4, 5):
            self.copy(which).start()

    def first(self):
        self.pass_on()
        self.arrived(4, self.part(1, True))

    def second(self):
        self.arrived(5, self.part(2, False))

    def pass_on(self):
        self.arrived(0, self.part(1, False))
        self.copy(2).start()
        self.arrived(1, self.part(2, True))
        self.copy(3).start()

    def finish(self):
        self.arrived(2, self.part(3, False))
        self.arrived(3, self.part(3, True))

    def step(self, k):
        pl.when(k == 1)(self.first)
        pl.when(k == 2)(self.second)
        pl.when(k == 3)(self.finish)


class AcrossSum:
    def __init__(self, links, place, parts, got, hop, cut):
        self.links, self.place, self.parts, self.got, self.hop, self.cut = links, place, parts, got, hop, cut
        self.base = links.take(4)
        links.later.append(lambda: [self.copy(which) for which in range(4)])

    def block(self, k):
        return self.parts.at[xor(self.place.j, k)]

    def copy(self, which):
        p = self.place
        if which < 2:
            src = self.block(3)
            src = src.at[self.cut : self.parts.shape[1]] if which else src.at[0 : self.cut]
            return self.links.copy(src, self.hop.at[which], self.base + which, p.peer(which + 1))
        return self.links.copy(self.block(which - 1), self.got.at[p.j], self.base + which, p.peer(which - 1))

    def far(self):
        self.copy(0).start()
        self.copy(1).start()

    def near(self):
        for which in range(2):
            self.copy(which).wait_recv()
            at = xor(self.place.j, 2 - which)
            rows = slice(self.cut, self.parts.shape[1]) if which else slice(0, self.cut)
            self.parts[at, rows] = (self.parts[at, rows].astype(WIDE) + self.hop[which].astype(WIDE)).astype(LOW)
            self.copy(3 - which).start()

    def total(self):
        j = self.place.j
        total = self.parts[j].astype(WIDE)
        for k in (1, 2):
            slot = self.got.at[xor(j, k)]
            self.links.copy(slot, slot, self.base + 1 + k, self.place.here).wait_recv()
            total = total + self.got[xor(j, k)].astype(WIDE)
        return total


class Reduce:
    def __init__(self, links, place, bufs):
        self.links, self.place = links, place
        self.part, self.got, self.total, self.near, self.second, self.far, self.final = bufs
        self.base = links.take(4)

    def fill(self, full):
        for z in range(4):
            for c in range(2):
                at = (2 * z + c) * BLOCK
                self.part[z, c] = full[at : at + BLOCK].astype(LOW)

    def pair(self):
        p = self.place
        self.sent = self.links.send(self.part.at[:, 1 - p.c], self.got, self.base, p.mate)

    def step1(self):
        p = self.place
        self.sent.wait_recv()
        for z in range(4):
            self.total[z] = (self.part[z, p.c].astype(WIDE) + self.got[z].astype(WIDE)).astype(LOW)
        self.first = [
            self.links.send(self.total.at[xor(p.z, 3)], self.near.at[1], self.base + 1, p.one),
            self.links.send(self.total.at[xor(p.z, 1)], self.near.at[0], self.base + 2, p.one),
        ]

    def step2(self):
        p = self.place
        self.first[0].wait_recv()
        self.second[...] = (self.total[xor(p.z, 2)].astype(WIDE) + self.near[1].astype(WIDE)).astype(LOW)
        self.last = self.links.send(self.second, self.far, self.base + 3, p.two)

    def finish(self, factor):
        p = self.place
        self.first[1].wait_recv()
        self.last.wait_recv()
        whole = self.total[p.z].astype(WIDE) + self.near[0].astype(WIDE) + self.far[...].astype(WIDE)
        self.final[...] = (whole * factor).astype(LOW)


class Place:
    def __init__(self):
        self.j, self.s = lax.axis_index("rep"), lax.axis_index("shard")
        self.z, self.c = self.s // 2, self.s % 2
        self.here = (self.j, self.s)
        self.mate = self.at(0, 1)
        self.one = self.at(1, 0)
        self.two = self.at(2, 0)

    def at(self, flip_z, flip_c):
        return (self.j, 2 * xor(self.z, flip_z) + (self.c + flip_c) % 2)

    def peer(self, k):
        return (xor(self.j, k), self.s)


TILES = tuple(
    (t, max(96 * t, 144 * q) - 144 * q, min(96 * t + 96, 144 * q + 144) - 144 * q, q, max(96 * t, 144 * q) - 96 * t)
    for t in range(6)
    for q in range(4)
    if max(96 * t, 144 * q) < min(96 * t + 96, 144 * q + 144)
)


def layer_kernel(
    factor,
    tok_hbm, cot_hbm, seg_in, g1_in, s1_in, qvb_in, pb_in, g2_in, s2_in, fb_in, ob_in, qkv_hbm, wp_hbm, fc_hbm, wo_hbm,
    y_hbm, gt_hbm, dq_hbm, dp_hbm, df_hbm, do_hbm, dv_hbm,
    sends, recvs, locals_,
    tok, qkv_in, wp_in, fc_in, wo_in, y_ref, gt_ref, dq_ref, dp_ref, df_ref, do_ref, dv_ref,
    vec_wide, vec_in, vec_all, nf, seg, cots, wq_in, wf_in, wq, wp, wf, wo, out_own, out_got, place_m, params,
    qkv, weights, att, att_rx, res, unit1, unit2, scales,
    ns, hid, slope, gpl, gns_tx, gns_rx, op_tx, op_rx, ga_tx, ga_rx, gnf_tx, gnf_rx, gnf_hop, pp_hop, gproj, gr,
    sums, acc, vt, vr, v2, vr2, dq_all, df_all,
    pt_own, pq, pp, pp_got, pp_sum, pp_rx, pz, pz_near, pz_second, pz_far, pp_all,
    *reduce_bufs,
):
    p = Place()
    j, s, z, c = p.j, p.s, p.z, p.c
    half = j // 2
    odd = j % 2 == 1
    links = Links(sends, recvs)

    def local(src, dst, index):
        made = pltpu.make_async_copy(src, dst, locals_.at[index])
        made.start()
        return made

    load_qkv = local(qkv_hbm, qkv_in, 0)
    load_wp = local(wp_hbm, wp_in, 1)
    load_cot = local(cot_hbm, cots.at[j], 2)
    load_fc = local(fc_hbm, fc_in, 3)
    load_wo = local(wo_hbm, wo_in, 4)
    load_tok = local(tok_hbm, tok, 5)

    partners = [p.at(fz, fc) for fz in range(4) for fc in range(2) if (fz, fc) != (0, 0)]
    partners += [p.peer(k) for k in (1, 2, 3)]
    partners += [(xor(j, k), 2 * z + 1 - c) for k in (1, 2, 3)]
    barrier = pltpu.get_barrier_semaphore()
    for device in partners:
        pl.semaphore_signal(barrier, inc=1, device_id=device, device_id_type=MESH)

    def columns(src, dst, count):
        for i in range(count):
            wide = src[:, pl.ds(pl.multiple_of(D * i + 128 * (3 * j // 2), 128), 256)]
            dst[:, THIRD * i : THIRD * (i + 1)] = jnp.where(odd, wide[:, 64:], wide[:, :THIRD])

    vec_wide[...] = jnp.zeros_like(vec_wide)
    for i, ref in enumerate((g1_in, s1_in, None, None, pb_in, g2_in, s2_in, ob_in)):
        if ref is not None:
            vec_wide[i : i + 1, 0:BLOCK] = ref[...].astype(WIDE)
    vec_wide[2:4, 0:BLOCK] = qvb_in[...].astype(WIDE)
    bias_row = fb_in[...].astype(WIDE)
    for i in range(2):
        low_part, high_part = (bias_row[:, THIRD * h + BLOCK * i : THIRD * h + BLOCK * (i + 1)] for h in range(2))
        vec_wide[8 + i : 9 + i, 0:BLOCK] = jnp.where(odd, high_part, low_part)
    vec_in[...] = vec_wide[...].astype(LOW)
    seg[j] = jnp.broadcast_to(seg_in[...].astype(WIDE), (8, ROWS))
    load_qkv.wait()
    columns(qkv_in, wq_in, 3)
    load_wp.wait()
    for t in range(6):
        pt_own[BLOCK * t : BLOCK * (t + 1)] = wp_in[:, 128 * t : 128 * (t + 1)]

    gq = Gather(links, p, wq_in, wq)
    gf = Gather(links, p, wf_in, wf)
    go = Gather(links, p, out_own, wo)
    rq, rf, ro = (Reduce(links, p, reduce_bufs[7 * i : 7 * i + 7]) for i in range(3))
    across_nf = Across(links, p, nf, ROWS // 2)
    across_cot = Across(links, p, cots, ROWS // 2)
    across_ns = Across(links, p, ns, ROWS // 2)
    across_df = Across(links, p, df_all, BLOCK // 2)
    sum_gnf = AcrossSum(links, p, gnf_tx, gnf_rx, gnf_hop, ROWS // 2)
    sum_pp = AcrossSum(links, p, pp_sum, pp_rx, pp_hop, 2)
    across_dq = Across(links, p, dq_all, BLOCK // 2)
    load_cot.wait()
    pl.semaphore_wait(barrier, len(partners))

    vec_base = links.take(8)
    vec_sent = []
    for i in range(1, 8):
        vec_sent.append(links.send(vec_in, vec_all.at[s], vec_base + i, p.at(i // 2, i % 2)))
    def to_peers(src_of, dst, base):
        return [links.send(src_of(k), dst.at[j], base + k, p.peer(k)) for k in (1, 2, 3)]

    def await_peer(dst, base, k):
        slot = dst.at[xor(j, k)]
        links.copy(slot, slot, base + k, p.here).wait_recv()

    quarter = pt_own.at[pl.ds(pl.multiple_of(144 * j, 16), 144)]
    pq_base = links.take(3)
    pq[j, c, z] = pt_own[pl.ds(pl.multiple_of(144 * j, 16), 144)]
    links.send(quarter, pq.at[j, c, z], pq_base, p.two)
    links.send(quarter, pq.at[j, c, z], pq_base + 1, p.one)
    gq.two()
    gq.one()

    def await_quarter(which, flip):
        slot = pq.at[j, c, xor(z, flip)]
        links.copy(slot, slot, pq_base + which, p.here).wait_recv()

    seg_base = links.take(4)
    to_peers(lambda k: seg.at[j], seg, seg_base)
    across_cot.start()
    load_wo.wait()
    out_base = links.take(1)
    out_sent = links.send(
        wo_in.at[pl.ds(pl.multiple_of((THIRD * j + BLOCK * (1 - c)) % 384, 16), BLOCK)], out_got, out_base, p.mate
    )
    load_fc.wait()
    columns(fc_in, wf_in, 4)
    gf.two()
    vec_all[s] = vec_in[...]

    row = lax.broadcasted_iota(jnp.int32, (1024, D), 0)
    col = lax.broadcasted_iota(jnp.int32, (1024, D), 1)
    inside = (row & 127) < BLOCK
    place_m[...] = jnp.where(inside & (col == BLOCK * (row >> 7) + (row & 127)), 1.0, 0.0).astype(LOW)

    load_tok.wait()
    tokens = tok[...].astype(WIDE)
    unit, scale1 = normalize(tokens)
    unit1[...] = unit
    for i in range(1, 8):
        vec_sent[i - 1].wait_recv()
    small = mm(jnp.concatenate([vec_all[i] for i in range(8)], axis=1), place_m[...])
    pieces = [vec_all[2 * (i // 2) + half][8 + i % 2 : 9 + i % 2] for i in range(8)]
    fc_bias = mm(jnp.concatenate(pieces, axis=1), place_m[...])
    params[0:8] = small[0:8]
    params[8:9] = fc_bias
    nf[j] = (unit * params[0:1] + params[1:2]).astype(LOW)
    across_nf.start()
    await_quarter(0, 2)
    links.send(pq.at[j, c, xor(z, 2)], pq.at[j, c, xor(z, 2)], pq_base + 2, p.one)

    out_sent.wait_recv()
    mine = wo_in[pl.ds(pl.multiple_of((THIRD * j + BLOCK * c) % 384, 16), BLOCK)]
    out_own[...] = jnp.where(c == half, mine, out_got[...])

    def of_heads(index):
        lane = lax.broadcasted_iota(jnp.int32, (D, THIRD), 0)
        out = lax.broadcasted_iota(jnp.int32, (D, THIRD), 1)
        return mm(params[index : index + 1].astype(LOW), jnp.where(lane == out + THIRD * j, 1.0, 0.0).astype(LOW))

    q_bias, v_bias = of_heads(2), of_heads(3)

    await_quarter(1, 1)
    await_quarter(2, 3)
    plane_base = links.take(4)
    for k in (1, 2):
        links.send(pq.at[j, c], pq.at[j, c], plane_base + k, p.peer(k))
    gq.step1()
    gf.one()
    go.two()
    gq.step2()
    gq.step3()
    def await_plane(k, which):
        slot = pq.at[xor(j, k), c]
        part = slot.at[0:2] if which == 0 else slot.at[2:4] if which == 1 else slot
        return part, plane_base + (k if which == 2 else 3 * which)

    for k, part in ((1, 0), (2, 1)):
        slot, index = await_plane(k, 2)
        links.copy(slot, slot, index, p.here).wait_recv()
        slot, _ = await_plane(k, part)
        links.send(slot, slot, plane_base + 3 * part, p.peer(3 - k))
    gq.finish()

    att_base = links.take(4)

    def attend(k, carry):
        r = xor(j, k)
        across_nf.step(k)

        @pl.when(k > 0)
        def _():
            await_peer(seg, seg_base, k)

        made = mm(nf[r], wq[...])
        query = (made[:, :THIRD] + q_bias).astype(LOW)
        keys = made[:, THIRD : 2 * THIRD].astype(LOW)
        values = (made[:, 2 * THIRD :] + v_bias).astype(LOW)
        qkv[r, :, 0:THIRD] = query
        qkv[r, :, 256 : 256 + THIRD] = keys
        qkv[r, :, 512 : 512 + THIRD] = values
        across = jnp.broadcast_to(seg[r, 0:1], (ROWS, ROWS))
        row_at = lax.broadcasted_iota(jnp.int32, (ROWS, ROWS), 0)
        col_at = lax.broadcasted_iota(jnp.int32, (ROWS, ROWS), 1)
        allowed = jnp.where((across == across.T) & (col_at <= row_at), 1.0, 0.0)
        scores = jnp.where(
            jnp.concatenate([allowed] * 3, axis=0) > 0.5, mm_t(heads_of(query), keys) * (1.0 / math.sqrt(HD)), NEG
        )
        raised = jnp.exp(scores - jnp.max(scores, axis=-1, keepdims=True))
        probs = raised / jnp.sum(raised, axis=-1, keepdims=True)
        weights[r] = probs
        att[r] = heads_join(mm(probs.astype(LOW), values)).astype(LOW)

        @pl.when(k > 0)
        def _():
            links.copy(att.at[r], att_rx.at[j], att_base + k, p.peer(k)).start()

        return carry

    lax.fori_loop(0, 3, attend, 0)
    gf.step1()
    go.one()
    lax.fori_loop(3, 4, attend, 0)
    att_rx[j] = att[j]
    across_cot.first()
    across_cot.second()

    for part in (0, 1):
        slot, index = await_plane(3, part)
        links.copy(slot, slot, index, p.here).wait_recv()
    mate_base = links.take(1)
    links.send(pq.at[:, c], pq.at[:, c], mate_base, p.mate)
    go.step1()
    links.copy(pq.at[:, 1 - c], pq.at[:, 1 - c], mate_base, p.here).wait_recv()

    def assemble(i, carry):
        for t, a, b, at, to in TILES:
            top = pl.multiple_of(BLOCK * i + to, 16)
            wp[pl.ds(top, b - a), 128 * t : 128 * (t + 1)] = pq[at, i % 2, i // 2, a:b]
        return carry

    lax.fori_loop(0, 8, assemble, 0)

    total = tokens + params[4:5]
    for k in (0, 1, 2, 3):
        if k > 0:
            await_peer(att_rx, att_base, k)
        r = xor(j, k)
        total = total + mm(att_rx[r], wp[pl.ds(pl.multiple_of(r * THIRD, 16), THIRD)])
    res[...] = total
    unit, scale2 = normalize(total)
    unit2[...] = unit
    scales[:, 0:1] = scale1
    scales[:, 1:2] = scale2
    ns[j] = (unit * params[5:6] + params[6:7]).astype(LOW)
    across_ns.start()
    gf.step2()
    gf.step3()
    gf.finish()

    op_base = links.take(4)
    acc[...] = jnp.zeros_like(acc)
    root = math.sqrt(2.0 / math.pi)

    def prepare(k, carry):
        r = xor(j, k)
        across_ns.step(k)
        pre = mm(ns[r], wf[...]) + params[8:9]
        square = pre * pre
        tanh = jnp.tanh(root * pre * (1.0 + 0.044715 * square))
        hid[r] = (0.5 * pre * (1.0 + tanh)).astype(LOW)
        slope[r] = 0.5 * (1.0 + tanh) + 0.5 * pre * (1.0 - tanh * tanh) * (root * (1.0 + 3 * 0.044715 * square))
        return carry

    def project(k, carry):
        r = xor(j, k)
        op_tx[r] = mm(hid[r], wo[...]).astype(LOW)

        @pl.when(k > 0)
        def _():
            links.copy(op_tx.at[r], op_rx.at[j], op_base + k, p.peer(k)).start()

        return carry

    lax.fori_loop(0, 1, prepare, 0)
    go.step2()
    go.step3()
    go.finish()
    lax.fori_loop(1, 3, lambda k, carry: project(k, prepare(k, carry)), 0)
    lax.fori_loop(3, 4, prepare, 0)
    across_cot.finish()

    def whole(ref):
        return ref[...].reshape(4 * ROWS, -1)

    ro.fill(t_mm(whole(hid), whole(cots)))
    ro.pair()
    gns_base = links.take(4)

    def feed(i, carry):
        k = (i + 1) % 4
        r = xor(j, k)
        grad_pre = mm_t(cots[r], wo[...]) * slope[r]
        acc[0:1, :] += jnp.sum(grad_pre, axis=0, keepdims=True)
        gpl[r] = grad_pre.astype(LOW)
        gns_tx[r] = mm_t(gpl[r], wf[...]).astype(LOW)

        @pl.when(k > 0)
        def _():
            links.copy(gns_tx.at[r], gns_rx.at[j], gns_base + k, p.peer(k)).start()

        return carry

    lax.fori_loop(0, 4, feed, 0)
    ro.step1()
    rf.fill(t_mm(whole(ns), whole(gpl)))
    rf.pair()
    lax.fori_loop(3, 4, project, 0)
    rf.step1()
    ro.step2()

    grad = gns_tx[j].astype(WIDE)
    for k in (1, 2, 3):
        await_peer(gns_rx, gns_base, k)
        grad = grad + gns_rx[xor(j, k)].astype(WIDE)
    cot_own = cots[j].astype(WIDE)
    sums[5:6] = jnp.sum(grad * unit2[...], axis=0, keepdims=True)
    sums[6:7] = jnp.sum(grad, axis=0, keepdims=True)
    sums[7:8] = jnp.sum(cot_own, axis=0, keepdims=True)
    grad_res = cot_own + normalize_back(grad, unit2[...], scales[:, 1:2], params[5:6])
    gr[...] = grad_res
    sums[4:5] = jnp.sum(grad_res, axis=0, keepdims=True)
    grad_low = grad_res.astype(LOW)
    ga_base = links.take(4)
    for k in (3, 1, 2, 0):
        r = xor(j, k)
        ga_tx[r] = mm_t(grad_low, wp[pl.ds(pl.multiple_of(r * THIRD, 16), THIRD)]).astype(LOW)
        if k > 0:
            links.send(ga_tx.at[r], ga_rx.at[j], ga_base + k, p.peer(k))
    ga_rx[j] = ga_tx[j]
    lax.fori_loop(0, 1, project, 0)
    for r in range(4):
        made = t_mm(att_rx[r], grad_low)
        for c_at in range(2):
            for t, a, b, at, to in TILES:
                top = BLOCK * c_at + to
                pp[c_at, at, r, a:b] = made[top : top + b - a, 128 * t : 128 * (t + 1)].astype(LOW)
    pp_base = links.take(1)
    pp_sent = links.send(pp.at[1 - c], pp_got, pp_base, p.mate)
    rf.step2()
    pp_sent.wait_recv()
    pp_sum[...] = (pp[c].astype(WIDE) + pp_got[...].astype(WIDE)).astype(LOW)
    sum_pp.far()
    acc[8:9, :] = jnp.zeros((1, D), WIDE)

    def attend_back(i, carry):
        k = 3 - i
        r = xor(j, k)

        @pl.when(k > 0)
        def _():
            await_peer(ga_rx, ga_base, k)

        grad_att = ga_rx[r]
        query = qkv[r, :, 0:THIRD]
        keys = qkv[r, :, 256 : 256 + THIRD]
        values = qkv[r, :, 512 : 512 + THIRD]
        probs = weights[r]
        stacked = heads_of(grad_att)
        grad_values = t_mm(probs.astype(LOW), stacked)
        grad_probs = mm_t(stacked, values)
        delta = jnp.sum(heads_of(grad_att.astype(WIDE) * att[r].astype(WIDE)), axis=-1, keepdims=True)
        grad_scores = (probs * (grad_probs - delta) * (1.0 / math.sqrt(HD))).astype(LOW)
        grad_query = heads_join(mm(grad_scores, keys))
        grad_keys = t_mm(grad_scores, heads_of(query))
        acc[8:9, 0:THIRD] += jnp.sum(grad_query, axis=0, keepdims=True)
        acc[8:9, 256 : 256 + THIRD] += jnp.sum(grad_values, axis=0, keepdims=True)
        made = jnp.concatenate([grad_query, grad_keys, grad_values], axis=1).astype(LOW)
        gproj[r] = made
        gnf_tx[r] = mm_t(made, wq[...]).astype(LOW)
        pl.when(k == 3)(sum_gnf.far)
        return carry

    lax.fori_loop(0, 1, attend_back, 0)
    sum_pp.near()
    lax.fori_loop(1, 4, attend_back, 0)
    rq.fill(t_mm(whole(nf), whole(gproj)))
    rq.pair()
    sum_gnf.near()
    rq.step1()

    ro.finish(factor)
    do_base = links.take(4)
    do_recv = links.take(4)
    slot = (2 * j + c) % 4
    for k in (1, 2, 3):
        links.send(ro.final, do_ref.at[slot], do_base + k, (xor(j, k), 2 * z + half), do_recv + slot)
    across = links.copy(ro.final, do_ref.at[slot], do_base, p.mate, do_recv + slot)

    @pl.when(c == half)
    def _():
        do_ref[slot] = ro.final[...]

    @pl.when(c != half)
    def _():
        across.start()
        across.wait_send()

    rf.finish(factor)
    df_all[j] = rf.final[...]
    across_df.start()

    pz[...] = sum_pp.total().astype(LOW)
    pz_base = links.take(3)
    pz_sent = [
        links.send(pz.at[xor(z, 3)], pz_near.at[1], pz_base, p.one),
        links.send(pz.at[xor(z, 1)], pz_near.at[0], pz_base + 1, p.one),
    ]
    rq.step2()

    grad = sum_gnf.total()
    sums[0:1] = jnp.sum(grad * unit1[...], axis=0, keepdims=True)
    sums[1:2] = jnp.sum(grad, axis=0, keepdims=True)
    gt_ref[...] = gr[...] + normalize_back(grad, unit1[...], scales[:, 0:1], params[0:1])
    stores = [local(gt_ref, gt_hbm, 0)]

    out = lax.broadcasted_iota(jnp.int32, (THIRD, D), 1)
    lane = lax.broadcasted_iota(jnp.int32, (THIRD, D), 0)
    spot = jnp.where(out == lane + THIRD * j, 1.0, 0.0).astype(LOW)
    for row_at, lane_at in ((2, 0), (3, 256)):
        parts = three(acc[8:9, lane_at : lane_at + THIRD])
        sums[row_at : row_at + 1] = mm(parts[0], spot) + mm(parts[1], spot) + mm(parts[2], spot)
    sums[8:16] = jnp.broadcast_to(acc[0:1, :], (8, D))
    parts = three(sums[...])
    spread_out = mm_t(parts[0], place_m[...]) + mm_t(parts[1], place_m[...]) + mm_t(parts[2], place_m[...])
    line = lax.broadcasted_iota(jnp.int32, (8, 128), 0)
    own_lines = (line >= 2 * (j % 2)) & (line < 2 * (j % 2) + 2)
    for i in range(8):
        vt[i, 0:8] = spread_out[0:8, 128 * i : 128 * i + 128]
        at = 256 * (i // 2)
        even, more = spread_out[8:16, at : at + 128], spread_out[8:16, at + 128 : at + 256]
        picked = jnp.where((line & 1) == 0, even, more)
        vt[i, 8:16] = jnp.where(own_lines & (half == i % 2), picked, 0.0)
    vt_base = links.take(8)
    vt_sent = []
    for i in range(1, 8):
        device = p.at(i // 2, i % 2)
        vt_sent.append(links.send(vt.at[device[1]], vr.at[i], vt_base + i, device))

    pz_sent[0].wait_recv()
    pz_second[...] = (pz[xor(z, 2)].astype(WIDE) + pz_near[1].astype(WIDE)).astype(LOW)
    pz_last = links.send(pz_second, pz_far, pz_base + 2, p.two)
    rq.finish(factor)
    dq_all[j] = rq.final[...]
    across_dq.start()

    mine = vt[s]
    for i in range(1, 8):
        vt_sent[i - 1].wait_recv()
        mine = mine + vr[i]
    v2[...] = mine
    v2_base = links.take(4)
    to_peers(lambda k: v2, vr2, v2_base)

    pz_sent[1].wait_recv()
    pz_last.wait_recv()
    made = pz[z].astype(WIDE) + pz_near[0].astype(WIDE) + pz_far[...].astype(WIDE)
    pp_all[j] = (made * factor).astype(LOW)
    dp_base = links.take(4)
    to_peers(lambda k: pp_all.at[j], pp_all, dp_base)
    across_df.first()
    across_df.second()

    made = res[...] + params[7:8] + op_tx[j].astype(WIDE)
    for k in (1, 2, 3):
        await_peer(op_rx, op_base, k)
        made = made + op_rx[xor(j, k)].astype(WIDE)
    y_ref[...] = made.astype(LOW)
    stores.append(local(y_ref, y_hbm, 1))
    for i in range(4):
        here = (2 * c + i // 2 == j) & (c == i % 2)

        @pl.when(jnp.logical_not(here))
        def _():
            links.copy(do_ref.at[i], do_ref.at[i], do_base, p.here, do_recv + i).wait_recv()

    stores.append(local(do_ref, do_hbm, 2))
    across_dq.first()
    across_dq.second()
    across_df.finish()

    def into(dst, src, count):
        for r in range(4):
            for i in range(count):
                at = D * i + THIRD * r
                dst[:, at : at + THIRD] = src[r, :, THIRD * i : THIRD * (i + 1)]

    into(df_ref, df_all, 4)
    stores.append(local(df_ref, df_hbm, 3))
    for k in (1, 2, 3):
        await_peer(pp_all, dp_base, k)
    for t, a, b, at, to in TILES:
        dp_ref[to : to + b - a, 128 * t : 128 * (t + 1)] = pp_all[at, a:b]
    stores.append(local(dp_ref, dp_hbm, 4))
    mine = v2[...]
    for k in (1, 2, 3):
        await_peer(vr2, v2_base, k)
        mine = mine + vr2[xor(j, k)]
    dv_ref[...] = mine * factor
    stores.append(local(dv_ref, dv_hbm, 5))
    across_dq.finish()
    into(dq_ref, dq_all, 3)
    stores.append(local(dq_ref, dq_hbm, 6))

    for buf_of, dst, base in (
        (att, att_rx, att_base),
        (gns_tx, gns_rx, gns_base),
        (op_tx, op_rx, op_base),
    ):
        for k in (1, 2, 3):
            links.copy(buf_of.at[xor(j, k)], dst.at[j], base + k, p.peer(k)).wait_send()
    links.drain()
    for made in stores:
        made.wait()


def widen_kernel(
    y, gt, dq, dp, df, do, dv,
    y_out, gt_out, dq_out, dp_out, df_out, do_out, qv_out, fb_out, g1_out, s1_out, pb_out, g2_out, s2_out, ob_out,
    ins, outs, y_low, gt_low, dq_low, dp_low, df_low, do_low, dq_wide, dp_wide, df_wide, do_wide,
):
    def local(src, dst, sems, index):
        made = pltpu.make_async_copy(src, dst, sems.at[index])
        made.start()
        return made

    work = ((dq, dq_low, dq_wide, dq_out), (df, df_low, df_wide, df_out), (do, do_low, do_wide, do_out), (dp, dp_low, dp_wide, dp_out))
    loads = [local(src, low, ins, i) for i, (src, low, _, _) in enumerate(work)]
    plain = ((y, y_low, y_out), (gt, gt_low, gt_out))
    passing = [local(src, low, ins, 4 + i) for i, (src, low, _) in enumerate(plain)]
    done = []
    qv_out[...] = dv[2:4, 0:BLOCK]
    for i in range(4):
        fb_out[:, BLOCK * i : BLOCK * (i + 1)] = dv[8 + i : 9 + i, 0:BLOCK]
    for ref, i in zip((g1_out, s1_out, pb_out, g2_out, s2_out, ob_out), (0, 1, 4, 5, 6, 7)):
        ref[...] = dv[i : i + 1, 0:BLOCK]
    for i, (_, low, wide, out) in enumerate(work):
        loads[i].wait()
        wide[...] = low[...].reshape(wide.shape).astype(WIDE)
        done.append(local(wide, out, outs, i))
    for i, (_, low, out) in enumerate(plain):
        passing[i].wait()
        done.append(local(low, out, outs, 4 + i))
    for made in done:
        made.wait()


def vmem(*shape, kind=LOW):
    return pltpu.VMEM(shape, kind)


def fused_device(
    tokens,
    segment_ids,
    first_gain,
    first_shift,
    qkv_weight,
    qv_bias,
    proj_weight,
    proj_bias,
    second_gain,
    second_shift,
    fc_weight,
    fc_bias,
    out_weight,
    out_bias,
    cotangent,
):
    shards, reps = lax.axis_size("shard"), lax.axis_size("rep")
    factor = 1.0 / math.sqrt(ROWS * reps * shards)

    def reduce_bufs(width):
        return [
            vmem(4, 2, BLOCK, width),
            vmem(4, BLOCK, width),
            vmem(4, BLOCK, width),
            vmem(2, BLOCK, width),
            vmem(BLOCK, width),
            vmem(BLOCK, width),
            vmem(BLOCK, width),
        ]

    blocks = lambda width, kind=LOW: vmem(4, ROWS, width, kind=kind)
    scratch = [
        pltpu.SemaphoreType.DMA((160,)),
        pltpu.SemaphoreType.DMA((160,)),
        pltpu.SemaphoreType.DMA((8,)),
        vmem(ROWS, D),
        vmem(BLOCK, 3 * D),
        vmem(BLOCK, D),
        vmem(BLOCK, FF),
        vmem(4 * BLOCK, D),
        vmem(ROWS, D),
        vmem(ROWS, D, kind=WIDE),
        vmem(BLOCK, 3 * D),
        vmem(BLOCK, D),
        vmem(BLOCK, FF),
        vmem(4, BLOCK, D),
        vmem(16, 128, kind=WIDE),
        vmem(16, 128, kind=WIDE),
        vmem(16, 128),
        vmem(8, 16, 128),
        blocks(D),
        vmem(4, 8, ROWS, kind=WIDE),
        blocks(D),
        vmem(BLOCK, 3 * THIRD),
        vmem(BLOCK, D),
        vmem(D, 3 * THIRD),
        vmem(D, D),
        vmem(D, D),
        vmem(D, D),
        vmem(BLOCK, D),
        vmem(BLOCK, D),
        vmem(1024, D),
        vmem(16, D, kind=WIDE),
        blocks(D),
        vmem(4, 3 * ROWS, 128, kind=WIDE),
        blocks(THIRD),
        blocks(THIRD),
        vmem(ROWS, D, kind=WIDE),
        vmem(ROWS, D, kind=WIDE),
        vmem(ROWS, D, kind=WIDE),
        vmem(ROWS, 128, kind=WIDE),
        blocks(D),
        blocks(D),
        blocks(D, WIDE),
        blocks(D),
        blocks(D),
        blocks(D),
        blocks(D),
        blocks(D),
        blocks(THIRD),
        blocks(THIRD),
        blocks(D),
        blocks(D),
        vmem(2, ROWS // 2, D),
        vmem(2, 2, 144, 128),
        blocks(3 * THIRD),
        vmem(ROWS, D, kind=WIDE),
        vmem(16, D, kind=WIDE),
        vmem(16, D, kind=WIDE),
        vmem(8, 16, 128, kind=WIDE),
        vmem(8, 16, 128, kind=WIDE),
        vmem(16, 128, kind=WIDE),
        vmem(4, 16, 128, kind=WIDE),
        vmem(4, BLOCK, 3 * THIRD),
        vmem(4, BLOCK, D),
        vmem(576, 128),
        vmem(4, 2, 4, 144, 128),
        vmem(2, 4, 4, 144, 128),
        vmem(4, 4, 144, 128),
        vmem(4, 4, 144, 128),
        vmem(4, 4, 144, 128),
        vmem(4, 144, 128),
        vmem(2, 144, 128),
        vmem(144, 128),
        vmem(144, 128),
        vmem(4, 144, 128),
    ]
    for width in (3 * THIRD, D, D):
        scratch += reduce_bufs(width)
    in_vmem = pl.BlockSpec(memory_space=pltpu.VMEM)
    anywhere = pl.BlockSpec(memory_space=pl.ANY)
    partial = pl.pallas_call(
        functools.partial(layer_kernel, factor),
        out_shape=(
            jax.ShapeDtypeStruct((ROWS, D), LOW),
            jax.ShapeDtypeStruct((ROWS, D), WIDE),
            jax.ShapeDtypeStruct((BLOCK, 3 * D), LOW),
            jax.ShapeDtypeStruct((BLOCK, D), LOW),
            jax.ShapeDtypeStruct((BLOCK, FF), LOW),
            jax.ShapeDtypeStruct((4, BLOCK, D), LOW),
            jax.ShapeDtypeStruct((16, 128), WIDE),
        ),
        in_specs=[anywhere] * 2 + [in_vmem] * 9 + [anywhere] * 4,
        out_specs=(anywhere,) * 7,
        scratch_shapes=scratch,
        compiler_params=pltpu.CompilerParams(
            collective_id=0, has_side_effects=True, vmem_limit_bytes=56 * 1024 * 1024
        ),
    )(
        tokens,
        cotangent,
        segment_ids,
        first_gain[None],
        first_shift[None],
        qv_bias,
        proj_bias[None],
        second_gain[None],
        second_shift[None],
        fc_bias[None],
        out_bias[None],
        qkv_weight,
        proj_weight,
        fc_weight,
        out_weight,
    )
    rows = [jax.ShapeDtypeStruct((1, BLOCK), WIDE)] * 6
    y, grad_tokens, qkv_grad, proj_grad, fc_grad, out_grad, qv_grad, fc_bias_grad, *sums = pl.pallas_call(
        widen_kernel,
        out_shape=(
            jax.ShapeDtypeStruct((ROWS, D), LOW),
            jax.ShapeDtypeStruct((ROWS, D), WIDE),
            jax.ShapeDtypeStruct((BLOCK, 3 * D), WIDE),
            jax.ShapeDtypeStruct((BLOCK, D), WIDE),
            jax.ShapeDtypeStruct((BLOCK, FF), WIDE),
            jax.ShapeDtypeStruct((4 * BLOCK, D), WIDE),
            jax.ShapeDtypeStruct((2, BLOCK), WIDE),
            jax.ShapeDtypeStruct((1, 4 * BLOCK), WIDE),
            *rows,
        ),
        in_specs=[anywhere] * 6 + [in_vmem],
        out_specs=(anywhere,) * 6 + (in_vmem,) * 8,
        scratch_shapes=[
            pltpu.SemaphoreType.DMA((6,)),
            pltpu.SemaphoreType.DMA((6,)),
            vmem(ROWS, D),
            vmem(ROWS, D, kind=WIDE),
            vmem(BLOCK, 3 * D),
            vmem(BLOCK, D),
            vmem(BLOCK, FF),
            vmem(4, BLOCK, D),
            vmem(BLOCK, 3 * D, kind=WIDE),
            vmem(BLOCK, D, kind=WIDE),
            vmem(BLOCK, FF, kind=WIDE),
            vmem(4 * BLOCK, D, kind=WIDE),
        ],
        compiler_params=pltpu.CompilerParams(vmem_limit_bytes=56 * 1024 * 1024),
    )(*partial)
    first_gain_grad, first_shift_grad, proj_bias_grad, second_gain_grad, second_shift_grad, out_bias_grad = (
        row.reshape(BLOCK) for row in sums
    )
    return (
        y,
        grad_tokens,
        first_gain_grad,
        first_shift_grad,
        qkv_grad,
        qv_grad,
        proj_grad,
        proj_bias_grad,
        second_gain_grad,
        second_shift_grad,
        fc_grad,
        fc_bias_grad.reshape(4 * BLOCK),
        out_grad,
        out_bias_grad,
    )


def solution(mesh):
    return jax.shard_map(
        fused_device if dict(mesh.shape) == {"rep": 4, "shard": 8} else per_device,
        mesh=mesh,
        in_specs=(
            P(("rep", "shard"), None),
            P(("rep", "shard"), None),
            P("shard"),
            P("shard"),
            P("shard", None),
            P(None, "shard"),
            P("shard", None),
            P("shard"),
            P("shard"),
            P("shard"),
            P("shard", None),
            P("shard"),
            P("shard", None),
            P("shard"),
            P(("rep", "shard"), None),
        ),
        out_specs=(
            P(("rep", "shard"), None),
            P(("rep", "shard"), None),
            P("shard"),
            P("shard"),
            P("shard", None),
            P(None, "shard"),
            P("shard", None),
            P("shard"),
            P("shard"),
            P("shard"),
            P("shard", None),
            P("shard"),
            P("shard", None),
            P("shard"),
        ),
        check_vma=False,
    )
```

```python
import functools
import math

import jax
import jax.numpy as jnp
from jax import lax
from jax.experimental import pallas as pl
from jax.experimental.pallas import tpu as pltpu
from jax.sharding import PartitionSpec as P

D = 768
HEADS = 12
HD = 64
FF = 3072


EPSILON = 1e-05


def layer_norm(field, norm_gain, norm_shift):
    center = field - jnp.mean(field, axis=-1, keepdims=True)
    spread = jnp.mean(center * center, axis=-1, keepdims=True)
    return center * lax.rsqrt(spread + EPSILON) * norm_gain + norm_shift


def gelu_tanh(field):
    return jax.nn.gelu(field, approximate=True)


def head_split(matrix):
    return matrix.reshape(matrix.shape[0], HEADS, HD)


def masked_scores(query, keys, segments):
    rows = query.shape[0]
    scores = jnp.einsum(
        "qhd,khd->hqk", head_split(query), head_split(keys), preferred_element_type=jnp.float32
    ) * (1.0 / math.sqrt(HD))
    position = lax.iota(jnp.int32, rows)
    allowed = (segments[:, None] == segments[None, :]) & (position[None, :] <= position[:, None])
    return jnp.where(allowed[None], scores, -1e30)


def attend_forward(query, keys, values, segments):
    rows = query.shape[0]
    scores = masked_scores(query, keys, segments)
    row_max = jnp.max(scores, axis=-1, keepdims=True)
    row_total = jnp.sum(jnp.exp(scores - row_max), axis=-1, keepdims=True)
    logsum = row_max + jnp.log(row_total)
    probs = jnp.exp(scores - logsum).astype(jnp.bfloat16)
    attended = jnp.einsum(
        "hqk,khd->qhd", probs, head_split(values), preferred_element_type=jnp.float32
    )
    return (attended.reshape(rows, D).astype(jnp.bfloat16), logsum)


def attend_backward(query, keys, values, segments, attended, logsum, grad_attended):
    rows = query.shape[0]
    scores = masked_scores(query, keys, segments)
    weights = jnp.exp(scores - logsum)
    grad_heads = head_split(grad_attended)
    grad_values = jnp.einsum(
        "hqk,qhd->khd", weights.astype(jnp.bfloat16), grad_heads, preferred_element_type=jnp.float32
    )
    grad_probs = jnp.einsum(
        "qhd,khd->hqk", grad_heads, head_split(values), preferred_element_type=jnp.float32
    )
    delta = jnp.einsum(
        "qhd,qhd->hq", grad_heads, head_split(attended), preferred_element_type=jnp.float32
    )
    grad_scores = (weights * (grad_probs - delta[..., None]) * (1.0 / math.sqrt(HD))).astype(
        jnp.bfloat16
    )
    grad_query = jnp.einsum(
        "hqk,khd->qhd", grad_scores, head_split(keys), preferred_element_type=jnp.float32
    )
    grad_keys = jnp.einsum(
        "hqk,qhd->khd", grad_scores, head_split(query), preferred_element_type=jnp.float32
    )
    return (grad_query.reshape(rows, D), grad_keys.reshape(rows, D), grad_values.reshape(rows, D))


def exchange(field, axis, split, concat):
    return lax.all_to_all(field, axis, split_axis=split, concat_axis=concat, tiled=True)


def spread(field, axis):
    parts = lax.axis_size(axis)
    return exchange(jnp.broadcast_to(field[None], (parts,) + field.shape), axis, 0, 0)


def by_replica(field, shards, reps):
    rows = field.shape[0]
    return (
        field.reshape(shards, reps, rows // (shards * reps), -1).swapaxes(0, 1).reshape(rows, -1)
    )


def per_device(
    tokens,
    segment_ids,
    first_gain,
    first_shift,
    qkv_weight,
    qv_bias,
    proj_weight,
    proj_bias,
    second_gain,
    second_shift,
    fc_weight,
    fc_bias,
    out_weight,
    out_bias,
    cotangent,
):
    low = jnp.bfloat16
    segments = segment_ids[0]
    own_rows = tokens.shape[0]
    shards = lax.axis_size("shard")
    reps = lax.axis_size("rep")
    factor = 1.0 / math.sqrt(own_rows * reps * shards)
    small = jnp.stack(
        [first_gain, first_shift, qv_bias[0], qv_bias[1], proj_bias, second_gain, second_shift, out_bias]
    )
    small_full = lax.all_gather(small, "shard", axis=1, tiled=True).astype(jnp.float32)
    gain_one, shift_one, q_bias, v_bias, proj_bias_full, gain_two, shift_two, out_bias_full = (
        small_full[i] for i in range(8)
    )
    qkv_full = lax.all_gather(qkv_weight, "shard", axis=0, tiled=True)
    proj_full = lax.all_gather(proj_weight, "shard", axis=0, tiled=True)
    fc_cols = exchange(fc_weight, "shard", 1, 0)
    inputs = tokens.astype(jnp.float32)
    normed_f, first_back = jax.vjp(layer_norm, inputs, gain_one, shift_one)
    normed_first = normed_f.astype(low)
    projected = jnp.dot(normed_first, qkv_full, preferred_element_type=jnp.float32)
    query = (projected[:, :D] + q_bias).astype(low)
    keys = projected[:, D : 2 * D].astype(low)
    values = (projected[:, 2 * D :] + v_bias).astype(low)
    attended, logsum = attend_forward(query, keys, values, segments)
    residual = (
        inputs + jnp.dot(attended, proj_full, preferred_element_type=jnp.float32) + proj_bias_full
    )
    cot_f = cotangent.astype(jnp.float32)
    normed_s, second_back = jax.vjp(layer_norm, residual, gain_two, shift_two)
    normed_all = lax.all_gather(normed_s.astype(low), "shard", axis=0, tiled=True)
    cot_later, normed_all = lax.optimization_barrier((cotangent, normed_all))
    cot_all = lax.all_gather(cot_later, "shard", axis=0, tiled=True)
    pre_act = jnp.dot(normed_all, fc_cols, preferred_element_type=jnp.float32) + fc_bias.astype(
        jnp.float32
    )
    activated, gelu_back = jax.vjp(gelu_tanh, pre_act)
    hidden = activated.astype(low)
    grad_hidden = jnp.dot(cot_all, out_weight.T, preferred_element_type=jnp.float32)
    (grad_pre,) = gelu_back(grad_hidden)
    grad_pre_low = grad_pre.astype(low)
    grad_normed_part = jnp.dot(grad_pre_low, fc_cols.T, preferred_element_type=jnp.float32).astype(low)
    grad_normed_low = lax.psum_scatter(grad_normed_part, "shard", scatter_dimension=0, tiled=True)
    term_out_weight = jnp.dot(hidden.T, cot_all, preferred_element_type=jnp.float32) * factor
    term_fc_weight = jnp.dot(normed_all.T, grad_pre_low, preferred_element_type=jnp.float32) * factor
    out_part = jnp.dot(hidden, out_weight, preferred_element_type=jnp.float32).astype(low)
    ff_terms = jnp.concatenate(
        [
            term_out_weight.astype(low).reshape(reps, -1, D),
            by_replica(term_fc_weight.astype(low), shards, reps).reshape(reps, -1, D),
        ],
        axis=1,
    )
    ff_sum = jnp.sum(exchange(ff_terms, "rep", 0, 0).astype(jnp.float32), axis=0).astype(low)
    first_later, attended_later, grad_normed_low, ff_sum = lax.optimization_barrier(
        (normed_first, attended, grad_normed_low, ff_sum)
    )
    first_all = lax.all_gather(first_later, "shard", axis=0, tiled=True)
    grad_normed_second = grad_normed_low.astype(jnp.float32)

    grad_from_norm, second_gain_sum, second_shift_sum = second_back(grad_normed_second)
    grad_residual = cot_f + grad_from_norm
    grad_residual_low = grad_residual.astype(low)
    grad_residual_all = lax.all_gather(grad_residual_low, "shard", axis=0, tiled=True)
    attended_cols = exchange(attended_later, "shard", 1, 0)
    grad_attended = jnp.dot(
        grad_residual_low, proj_full.T, preferred_element_type=jnp.float32
    ).astype(low)
    out_rows = out_weight.shape[0] // reps
    out_piece = ff_sum[:out_rows]
    fc_piece = ff_sum[out_rows:].reshape(D // reps, -1)
    fc_piece = exchange(fc_piece, "shard", 0, 1)
    ff_all = spread(jnp.concatenate([out_piece, fc_piece.reshape(-1, D)]), "rep").astype(jnp.float32)

    grad_query, grad_keys, grad_values = attend_backward(
        query, keys, values, segments, attended, logsum, grad_attended
    )
    grad_projected = jnp.concatenate([grad_query, grad_keys, grad_values], axis=1).astype(low)
    grad_projected, ff_all = lax.optimization_barrier((grad_projected, ff_all))
    out_grad = ff_all[:, :out_rows].reshape(-1, D)
    fc_grad = ff_all[:, out_rows:].reshape(-1, FF)
    grad_cols = exchange(grad_projected, "shard", 1, 0)
    grad_normed_first = jnp.dot(grad_projected, qkv_full.T, preferred_element_type=jnp.float32)
    out_later, grad_cols = lax.optimization_barrier((out_part, grad_cols))
    out_sum = lax.psum_scatter(out_later, "shard", scatter_dimension=0, tiled=True)
    result = (residual + out_sum.astype(jnp.float32) + out_bias_full).astype(low)
    term_qkv_weight = jnp.dot(first_all.T, grad_cols, preferred_element_type=jnp.float32) * factor
    term_proj_weight = (
        jnp.dot(attended_cols.T, grad_residual_all, preferred_element_type=jnp.float32) * factor
    )
    attn_terms = jnp.concatenate(
        [
            term_proj_weight.astype(low).reshape(reps, -1, D),
            by_replica(term_qkv_weight.astype(low), shards, reps).reshape(reps, -1, D),
        ],
        axis=1,
    )
    attn_sum = jnp.sum(exchange(attn_terms, "rep", 0, 0).astype(jnp.float32), axis=0).astype(low)
    proj_rows = proj_weight.shape[0] // reps
    proj_piece = attn_sum[:proj_rows]
    qkv_piece = attn_sum[proj_rows:].reshape(D // reps, -1)
    qkv_piece = exchange(qkv_piece, "shard", 0, 1)
    attn_all = spread(jnp.concatenate([proj_piece, qkv_piece.reshape(-1, D)]), "rep").astype(
        jnp.float32
    )
    proj_grad = attn_all[:, :proj_rows].reshape(-1, D)
    qkv_grad = attn_all[:, proj_rows:].reshape(-1, 3 * D)

    grad_input_norm, first_gain_sum, first_shift_sum = first_back(grad_normed_first)
    grad_inputs = grad_residual + grad_input_norm
    terms = jnp.stack(
        [
            first_gain_sum,
            first_shift_sum,
            jnp.sum(grad_query, axis=0),
            jnp.sum(grad_values, axis=0),
            jnp.sum(grad_residual, axis=0),
            second_gain_sum,
            second_shift_sum,
            jnp.sum(cot_f, axis=0),
        ]
    )
    count = terms.shape[0]
    terms = terms.reshape(count, shards, -1).swapaxes(0, 1).reshape(shards, -1)
    own_terms = jnp.concatenate(
        [jnp.sum(exchange(terms, "shard", 0, 0), axis=0), jnp.sum(grad_pre, axis=0)]
    )
    sums = jnp.sum(spread(own_terms, "rep"), axis=0) * factor
    own_cols = D // shards
    fc_bias_grad = sums[count * own_cols :]
    sums = sums[: count * own_cols].reshape(count, own_cols)
    return (
        result,
        grad_inputs,
        sums[0],
        sums[1],
        qkv_grad,
        sums[2:4],
        proj_grad,
        sums[4],
        sums[5],
        sums[6],
        fc_grad,
        fc_bias_grad,
        out_grad,
        sums[7],
    )

MESH = pl.DeviceIdType.MESH
LOW = jnp.bfloat16
WIDE = jnp.float32
ROWS = 128
BLOCK = 96
THIRD = 192
NEG = -1e30


def xor(a, b):
    return (a // 2 + b // 2) % 2 * 2 + (a + b) % 2


def mm(a, b):
    return jnp.dot(a, b, preferred_element_type=WIDE)


def mm_t(a, b):
    return lax.dot_general(a, b, (((1,), (1,)), ((), ())), preferred_element_type=WIDE)


def t_mm(a, b):
    return lax.dot_general(a, b, (((0,), (0,)), ((), ())), preferred_element_type=WIDE)


def three(field):
    first = field.astype(LOW)
    rest = field - first.astype(WIDE)
    second = rest.astype(LOW)
    return first, second, (rest - second.astype(WIDE)).astype(LOW)


def normalize(field):
    center = field - jnp.mean(field, axis=-1, keepdims=True)
    scale = lax.rsqrt(jnp.mean(center * center, axis=-1, keepdims=True) + EPSILON)
    return center * scale, scale


def normalize_back(grad, unit, scale, gain):
    inner = grad * gain
    mean = jnp.mean(inner, axis=-1, keepdims=True)
    along = jnp.mean(inner * unit, axis=-1, keepdims=True)
    return scale * (inner - mean - unit * along)


def heads_of(field):
    lane = lax.broadcasted_iota(jnp.int32, field.shape, 1)
    zero = jnp.zeros_like(field)
    return jnp.concatenate(
        [jnp.where((lane >= h * HD) & (lane < (h + 1) * HD), field, zero) for h in range(3)], axis=0
    )


def heads_join(stacked):
    lane = lax.broadcasted_iota(jnp.int32, (ROWS, THIRD), 1)
    return jnp.where(
        lane < HD, stacked[:ROWS], jnp.where(lane < 2 * HD, stacked[ROWS : 2 * ROWS], stacked[2 * ROWS :])
    )


class Links:
    def __init__(self, sends, recvs):
        self.sends, self.recvs, self.used, self.open, self.later = sends, recvs, 0, [], []

    def take(self, count=1):
        self.used += count
        return self.used - count

    def copy(self, src, dst, index, device, recv_index=None):
        recv_index = index if recv_index is None else recv_index
        return pltpu.make_async_remote_copy(
            src_ref=src,
            dst_ref=dst,
            send_sem=self.sends.at[index],
            recv_sem=self.recvs.at[recv_index],
            device_id=device,
            device_id_type=MESH,
        )

    def send(self, src, dst, index, device, recv_index=None):
        made = self.copy(src, dst, index, device, recv_index)
        made.start()
        self.open.append(made)
        return made

    def drain(self):
        for made in self.open:
            made.wait_send()
        for copies in self.later:
            for made in copies():
                made.wait_send()


class Gather:
    def __init__(self, links, place, own, full):
        self.links, self.place, self.own, self.full = links, place, own, full
        self.base = links.take(7)

    def slot(self, z, c):
        return self.full.at[pl.ds(pl.multiple_of((2 * z + c) * BLOCK, 16), BLOCK)]

    def arrived(self, which, slot):
        self.links.copy(slot, slot, self.base + which, self.place.here).wait_recv()

    def pass_on(self, which, slot, device):
        self.links.send(slot, slot, self.base + which, device)

    def two(self):
        p = self.place
        self.links.send(self.own, self.slot(p.z, p.c), self.base, p.two)

    def one(self):
        p = self.place
        mine = self.slot(p.z, p.c)
        self.links.send(self.own, mine, self.base + 1, p.one)
        self.links.send(self.own, mine, self.base + 2, p.mate)
        mine[...] = self.own[...]

    def step1(self):
        p = self.place
        slot = self.slot(xor(p.z, 2), p.c)
        self.arrived(0, slot)
        self.pass_on(3, slot, p.one)
        self.pass_on(4, slot, p.mate)

    def step2(self):
        p = self.place
        slot = self.slot(xor(p.z, 1), p.c)
        self.arrived(1, slot)
        self.pass_on(5, slot, p.mate)

    def step3(self):
        p = self.place
        slot = self.slot(xor(p.z, 3), p.c)
        self.arrived(3, slot)
        self.pass_on(6, slot, p.mate)

    def finish(self):
        p = self.place
        for which, flip in ((2, 0), (4, 2), (5, 1), (6, 3)):
            self.arrived(which, self.slot(xor(p.z, flip), 1 - p.c))


class Across:
    def __init__(self, links, place, buf, cut):
        self.links, self.place, self.buf, self.cut = links, place, buf, cut
        self.base = links.take(6)
        links.later.append(self.copies)

    def part(self, k, second):
        slot = self.buf.at[xor(self.place.j, k)]
        rows = self.buf.shape[1]
        return slot.at[self.cut : rows] if second else slot.at[0 : self.cut]

    def copy(self, which):
        p, links = self.place, self.links
        k, second = ((0, False), (0, True), (1, False), (2, True), (0, True), (0, False))[which]
        src = self.part(k, second)
        return links.copy(src, src, self.base + which, p.peer((1, 2, 2, 1, 1, 2)[which]))

    def copies(self):
        return [self.copy(which) for which in range(6)]

    def arrived(self, which, slot):
        self.links.copy(slot, slot, self.base + which, self.place.here).wait_recv()

    def start(self):
        for which in (0, 1, 4, 5):
            self.copy(which).start()

    def first(self):
        self.pass_on()
        self.arrived(4, self.part(1, True))

    def second(self):
        self.arrived(5, self.part(2, False))

    def pass_on(self):
        self.arrived(0, self.part(1, False))
        self.copy(2).start()
        self.arrived(1, self.part(2, True))
        self.copy(3).start()

    def finish(self):
        self.arrived(2, self.part(3, False))
        self.arrived(3, self.part(3, True))

    def step(self, k):
        pl.when(k == 1)(self.first)
        pl.when(k == 2)(self.second)
        pl.when(k == 3)(self.finish)


class AcrossSum:
    def __init__(self, links, place, parts, got, hop, cut):
        self.links, self.place, self.parts, self.got, self.hop, self.cut = links, place, parts, got, hop, cut
        self.base = links.take(4)
        links.later.append(lambda: [self.copy(which) for which in range(4)])

    def block(self, k):
        return self.parts.at[xor(self.place.j, k)]

    def copy(self, which):
        p = self.place
        if which < 2:
            src = self.block(3)
            src = src.at[self.cut : self.parts.shape[1]] if which else src.at[0 : self.cut]
            return self.links.copy(src, self.hop.at[which], self.base + which, p.peer(which + 1))
        return self.links.copy(self.block(which - 1), self.got.at[p.j], self.base + which, p.peer(which - 1))

    def far(self):
        self.copy(0).start()
        self.copy(1).start()

    def near(self):
        for which in range(2):
            self.copy(which).wait_recv()
            at = xor(self.place.j, 2 - which)
            rows = slice(self.cut, self.parts.shape[1]) if which else slice(0, self.cut)
            self.parts[at, rows] = (self.parts[at, rows].astype(WIDE) + self.hop[which].astype(WIDE)).astype(LOW)
            self.copy(3 - which).start()

    def total(self):
        j = self.place.j
        total = self.parts[j].astype(WIDE)
        for k in (1, 2):
            slot = self.got.at[xor(j, k)]
            self.links.copy(slot, slot, self.base + 1 + k, self.place.here).wait_recv()
            total = total + self.got[xor(j, k)].astype(WIDE)
        return total


class Reduce:
    def __init__(self, links, place, bufs):
        self.links, self.place = links, place
        self.part, self.got, self.total, self.near, self.second, self.far, self.final = bufs
        self.base = links.take(4)

    def fill(self, full):
        for z in range(4):
            for c in range(2):
                at = (2 * z + c) * BLOCK
                self.part[z, c] = full[at : at + BLOCK].astype(LOW)

    def pair(self):
        p = self.place
        self.sent = self.links.send(self.part.at[:, 1 - p.c], self.got, self.base, p.mate)

    def step1(self):
        p = self.place
        self.sent.wait_recv()
        for z in range(4):
            self.total[z] = (self.part[z, p.c].astype(WIDE) + self.got[z].astype(WIDE)).astype(LOW)
        self.first = [
            self.links.send(self.total.at[xor(p.z, 3)], self.near.at[1], self.base + 1, p.one),
            self.links.send(self.total.at[xor(p.z, 1)], self.near.at[0], self.base + 2, p.one),
        ]

    def step2(self):
        p = self.place
        self.first[0].wait_recv()
        self.second[...] = (self.total[xor(p.z, 2)].astype(WIDE) + self.near[1].astype(WIDE)).astype(LOW)
        self.last = self.links.send(self.second, self.far, self.base + 3, p.two)

    def finish(self, factor):
        p = self.place
        self.first[1].wait_recv()
        self.last.wait_recv()
        whole = self.total[p.z].astype(WIDE) + self.near[0].astype(WIDE) + self.far[...].astype(WIDE)
        self.final[...] = (whole * factor).astype(LOW)


class Place:
    def __init__(self):
        self.j, self.s = lax.axis_index("rep"), lax.axis_index("shard")
        self.z, self.c = self.s // 2, self.s % 2
        self.here = (self.j, self.s)
        self.mate = self.at(0, 1)
        self.one = self.at(1, 0)
        self.two = self.at(2, 0)

    def at(self, flip_z, flip_c):
        return (self.j, 2 * xor(self.z, flip_z) + (self.c + flip_c) % 2)

    def peer(self, k):
        return (xor(self.j, k), self.s)


TILES = tuple(
    (t, max(96 * t, 144 * q) - 144 * q, min(96 * t + 96, 144 * q + 144) - 144 * q, q, max(96 * t, 144 * q) - 96 * t)
    for t in range(6)
    for q in range(4)
    if max(96 * t, 144 * q) < min(96 * t + 96, 144 * q + 144)
)


def layer_kernel(
    factor,
    tok_hbm, cot_hbm, seg_in, g1_in, s1_in, qvb_in, pb_in, g2_in, s2_in, fb_in, ob_in, qkv_hbm, wp_hbm, fc_hbm, wo_hbm,
    y_hbm, gt_hbm, dq_hbm, dp_hbm, df_hbm, do_hbm, dv_hbm,
    sends, recvs, locals_,
    tok, qkv_in, wp_in, fc_in, wo_in, y_ref, gt_ref, dq_ref, dp_ref, df_ref, do_ref, dv_ref,
    vec_wide, vec_in, vec_all, nf, seg, cots, wq_in, wf_in, wq, wp, wf, wo, out_own, out_got, place_m, params,
    qkv, weights, att, att_rx, res, unit1, unit2, scales,
    ns, hid, slope, gpl, gns_tx, gns_rx, op_tx, op_rx, ga_tx, ga_rx, gnf_tx, gnf_rx, gnf_hop, pp_hop, gproj, gr,
    sums, acc, vt, vr, v2, vr2, dq_all, df_all,
    pt_own, pq, pp, pp_got, pp_sum, pp_rx, pz, pz_near, pz_second, pz_far, pp_all,
    *reduce_bufs,
):
    p = Place()
    j, s, z, c = p.j, p.s, p.z, p.c
    half = j // 2
    odd = j % 2 == 1
    links = Links(sends, recvs)

    def local(src, dst, index):
        made = pltpu.make_async_copy(src, dst, locals_.at[index])
        made.start()
        return made

    load_qkv = local(qkv_hbm, qkv_in, 0)
    load_wp = local(wp_hbm, wp_in, 1)
    load_cot = local(cot_hbm, cots.at[j], 2)
    load_fc = local(fc_hbm, fc_in, 3)
    load_wo = local(wo_hbm, wo_in, 4)
    load_tok = local(tok_hbm, tok, 5)

    partners = [p.at(fz, fc) for fz in range(4) for fc in range(2) if (fz, fc) != (0, 0)]
    partners += [p.peer(k) for k in (1, 2, 3)]
    partners += [(xor(j, k), 2 * z + 1 - c) for k in (1, 2, 3)]
    barrier = pltpu.get_barrier_semaphore()
    for device in partners:
        pl.semaphore_signal(barrier, inc=1, device_id=device, device_id_type=MESH)

    def columns(src, dst, count):
        for i in range(count):
            wide = src[:, pl.ds(pl.multiple_of(D * i + 128 * (3 * j // 2), 128), 256)]
            dst[:, THIRD * i : THIRD * (i + 1)] = jnp.where(odd, wide[:, 64:], wide[:, :THIRD])

    vec_wide[...] = jnp.zeros_like(vec_wide)
    for i, ref in enumerate((g1_in, s1_in, None, None, pb_in, g2_in, s2_in, ob_in)):
        if ref is not None:
            vec_wide[i : i + 1, 0:BLOCK] = ref[...].astype(WIDE)
    vec_wide[2:4, 0:BLOCK] = qvb_in[...].astype(WIDE)
    bias_row = fb_in[...].astype(WIDE)
    for i in range(2):
        low_part, high_part = (bias_row[:, THIRD * h + BLOCK * i : THIRD * h + BLOCK * (i + 1)] for h in range(2))
        vec_wide[8 + i : 9 + i, 0:BLOCK] = jnp.where(odd, high_part, low_part)
    vec_in[...] = vec_wide[...].astype(LOW)
    seg[j] = jnp.broadcast_to(seg_in[...].astype(WIDE), (8, ROWS))
    load_qkv.wait()
    columns(qkv_in, wq_in, 3)
    load_wp.wait()
    for t in range(6):
        pt_own[BLOCK * t : BLOCK * (t + 1)] = wp_in[:, 128 * t : 128 * (t + 1)]

    gq = Gather(links, p, wq_in, wq)
    gf = Gather(links, p, wf_in, wf)
    go = Gather(links, p, out_own, wo)
    rq, rf, ro = (Reduce(links, p, reduce_bufs[7 * i : 7 * i + 7]) for i in range(3))
    across_nf = Across(links, p, nf, ROWS // 2)
    across_cot = Across(links, p, cots, ROWS // 2)
    across_ns = Across(links, p, ns, ROWS // 2)
    across_df = Across(links, p, df_all, BLOCK // 2)
    sum_gnf = AcrossSum(links, p, gnf_tx, gnf_rx, gnf_hop, ROWS // 2)
    sum_pp = AcrossSum(links, p, pp_sum, pp_rx, pp_hop, 2)
    across_dq = Across(links, p, dq_all, BLOCK // 2)
    load_cot.wait()
    pl.semaphore_wait(barrier, len(partners))

    vec_base = links.take(8)
    vec_sent = []
    for i in range(1, 8):
        vec_sent.append(links.send(vec_in, vec_all.at[s], vec_base + i, p.at(i // 2, i % 2)))
    def to_peers(src_of, dst, base):
        return [links.send(src_of(k), dst.at[j], base + k, p.peer(k)) for k in (1, 2, 3)]

    def await_peer(dst, base, k):
        slot = dst.at[xor(j, k)]
        links.copy(slot, slot, base + k, p.here).wait_recv()

    quarter = pt_own.at[pl.ds(pl.multiple_of(144 * j, 16), 144)]
    pq_base = links.take(3)
    pq[j, c, z] = pt_own[pl.ds(pl.multiple_of(144 * j, 16), 144)]
    links.send(quarter, pq.at[j, c, z], pq_base, p.two)
    links.send(quarter, pq.at[j, c, z], pq_base + 1, p.one)
    gq.two()
    gq.one()

    def await_quarter(which, flip):
        slot = pq.at[j, c, xor(z, flip)]
        links.copy(slot, slot, pq_base + which, p.here).wait_recv()

    seg_base = links.take(4)
    to_peers(lambda k: seg.at[j], seg, seg_base)
    across_cot.start()
    load_wo.wait()
    out_base = links.take(1)
    out_sent = links.send(
        wo_in.at[pl.ds(pl.multiple_of((THIRD * j + BLOCK * (1 - c)) % 384, 16), BLOCK)], out_got, out_base, p.mate
    )
    load_fc.wait()
    columns(fc_in, wf_in, 4)
    gf.two()
    vec_all[s] = vec_in[...]

    row = lax.broadcasted_iota(jnp.int32, (1024, D), 0)
    col = lax.broadcasted_iota(jnp.int32, (1024, D), 1)
    inside = (row & 127) < BLOCK
    place_m[...] = jnp.where(inside & (col == BLOCK * (row >> 7) + (row & 127)), 1.0, 0.0).astype(LOW)

    load_tok.wait()
    tokens = tok[...].astype(WIDE)
    unit, scale1 = normalize(tokens)
    unit1[...] = unit
    for i in range(1, 8):
        vec_sent[i - 1].wait_recv()
    small = mm(jnp.concatenate([vec_all[i] for i in range(8)], axis=1), place_m[...])
    pieces = [vec_all[2 * (i // 2) + half][8 + i % 2 : 9 + i % 2] for i in range(8)]
    fc_bias = mm(jnp.concatenate(pieces, axis=1), place_m[...])
    params[0:8] = small[0:8]
    params[8:9] = fc_bias
    nf[j] = (unit * params[0:1] + params[1:2]).astype(LOW)
    across_nf.start()
    await_quarter(0, 2)
    links.send(pq.at[j, c, xor(z, 2)], pq.at[j, c, xor(z, 2)], pq_base + 2, p.one)

    out_sent.wait_recv()
    mine = wo_in[pl.ds(pl.multiple_of((THIRD * j + BLOCK * c) % 384, 16), BLOCK)]
    out_own[...] = jnp.where(c == half, mine, out_got[...])

    def of_heads(index):
        lane = lax.broadcasted_iota(jnp.int32, (D, THIRD), 0)
        out = lax.broadcasted_iota(jnp.int32, (D, THIRD), 1)
        return mm(params[index : index + 1].astype(LOW), jnp.where(lane == out + THIRD * j, 1.0, 0.0).astype(LOW))

    q_bias, v_bias = of_heads(2), of_heads(3)

    await_quarter(1, 1)
    await_quarter(2, 3)
    plane_base = links.take(4)
    for k in (1, 2):
        links.send(pq.at[j, c], pq.at[j, c], plane_base + k, p.peer(k))
    gq.step1()
    gf.one()
    go.two()
    gq.step2()
    gq.step3()
    def await_plane(k, which):
        slot = pq.at[xor(j, k), c]
        part = slot.at[0:2] if which == 0 else slot.at[2:4] if which == 1 else slot
        return part, plane_base + (k if which == 2 else 3 * which)

    for k, part in ((1, 0), (2, 1)):
        slot, index = await_plane(k, 2)
        links.copy(slot, slot, index, p.here).wait_recv()
        slot, _ = await_plane(k, part)
        links.send(slot, slot, plane_base + 3 * part, p.peer(3 - k))
    gq.finish()

    att_base = links.take(4)

    def attend(k, carry):
        r = xor(j, k)
        across_nf.step(k)

        @pl.when(k > 0)
        def _():
            await_peer(seg, seg_base, k)

        made = mm(nf[r], wq[...])
        query = (made[:, :THIRD] + q_bias).astype(LOW)
        keys = made[:, THIRD : 2 * THIRD].astype(LOW)
        values = (made[:, 2 * THIRD :] + v_bias).astype(LOW)
        qkv[r, :, 0:THIRD] = query
        qkv[r, :, 256 : 256 + THIRD] = keys
        qkv[r, :, 512 : 512 + THIRD] = values
        across = jnp.broadcast_to(seg[r, 0:1], (ROWS, ROWS))
        row_at = lax.broadcasted_iota(jnp.int32, (ROWS, ROWS), 0)
        col_at = lax.broadcasted_iota(jnp.int32, (ROWS, ROWS), 1)
        allowed = jnp.where((across == across.T) & (col_at <= row_at), 1.0, 0.0)
        scores = jnp.where(
            jnp.concatenate([allowed] * 3, axis=0) > 0.5, mm_t(heads_of(query), keys) * (1.0 / math.sqrt(HD)), NEG
        )
        raised = jnp.exp(scores - jnp.max(scores, axis=-1, keepdims=True))
        probs = raised / jnp.sum(raised, axis=-1, keepdims=True)
        weights[r] = probs
        att[r] = heads_join(mm(probs.astype(LOW), values)).astype(LOW)

        @pl.when(k > 0)
        def _():
            links.copy(att.at[r], att_rx.at[j], att_base + k, p.peer(k)).start()

        return carry

    lax.fori_loop(0, 3, attend, 0)
    gf.step1()
    go.one()
    lax.fori_loop(3, 4, attend, 0)
    att_rx[j] = att[j]
    across_cot.first()
    across_cot.second()

    for part in (0, 1):
        slot, index = await_plane(3, part)
        links.copy(slot, slot, index, p.here).wait_recv()
    mate_base = links.take(1)
    links.send(pq.at[:, c], pq.at[:, c], mate_base, p.mate)
    go.step1()
    links.copy(pq.at[:, 1 - c], pq.at[:, 1 - c], mate_base, p.here).wait_recv()

    def assemble(i, carry):
        for t, a, b, at, to in TILES:
            top = pl.multiple_of(BLOCK * i + to, 16)
            wp[pl.ds(top, b - a), 128 * t : 128 * (t + 1)] = pq[at, i % 2, i // 2, a:b]
        return carry

    lax.fori_loop(0, 8, assemble, 0)

    total = tokens + params[4:5]
    for k in (0, 1, 2, 3):
        if k > 0:
            await_peer(att_rx, att_base, k)
        r = xor(j, k)
        total = total + mm(att_rx[r], wp[pl.ds(pl.multiple_of(r * THIRD, 16), THIRD)])
    res[...] = total
    unit, scale2 = normalize(total)
    unit2[...] = unit
    scales[:, 0:1] = scale1
    scales[:, 1:2] = scale2
    ns[j] = (unit * params[5:6] + params[6:7]).astype(LOW)
    across_ns.start()
    gf.step2()
    gf.step3()
    gf.finish()

    op_base = links.take(4)
    acc[...] = jnp.zeros_like(acc)
    root = math.sqrt(2.0 / math.pi)

    def prepare(k, carry):
        r = xor(j, k)
        across_ns.step(k)
        pre = mm(ns[r], wf[...]) + params[8:9]
        square = pre * pre
        tanh = jnp.tanh(root * pre * (1.0 + 0.044715 * square))
        hid[r] = (0.5 * pre * (1.0 + tanh)).astype(LOW)
        slope[r] = 0.5 * (1.0 + tanh) + 0.5 * pre * (1.0 - tanh * tanh) * (root * (1.0 + 3 * 0.044715 * square))
        return carry

    def project(k, carry):
        r = xor(j, k)
        op_tx[r] = mm(hid[r], wo[...]).astype(LOW)

        @pl.when(k > 0)
        def _():
            links.copy(op_tx.at[r], op_rx.at[j], op_base + k, p.peer(k)).start()

        return carry

    lax.fori_loop(0, 1, prepare, 0)
    go.step2()
    go.step3()
    go.finish()
    lax.fori_loop(1, 3, lambda k, carry: project(k, prepare(k, carry)), 0)
    lax.fori_loop(3, 4, prepare, 0)
    across_cot.finish()

    def whole(ref):
        return ref[...].reshape(4 * ROWS, -1)

    ro.fill(t_mm(whole(hid), whole(cots)))
    ro.pair()
    gns_base = links.take(4)

    def feed(i, carry):
        k = (i + 1) % 4
        r = xor(j, k)
        grad_pre = mm_t(cots[r], wo[...]) * slope[r]
        acc[0:1, :] += jnp.sum(grad_pre, axis=0, keepdims=True)
        gpl[r] = grad_pre.astype(LOW)
        gns_tx[r] = mm_t(gpl[r], wf[...]).astype(LOW)

        @pl.when(k > 0)
        def _():
            links.copy(gns_tx.at[r], gns_rx.at[j], gns_base + k, p.peer(k)).start()

        return carry

    lax.fori_loop(0, 4, feed, 0)
    ro.step1()
    rf.fill(t_mm(whole(ns), whole(gpl)))
    rf.pair()
    rf.step1()
    ro.step2()

    grad = gns_tx[j].astype(WIDE)
    for k in (1, 2, 3):
        await_peer(gns_rx, gns_base, k)
        grad = grad + gns_rx[xor(j, k)].astype(WIDE)
    cot_own = cots[j].astype(WIDE)
    sums[5:6] = jnp.sum(grad * unit2[...], axis=0, keepdims=True)
    sums[6:7] = jnp.sum(grad, axis=0, keepdims=True)
    sums[7:8] = jnp.sum(cot_own, axis=0, keepdims=True)
    grad_res = cot_own + normalize_back(grad, unit2[...], scales[:, 1:2], params[5:6])
    gr[...] = grad_res
    sums[4:5] = jnp.sum(grad_res, axis=0, keepdims=True)
    grad_low = grad_res.astype(LOW)
    ga_base = links.take(4)
    for k in (3, 1, 2, 0):
        r = xor(j, k)
        ga_tx[r] = mm_t(grad_low, wp[pl.ds(pl.multiple_of(r * THIRD, 16), THIRD)]).astype(LOW)
        if k > 0:
            links.send(ga_tx.at[r], ga_rx.at[j], ga_base + k, p.peer(k))
    ga_rx[j] = ga_tx[j]
    lax.fori_loop(3, 4, project, 0)
    lax.fori_loop(0, 1, project, 0)
    for r in range(4):
        made = t_mm(att_rx[r], grad_low)
        for c_at in range(2):
            for t, a, b, at, to in TILES:
                top = BLOCK * c_at + to
                pp[c_at, at, r, a:b] = made[top : top + b - a, 128 * t : 128 * (t + 1)].astype(LOW)
    pp_base = links.take(1)
    pp_sent = links.send(pp.at[1 - c], pp_got, pp_base, p.mate)
    rf.step2()
    pp_sent.wait_recv()
    pp_sum[...] = (pp[c].astype(WIDE) + pp_got[...].astype(WIDE)).astype(LOW)
    sum_pp.far()
    acc[8:9, :] = jnp.zeros((1, D), WIDE)

    def attend_back(i, carry):
        k = 3 - i
        r = xor(j, k)

        @pl.when(k > 0)
        def _():
            await_peer(ga_rx, ga_base, k)

        grad_att = ga_rx[r]
        query = qkv[r, :, 0:THIRD]
        keys = qkv[r, :, 256 : 256 + THIRD]
        values = qkv[r, :, 512 : 512 + THIRD]
        probs = weights[r]
        stacked = heads_of(grad_att)
        grad_values = t_mm(probs.astype(LOW), stacked)
        grad_probs = mm_t(stacked, values)
        delta = jnp.sum(heads_of(grad_att.astype(WIDE) * att[r].astype(WIDE)), axis=-1, keepdims=True)
        grad_scores = (probs * (grad_probs - delta) * (1.0 / math.sqrt(HD))).astype(LOW)
        grad_query = heads_join(mm(grad_scores, keys))
        grad_keys = t_mm(grad_scores, heads_of(query))
        acc[8:9, 0:THIRD] += jnp.sum(grad_query, axis=0, keepdims=True)
        acc[8:9, 256 : 256 + THIRD] += jnp.sum(grad_values, axis=0, keepdims=True)
        made = jnp.concatenate([grad_query, grad_keys, grad_values], axis=1).astype(LOW)
        gproj[r] = made
        gnf_tx[r] = mm_t(made, wq[...]).astype(LOW)
        pl.when(k == 3)(sum_gnf.far)
        return carry

    lax.fori_loop(0, 1, attend_back, 0)
    sum_pp.near()
    lax.fori_loop(1, 4, attend_back, 0)
    rq.fill(t_mm(whole(nf), whole(gproj)))
    rq.pair()
    sum_gnf.near()
    rq.step1()

    ro.finish(factor)
    do_base = links.take(4)
    do_recv = links.take(4)
    slot = (2 * j + c) % 4
    for k in (1, 2, 3):
        links.send(ro.final, do_ref.at[slot], do_base + k, (xor(j, k), 2 * z + half), do_recv + slot)
    across = links.copy(ro.final, do_ref.at[slot], do_base, p.mate, do_recv + slot)

    @pl.when(c == half)
    def _():
        do_ref[slot] = ro.final[...]

    @pl.when(c != half)
    def _():
        across.start()
        across.wait_send()

    rq.step2()
    rf.finish(factor)
    df_all[j] = rf.final[...]
    across_df.start()

    pz[...] = sum_pp.total().astype(LOW)
    pz_base = links.take(3)
    pz_sent = [
        links.send(pz.at[xor(z, 3)], pz_near.at[1], pz_base, p.one),
        links.send(pz.at[xor(z, 1)], pz_near.at[0], pz_base + 1, p.one),
    ]

    grad = sum_gnf.total()
    sums[0:1] = jnp.sum(grad * unit1[...], axis=0, keepdims=True)
    sums[1:2] = jnp.sum(grad, axis=0, keepdims=True)
    gt_ref[...] = gr[...] + normalize_back(grad, unit1[...], scales[:, 0:1], params[0:1])
    stores = [local(gt_ref, gt_hbm, 0)]

    out = lax.broadcasted_iota(jnp.int32, (THIRD, D), 1)
    lane = lax.broadcasted_iota(jnp.int32, (THIRD, D), 0)
    spot = jnp.where(out == lane + THIRD * j, 1.0, 0.0).astype(LOW)
    for row_at, lane_at in ((2, 0), (3, 256)):
        parts = three(acc[8:9, lane_at : lane_at + THIRD])
        sums[row_at : row_at + 1] = mm(parts[0], spot) + mm(parts[1], spot) + mm(parts[2], spot)
    sums[8:16] = jnp.broadcast_to(acc[0:1, :], (8, D))
    parts = three(sums[...])
    spread_out = mm_t(parts[0], place_m[...]) + mm_t(parts[1], place_m[...]) + mm_t(parts[2], place_m[...])
    line = lax.broadcasted_iota(jnp.int32, (8, 128), 0)
    own_lines = (line >= 2 * (j % 2)) & (line < 2 * (j % 2) + 2)
    for i in range(8):
        vt[i, 0:8] = spread_out[0:8, 128 * i : 128 * i + 128]
        at = 256 * (i // 2)
        even, more = spread_out[8:16, at : at + 128], spread_out[8:16, at + 128 : at + 256]
        picked = jnp.where((line & 1) == 0, even, more)
        vt[i, 8:16] = jnp.where(own_lines & (half == i % 2), picked, 0.0)
    vt_base = links.take(8)
    vt_sent = []
    for i in range(1, 8):
        device = p.at(i // 2, i % 2)
        vt_sent.append(links.send(vt.at[device[1]], vr.at[i], vt_base + i, device))

    pz_sent[0].wait_recv()
    pz_second[...] = (pz[xor(z, 2)].astype(WIDE) + pz_near[1].astype(WIDE)).astype(LOW)
    pz_last = links.send(pz_second, pz_far, pz_base + 2, p.two)
    rq.finish(factor)
    dq_all[j] = rq.final[...]
    across_dq.start()

    mine = vt[s]
    for i in range(1, 8):
        vt_sent[i - 1].wait_recv()
        mine = mine + vr[i]
    v2[...] = mine
    v2_base = links.take(4)
    to_peers(lambda k: v2, vr2, v2_base)

    pz_sent[1].wait_recv()
    pz_last.wait_recv()
    made = pz[z].astype(WIDE) + pz_near[0].astype(WIDE) + pz_far[...].astype(WIDE)
    pp_all[j] = (made * factor).astype(LOW)
    dp_base = links.take(4)
    to_peers(lambda k: pp_all.at[j], pp_all, dp_base)
    across_df.first()
    across_df.second()

    made = res[...] + params[7:8] + op_tx[j].astype(WIDE)
    for k in (1, 2, 3):
        await_peer(op_rx, op_base, k)
        made = made + op_rx[xor(j, k)].astype(WIDE)
    y_ref[...] = made.astype(LOW)
    stores.append(local(y_ref, y_hbm, 1))
    for i in range(4):
        here = (2 * c + i // 2 == j) & (c == i % 2)

        @pl.when(jnp.logical_not(here))
        def _():
            links.copy(do_ref.at[i], do_ref.at[i], do_base, p.here, do_recv + i).wait_recv()

    stores.append(local(do_ref, do_hbm, 2))
    across_dq.first()
    across_dq.second()
    across_df.finish()

    def into(dst, src, count):
        for r in range(4):
            for i in range(count):
                at = D * i + THIRD * r
                dst[:, at : at + THIRD] = src[r, :, THIRD * i : THIRD * (i + 1)]

    into(df_ref, df_all, 4)
    stores.append(local(df_ref, df_hbm, 3))
    for k in (1, 2, 3):
        await_peer(pp_all, dp_base, k)
    for t, a, b, at, to in TILES:
        dp_ref[to : to + b - a, 128 * t : 128 * (t + 1)] = pp_all[at, a:b]
    stores.append(local(dp_ref, dp_hbm, 4))
    mine = v2[...]
    for k in (1, 2, 3):
        await_peer(vr2, v2_base, k)
        mine = mine + vr2[xor(j, k)]
    dv_ref[...] = mine * factor
    stores.append(local(dv_ref, dv_hbm, 5))
    across_dq.finish()
    into(dq_ref, dq_all, 3)
    stores.append(local(dq_ref, dq_hbm, 6))

    for buf_of, dst, base in (
        (att, att_rx, att_base),
        (gns_tx, gns_rx, gns_base),
        (op_tx, op_rx, op_base),
    ):
        for k in (1, 2, 3):
            links.copy(buf_of.at[xor(j, k)], dst.at[j], base + k, p.peer(k)).wait_send()
    links.drain()
    for made in stores:
        made.wait()


def widen_kernel(
    y, gt, dq, dp, df, do, dv,
    y_out, gt_out, dq_out, dp_out, df_out, do_out, qv_out, fb_out, g1_out, s1_out, pb_out, g2_out, s2_out, ob_out,
    ins, outs, y_low, gt_low, dq_low, dp_low, df_low, do_low, dq_wide, dp_wide, df_wide, do_wide,
):
    def local(src, dst, sems, index):
        made = pltpu.make_async_copy(src, dst, sems.at[index])
        made.start()
        return made

    work = ((dq, dq_low, dq_wide, dq_out), (df, df_low, df_wide, df_out), (do, do_low, do_wide, do_out), (dp, dp_low, dp_wide, dp_out))
    loads = [local(src, low, ins, i) for i, (src, low, _, _) in enumerate(work)]
    plain = ((y, y_low, y_out), (gt, gt_low, gt_out))
    passing = [local(src, low, ins, 4 + i) for i, (src, low, _) in enumerate(plain)]
    done = []
    qv_out[...] = dv[2:4, 0:BLOCK]
    for i in range(4):
        fb_out[:, BLOCK * i : BLOCK * (i + 1)] = dv[8 + i : 9 + i, 0:BLOCK]
    for ref, i in zip((g1_out, s1_out, pb_out, g2_out, s2_out, ob_out), (0, 1, 4, 5, 6, 7)):
        ref[...] = dv[i : i + 1, 0:BLOCK]
    for i, (_, low, wide, out) in enumerate(work):
        loads[i].wait()
        wide[...] = low[...].reshape(wide.shape).astype(WIDE)
        done.append(local(wide, out, outs, i))
    for i, (_, low, out) in enumerate(plain):
        passing[i].wait()
        done.append(local(low, out, outs, 4 + i))
    for made in done:
        made.wait()


def vmem(*shape, kind=LOW):
    return pltpu.VMEM(shape, kind)


def fused_device(
    tokens,
    segment_ids,
    first_gain,
    first_shift,
    qkv_weight,
    qv_bias,
    proj_weight,
    proj_bias,
    second_gain,
    second_shift,
    fc_weight,
    fc_bias,
    out_weight,
    out_bias,
    cotangent,
):
    shards, reps = lax.axis_size("shard"), lax.axis_size("rep")
    factor = 1.0 / math.sqrt(ROWS * reps * shards)

    def reduce_bufs(width):
        return [
            vmem(4, 2, BLOCK, width),
            vmem(4, BLOCK, width),
            vmem(4, BLOCK, width),
            vmem(2, BLOCK, width),
            vmem(BLOCK, width),
            vmem(BLOCK, width),
            vmem(BLOCK, width),
        ]

    blocks = lambda width, kind=LOW: vmem(4, ROWS, width, kind=kind)
    scratch = [
        pltpu.SemaphoreType.DMA((160,)),
        pltpu.SemaphoreType.DMA((160,)),
        pltpu.SemaphoreType.DMA((8,)),
        vmem(ROWS, D),
        vmem(BLOCK, 3 * D),
        vmem(BLOCK, D),
        vmem(BLOCK, FF),
        vmem(4 * BLOCK, D),
        vmem(ROWS, D),
        vmem(ROWS, D, kind=WIDE),
        vmem(BLOCK, 3 * D),
        vmem(BLOCK, D),
        vmem(BLOCK, FF),
        vmem(4, BLOCK, D),
        vmem(16, 128, kind=WIDE),
        vmem(16, 128, kind=WIDE),
        vmem(16, 128),
        vmem(8, 16, 128),
        blocks(D),
        vmem(4, 8, ROWS, kind=WIDE),
        blocks(D),
        vmem(BLOCK, 3 * THIRD),
        vmem(BLOCK, D),
        vmem(D, 3 * THIRD),
        vmem(D, D),
        vmem(D, D),
        vmem(D, D),
        vmem(BLOCK, D),
        vmem(BLOCK, D),
        vmem(1024, D),
        vmem(16, D, kind=WIDE),
        blocks(D),
        vmem(4, 3 * ROWS, 128, kind=WIDE),
        blocks(THIRD),
        blocks(THIRD),
        vmem(ROWS, D, kind=WIDE),
        vmem(ROWS, D, kind=WIDE),
        vmem(ROWS, D, kind=WIDE),
        vmem(ROWS, 128, kind=WIDE),
        blocks(D),
        blocks(D),
        blocks(D, WIDE),
        blocks(D),
        blocks(D),
        blocks(D),
        blocks(D),
        blocks(D),
        blocks(THIRD),
        blocks(THIRD),
        blocks(D),
        blocks(D),
        vmem(2, ROWS // 2, D),
        vmem(2, 2, 144, 128),
        blocks(3 * THIRD),
        vmem(ROWS, D, kind=WIDE),
        vmem(16, D, kind=WIDE),
        vmem(16, D, kind=WIDE),
        vmem(8, 16, 128, kind=WIDE),
        vmem(8, 16, 128, kind=WIDE),
        vmem(16, 128, kind=WIDE),
        vmem(4, 16, 128, kind=WIDE),
        vmem(4, BLOCK, 3 * THIRD),
        vmem(4, BLOCK, D),
        vmem(576, 128),
        vmem(4, 2, 4, 144, 128),
        vmem(2, 4, 4, 144, 128),
        vmem(4, 4, 144, 128),
        vmem(4, 4, 144, 128),
        vmem(4, 4, 144, 128),
        vmem(4, 144, 128),
        vmem(2, 144, 128),
        vmem(144, 128),
        vmem(144, 128),
        vmem(4, 144, 128),
    ]
    for width in (3 * THIRD, D, D):
        scratch += reduce_bufs(width)
    in_vmem = pl.BlockSpec(memory_space=pltpu.VMEM)
    anywhere = pl.BlockSpec(memory_space=pl.ANY)
    partial = pl.pallas_call(
        functools.partial(layer_kernel, factor),
        out_shape=(
            jax.ShapeDtypeStruct((ROWS, D), LOW),
            jax.ShapeDtypeStruct((ROWS, D), WIDE),
            jax.ShapeDtypeStruct((BLOCK, 3 * D), LOW),
            jax.ShapeDtypeStruct((BLOCK, D), LOW),
            jax.ShapeDtypeStruct((BLOCK, FF), LOW),
            jax.ShapeDtypeStruct((4, BLOCK, D), LOW),
            jax.ShapeDtypeStruct((16, 128), WIDE),
        ),
        in_specs=[anywhere] * 2 + [in_vmem] * 9 + [anywhere] * 4,
        out_specs=(anywhere,) * 7,
        scratch_shapes=scratch,
        compiler_params=pltpu.CompilerParams(
            collective_id=0, has_side_effects=True, vmem_limit_bytes=56 * 1024 * 1024
        ),
    )(
        tokens,
        cotangent,
        segment_ids,
        first_gain[None],
        first_shift[None],
        qv_bias,
        proj_bias[None],
        second_gain[None],
        second_shift[None],
        fc_bias[None],
        out_bias[None],
        qkv_weight,
        proj_weight,
        fc_weight,
        out_weight,
    )
    rows = [jax.ShapeDtypeStruct((1, BLOCK), WIDE)] * 6
    y, grad_tokens, qkv_grad, proj_grad, fc_grad, out_grad, qv_grad, fc_bias_grad, *sums = pl.pallas_call(
        widen_kernel,
        out_shape=(
            jax.ShapeDtypeStruct((ROWS, D), LOW),
            jax.ShapeDtypeStruct((ROWS, D), WIDE),
            jax.ShapeDtypeStruct((BLOCK, 3 * D), WIDE),
            jax.ShapeDtypeStruct((BLOCK, D), WIDE),
            jax.ShapeDtypeStruct((BLOCK, FF), WIDE),
            jax.ShapeDtypeStruct((4 * BLOCK, D), WIDE),
            jax.ShapeDtypeStruct((2, BLOCK), WIDE),
            jax.ShapeDtypeStruct((1, 4 * BLOCK), WIDE),
            *rows,
        ),
        in_specs=[anywhere] * 6 + [in_vmem],
        out_specs=(anywhere,) * 6 + (in_vmem,) * 8,
        scratch_shapes=[
            pltpu.SemaphoreType.DMA((6,)),
            pltpu.SemaphoreType.DMA((6,)),
            vmem(ROWS, D),
            vmem(ROWS, D, kind=WIDE),
            vmem(BLOCK, 3 * D),
            vmem(BLOCK, D),
            vmem(BLOCK, FF),
            vmem(4, BLOCK, D),
            vmem(BLOCK, 3 * D, kind=WIDE),
            vmem(BLOCK, D, kind=WIDE),
            vmem(BLOCK, FF, kind=WIDE),
            vmem(4 * BLOCK, D, kind=WIDE),
        ],
        compiler_params=pltpu.CompilerParams(vmem_limit_bytes=56 * 1024 * 1024),
    )(*partial)
    first_gain_grad, first_shift_grad, proj_bias_grad, second_gain_grad, second_shift_grad, out_bias_grad = (
        row.reshape(BLOCK) for row in sums
    )
    return (
        y,
        grad_tokens,
        first_gain_grad,
        first_shift_grad,
        qkv_grad,
        qv_grad,
        proj_grad,
        proj_bias_grad,
        second_gain_grad,
        second_shift_grad,
        fc_grad,
        fc_bias_grad.reshape(4 * BLOCK),
        out_grad,
        out_bias_grad,
    )


def solution(mesh):
    return jax.shard_map(
        fused_device if dict(mesh.shape) == {"rep": 4, "shard": 8} else per_device,
        mesh=mesh,
        in_specs=(
            P(("rep", "shard"), None),
            P(("rep", "shard"), None),
            P("shard"),
            P("shard"),
            P("shard", None),
            P(None, "shard"),
            P("shard", None),
            P("shard"),
            P("shard"),
            P("shard"),
            P("shard", None),
            P("shard"),
            P("shard", None),
            P("shard"),
            P(("rep", "shard"), None),
        ),
        out_specs=(
            P(("rep", "shard"), None),
            P(("rep", "shard"), None),
            P("shard"),
            P("shard"),
            P("shard", None),
            P(None, "shard"),
            P("shard", None),
            P("shard"),
            P("shard"),
            P("shard"),
            P("shard", None),
            P("shard"),
            P("shard", None),
            P("shard"),
        ),
        check_vma=False,
    )
```
